32 devices in a mesh: row: 8 (over z, x), col: 4 (over y, core).
Axes of the slice: x: 2, y: 2, z: 4, core: 2. Of those that a mesh axis runs over, the one named last changes fastest.
Arguments:
- mom_a: float32 [1536, 12288], P('row', 'col'), may hold values from -6 to 6
- grad_a: float32 [1536, 12288], P('row', 'col'), may hold values from -6 to 6
- basis_a: float32 [512, 12288], P('row', 'col'), may hold values from -0.0546875 to 0.0546875
- mom_b: float32 [7168, 1536], P('row', 'col'), may hold values from -6 to 6
- grad_b: float32 [7168, 1536], P('row', 'col'), may hold values from -6 to 6
- basis_b: float32 [512, 1536], P('row', 'col'), may hold values from -0.15625 to 0.15625
Outputs:
- new_mom_a: float32 [1536, 12288], P('row', 'col')
- update_a: bfloat16 [1536, 12288], P('row', 'col')
- new_basis_a: float32 [512, 12288], P('row', 'col')
- new_mom_b: float32 [7168, 1536], P('row', 'col')
- update_b: bfloat16 [7168, 1536], P('row', 'col')
- new_basis_b: float32 [512, 1536], P('row', 'col')
The draws below stay inside these ranges and needn't reach their ends.
All inputs are finite; a program needn't handle non-finite values.
Results may differ from the reference program's by a relative error of at most 0.0049.
Values sent between devices are 32-bit elements; how exact they have to be, the bound alone decides.
A program may use at most 128 MiB of HBM per device.

```python
import math
import jax
import jax.numpy as jnp
from jax import lax

M_A = 1536
N_A = 12288
M_B = 7168
N_B = 1536
RANK = 512


def strong_factors(key, offset, row_count, col_count):
    strong_rank = 3 * RANK // 4
    left_factor = jax.random.normal(jax.random.fold_in(key, offset + 1), (row_count, strong_rank), jnp.float32) / math.sqrt(row_count)
    right_factor = jax.random.normal(jax.random.fold_in(key, offset + 2), (strong_rank, col_count), jnp.float32) / math.sqrt(col_count)
    low_end = 1.0
    high_end = 5.0
    strength = jnp.exp(jax.random.uniform(jax.random.fold_in(key, offset + 3), (strong_rank,), jnp.float32, math.log(low_end), math.log(high_end)))
    ratios = jax.random.uniform(jax.random.fold_in(key, offset + 4), (strong_rank,), jnp.float32, 0.5, 1.5)
    amplitude = 0.2 * math.sqrt(row_count * col_count / RANK)
    return (left_factor * amplitude, right_factor, strength, ratios)


def noise_field(key, offset, row_count, col_count):
    noise_term = jax.random.normal(key_mix(key, offset), (row_count, col_count), jnp.float32)
    return 0.2 * noise_term


def key_mix(key, offset):
    return jax.random.fold_in(key, offset)


def draw_matrix(key, offset, row_count, col_count, second):
    left_factor, right_factor, strength, ratios = strong_factors(key, offset, row_count, col_count)
    if second:
        weights = strength * ratios
        noise_offset = offset + 20
    else:
        weights = strength
        noise_offset = offset + 10
    low_rank = jnp.dot(left_factor * weights[None, :], right_factor, precision=lax.Precision.HIGHEST, preferred_element_type=jnp.float32)
    noise_term = noise_field(key, noise_offset, row_count, col_count)
    return jnp.clip(low_rank + noise_term, -6.0, 6.0)


def draw_mom_a(key, part):
    return draw_matrix(key, 100, M_A, N_A, False)


def draw_grad_a(key, part):
    return draw_matrix(key, 100, M_A, N_A, True)


def draw_mom_b(key, part):
    return draw_matrix(key, 200, M_B, N_B, False)


def draw_grad_b(key, part):
    return draw_matrix(key, 200, M_B, N_B, True)


def levels(stream_key, shape, pieces, low, largest):
    def one(position, blocks):
        heights = jax.random.uniform(jax.random.fold_in(jax.random.fold_in(stream_key, 6), position), (blocks,), jnp.float32, low / len(pieces), largest / len(pieces))
        return jnp.repeat(jnp.exp(heights), shape[position] // blocks).reshape((-1,) + (1,) * (len(shape) - position - 1))

    factor_of = one(*pieces[0])
    for cut in pieces[1:]:
        factor_of = factor_of * one(*cut)
    return factor_of


def bell_draw(rng, dims, width, limit, split=(), held_as=jnp.bfloat16):
    values = jax.random.normal(rng, dims, jnp.float32) * width
    if len(split) > 0:
        values = levels(rng, dims, split, -0.22, 0.18) * values
    return jnp.clip(values, min=-limit, max=limit).astype(held_as)


def setup_inputs(seed: int = 0) -> dict:
    keys = jax.random.split(jax.random.key(seed), 7)
    return {
        "mom_a": draw_mom_a(jax.random.fold_in(keys[6], 71), 0),
        "grad_a": draw_grad_a(jax.random.fold_in(keys[6], 71), 0),
        "basis_a": bell_draw(keys[2], (RANK, N_A), N_A ** -0.5, 0.0546875, ((0, 8), (1, 4)), jnp.float32),
        "mom_b": draw_mom_b(jax.random.fold_in(keys[6], 71), 0),
        "grad_b": draw_grad_b(jax.random.fold_in(keys[6], 71), 0),
        "basis_b": bell_draw(keys[5], (RANK, N_B), N_B ** -0.5, 0.15625, ((0, 8), (1, 4)), jnp.float32),
    }


MU = 0.95
EPS = 1e-06

def dion_step(mom, grad, basis):
    highest = lax.Precision.HIGHEST
    buffer = MU * mom + grad
    proj = jnp.dot(buffer.astype(jnp.float32), basis.T.astype(jnp.float32), precision=highest, preferred_element_type=jnp.float32)
    gram = jnp.dot(proj.T.astype(jnp.float32), proj.astype(jnp.float32), precision=highest, preferred_element_type=jnp.float32)
    lower = jnp.linalg.cholesky(gram)
    ortho = lax.linalg.triangular_solve(lower, proj, left_side=False, lower=True, transpose_a=True)
    trans = jnp.dot(ortho.T.astype(jnp.float32), buffer.astype(jnp.float32), precision=highest, preferred_element_type=jnp.float32)
    new_mom = buffer - (1.0 - MU) * jnp.dot(ortho.astype(jnp.float32), trans.astype(jnp.float32), precision=highest, preferred_element_type=jnp.float32)
    norms = jnp.sqrt(lax.optimization_barrier(jnp.sum(trans * trans, axis=1, keepdims=True)) + EPS)
    new_basis = trans / norms
    scale = math.sqrt(buffer.shape[0] * buffer.shape[1] / basis.shape[0])
    update = (jnp.dot(ortho.astype(jnp.float32), new_basis.astype(jnp.float32), precision=highest, preferred_element_type=jnp.float32) * scale).astype(jnp.bfloat16)
    return (new_mom, update, new_basis)

def reference(mom_a, grad_a, basis_a, mom_b, grad_b, basis_b):
    first = dion_step(mom_a, grad_a, basis_a)
    second = dion_step(mom_b, grad_b, basis_b)
    return (first[0], first[1], first[2], second[0], second[1], second[2])
```

```python
import functools
import math

import jax
import jax.numpy as jnp
from jax import lax
from jax.experimental import pallas as pl
from jax.experimental.pallas import tpu as pltpu
from jax.sharding import PartitionSpec as P

MU = 0.95
EPS = 1e-06
BLOCK = 128
HIGHEST = lax.Precision.HIGHEST
MESH = pl.DeviceIdType.MESH
VMEM = pl.BlockSpec(memory_space=pltpu.VMEM)
DMA = pltpu.SemaphoreType.DMA
LAST = ((1,), (1,))
FIRST = ((0,), (0,))
PLAIN = ((1,), (0,))
SIDES = 2


def dot(x, y, contract=PLAIN, precision=HIGHEST):
    return lax.dot_general(
        x, y, (contract, ((), ())), precision=precision, preferred_element_type=jnp.float32
    )


def remote(src, dst, send, recv, device):
    return pltpu.make_async_remote_copy(
        src_ref=src,
        dst_ref=dst,
        send_sem=send,
        recv_sem=recv,
        device_id=device,
        device_id_type=MESH,
    )


def partner(position, bit):
    return position + bit - 2 * bit * lax.rem(position // bit, 2)


def col_bits(col_count):
    bits, bit = [], 1
    while bit < col_count:
        bits.append(bit)
        bit *= 2
    return bits


def greet_row(row, row_count, barrier):
    for k in range(1, row_count):
        peer = lax.rem(row + k, row_count)
        pl.semaphore_signal(barrier, inc=1, device_id={"row": peer}, device_id_type=MESH)


def greet_cols(col, bits, barrier):
    for bit in bits:
        peer = partner(col, bit)
        pl.semaphore_signal(barrier, inc=1, device_id={"col": peer}, device_id_type=MESH)


class Gather:
    def __init__(self, row_count, sources, outs, sems):
        self.depth = row_count // SIDES
        self.row = lax.axis_index("row")
        self.place = self.row // SIDES
        lane = lax.rem(self.row, SIDES)
        self.other = self.place * SIDES + (1 - lane)
        self.sources, self.outs = sources, outs
        self.up_s, self.up_r, self.dn_s, self.dn_r, self.side_s, self.side_r, self.own = sems
        self.has_up = self.place < self.depth - 1
        self.has_dn = self.place > 0

    @staticmethod
    def scratch(row_count, count):
        depth = row_count // SIDES
        line = DMA((count, depth))
        side = DMA((count, 2, depth))
        return [line, line, line, line, side, side, DMA((count,))]

    def up(self, i, slot, d, first=False):
        src = self.sources[i] if first else self.outs[i].at[slot]
        device = {"row": self.row + SIDES}
        return remote(src, self.outs[i].at[slot], self.up_s.at[i, d], self.up_r.at[i, d], device)

    def dn(self, i, slot, d, first=False):
        src = self.sources[i] if first else self.outs[i].at[slot]
        device = {"row": self.row - SIDES}
        return remote(src, self.outs[i].at[slot], self.dn_s.at[i, d], self.dn_r.at[i, d], device)

    def side(self, i, slot, way, d, first=False):
        src = self.sources[i] if first else self.outs[i].at[slot]
        sems = self.side_s.at[i, way, d], self.side_r.at[i, way, d]
        return remote(src, self.outs[i].at[slot], *sems, {"row": self.other})

    def local(self, i):
        return pltpu.make_async_copy(self.sources[i], self.outs[i].at[self.row], self.own.at[i])

    def each(self):
        return range(len(self.sources))

    def start(self):
        for i in self.each():

            @pl.when(self.has_up)
            def _():
                self.up(i, self.row, 0, True).start()

            @pl.when(self.has_dn)
            def _():
                self.dn(i, self.row, 0, True).start()

            self.side(i, self.row, 0, 0, True).start()
        for i in self.each():
            self.local(i).start()

    def below(self, d):
        return self.row - d * SIDES

    def above(self, d):
        return self.row + d * SIDES

    def has_below(self, d):
        return self.place - d >= 0

    def has_above(self, d):
        return self.place + d < self.depth

    def forward(self, d):
        low, high = self.below(d), self.above(d)

        @pl.when(self.has_below(d))
        def _():
            for i in self.each():
                self.up(i, low, d - 1).wait_recv()

                @pl.when(self.has_up)
                def _():
                    self.up(i, low, d).start()

                self.side(i, low, 0, d).start()

        @pl.when(self.has_above(d))
        def _():
            for i in self.each():
                self.dn(i, high, d - 1).wait_recv()

                @pl.when(self.has_dn)
                def _():
                    self.dn(i, high, d).start()

                self.side(i, high, 1, d).start()

    def across(self, way, d):
        step = d * SIDES
        return self.other + (step if way else -step)

    def wait_side(self, way, d):
        for i in self.each():
            self.side(i, self.across(way, d), way, d).wait_recv()

    def drain(self):
        for i in self.each():

            @pl.when(self.has_up)
            def _():
                self.up(i, self.row, 0, True).wait_send()

            @pl.when(self.has_dn)
            def _():
                self.dn(i, self.row, 0, True).wait_send()

            self.side(i, self.row, 0, 0, True).wait_send()

        def later(d, carry):
            for i in self.each():

                @pl.when(self.has_below(d))
                def _():
                    @pl.when(self.has_up)
                    def _():
                        self.up(i, self.below(d), d).wait_send()

                    self.side(i, self.below(d), 0, d).wait_send()

                @pl.when(self.has_above(d))
                def _():
                    @pl.when(self.has_dn)
                    def _():
                        self.dn(i, self.above(d), d).wait_send()

                    self.side(i, self.above(d), 1, d).wait_send()

            return carry

        lax.fori_loop(1, self.depth, later, 0)


class ColSum:
    def __init__(self, bits, sums, landed, send, recv):
        self.bits, self.sums, self.landed, self.send, self.recv = bits, sums, landed, send, recv
        self.col = lax.axis_index("col")

    def copy(self, stage):
        device = {"col": partner(self.col, self.bits[stage])}
        sems = self.send.at[stage], self.recv.at[stage]
        return remote(self.sums[stage], self.landed[stage], *sems, device)

    def finish(self, stage):
        self.copy(stage).wait_recv()
        self.sums[stage + 1][...] = self.sums[stage][...] + self.landed[stage][...]

    def drain(self):
        for stage in range(len(self.bits)):
            self.copy(stage).wait_send()


def project_kernel(row_count, bits, *refs):
    stages = len(bits)
    basis_a, basis_b, buffer_a, buffer_b, cut_a, out_a, out_b, tall = refs[:8]
    all_a, all_b = refs[8:10]
    sums_a = list(refs[10 : 10 + stages]) + [out_a]
    sums_b = list(refs[10 + stages : 10 + 2 * stages]) + [out_b]
    landed_a = refs[10 + 2 * stages : 10 + 3 * stages]
    landed_b = refs[10 + 3 * stages : 10 + 4 * stages]
    gather_sems = refs[10 + 4 * stages : 17 + 4 * stages]
    small_s, small_r, small_own, cut_s, cut_r, cut_own = refs[17 + 4 * stages : 23 + 4 * stages]
    cs_a, cr_a, cs_b, cr_b = refs[23 + 4 * stages :]
    row, col = lax.axis_index("row"), lax.axis_index("col")
    share = basis_a.shape[0]
    depth = row_count // SIDES

    barrier = pltpu.get_barrier_semaphore()
    greet_row(row, row_count, barrier)
    greet_cols(col, bits, barrier)
    pl.semaphore_wait(barrier, row_count - 1 + stages)

    def small(k):
        peer = lax.rem(row + k, row_count)
        return remote(basis_b, all_b.at[row], small_s.at[k], small_r.at[k], {"row": peer})

    def cut(k):
        peer = lax.rem(row + k, row_count)
        return remote(cut_a.at[peer], tall.at[row], cut_s.at[k], cut_r.at[k], {"row": peer})

    small_local = pltpu.make_async_copy(basis_b, all_b.at[row], small_own)
    cut_local = pltpu.make_async_copy(cut_a.at[row], tall.at[row], cut_own)
    for k in range(1, row_count):
        small(k).start()
    gather = Gather(row_count, [basis_a], [all_a], gather_sems)
    gather.start()
    small_local.start()
    cut_local.start()

    def project(slot):
        rows = pl.ds(pl.multiple_of(slot * share, share), share)
        sums_a[0][rows, :] = dot(all_a[slot], buffer_a[...], LAST)

    gather.local(0).wait()
    project(row)
    small_local.wait()
    for k in range(1, row_count):
        small(k).wait_recv()
    for k in range(row_count):
        sums_b[0][k * share : (k + 1) * share, :] = dot(all_b[k], buffer_b[...], LAST)
    total_a = ColSum(bits, sums_a, landed_a, cs_a, cr_a)
    total_b = ColSum(bits, sums_b, landed_b, cs_b, cr_b)
    total_b.copy(0).start()

    def advance(d, carry):
        gather.forward(d)

        @pl.when(d == min(2, depth - 1))
        def _():
            for k in range(1, row_count):
                cut(k).start()

        @pl.when(gather.has_below(d - 1))
        def _():
            gather.wait_side(0, d - 1)

        @pl.when((d > 1) & gather.has_above(d - 1))
        def _():
            gather.wait_side(1, d - 1)

        def use(k, inner):
            line, way = k // 2, lax.rem(k, 2)
            step = (d - line) * (2 * way - 1)
            there = gather.place + step
            here = (there >= 0) & (there < depth) & ((way == 0) | (d - line > 0))

            @pl.when(here)
            def _():
                base = gather.row + line * (gather.other - gather.row)
                project(base + step * SIDES)

            return inner

        lax.fori_loop(0, 4, use, 0)
        return carry

    lax.fori_loop(1, depth, advance, 0)
    for stage in range(stages):
        total_b.finish(stage)
        if stage + 1 < stages:
            total_b.copy(stage + 1).start()

    def finish(way, carry):
        step = (depth - 1) * (2 * way - 1)
        there = gather.place + step

        @pl.when((there >= 0) & (there < depth))
        def _():
            project(gather.other + step * SIDES)

        return carry

    @pl.when(gather.has_below(depth - 1))
    def _():
        gather.wait_side(0, depth - 1)

    @pl.when(gather.has_above(depth - 1))
    def _():
        gather.wait_side(1, depth - 1)

    lax.fori_loop(0, 2, finish, 0)
    for stage in range(stages):
        total_a.copy(stage).start()
        total_a.finish(stage)
    cut_local.wait()
    for k in range(1, row_count):
        cut(k).wait()
        small(k).wait_send()
    gather.drain()
    total_a.drain()
    total_b.drain()


def project(basis_a, basis_b, buffer_a, buffer_b, cut_a):
    row_count, col_count = lax.axis_size("row"), lax.axis_size("col")
    bits = col_bits(col_count)
    stages = len(bits)
    share, rows_a, rows_b = basis_a.shape[0], buffer_a.shape[0], buffer_b.shape[0]
    rank = share * row_count
    float_a, float_b = (
        jax.ShapeDtypeStruct((rank, rows_a), jnp.float32),
        jax.ShapeDtypeStruct((rank, rows_b), jnp.float32),
    )
    space_a, space_b = pltpu.VMEM(float_a.shape, jnp.float32), pltpu.VMEM(float_b.shape, jnp.float32)
    return pl.pallas_call(
        functools.partial(project_kernel, row_count, bits),
        out_shape=[float_a, float_b, jax.ShapeDtypeStruct(cut_a.shape, jnp.float32)],
        in_specs=[VMEM] * 5,
        out_specs=[VMEM] * 3,
        scratch_shapes=[
            pltpu.VMEM((row_count,) + basis_a.shape, jnp.float32),
            pltpu.VMEM((row_count,) + basis_b.shape, jnp.float32),
        ]
        + [space_a] * stages
        + [space_b] * stages
        + [space_a] * stages
        + [space_b] * stages
        + Gather.scratch(row_count, 1)
        + [DMA((row_count,)), DMA((row_count,)), DMA(())] * 2
        + [DMA((stages,))] * 4,
        name="project",
        compiler_params=pltpu.CompilerParams(
            collective_id=1, has_side_effects=True, vmem_limit_bytes=60 * 2**20
        ),
    )(basis_a, basis_b, buffer_a, buffer_b, cut_a)


def factor(rank, grams, outs, works, diags, between):
    eye_rows = lax.broadcasted_iota(jnp.int32, (rank, rank), 0)
    eye_cols = lax.broadcasted_iota(jnp.int32, (rank, rank), 1)
    for gram, work in zip(grams, works):
        work[:, :rank] = gram[...]
        work[:, rank:] = (eye_rows == eye_cols).astype(jnp.float32)
    rows = lax.broadcasted_iota(jnp.int32, (BLOCK, 1), 0)
    lanes = lax.broadcasted_iota(jnp.int32, (1, BLOCK), 1)
    for k in range(rank // BLOCK):
        low, high = k * BLOCK, (k + 1) * BLOCK
        for work, diag in zip(works, diags):
            diag[:, :BLOCK] = work[low:high, low:high]
            diag[:, BLOCK:] = (rows == lanes).astype(jnp.float32)

        def step(j, carry):
            for diag in diags:
                here = lanes == j
                row = diag[pl.ds(j, 1), :]
                col = jnp.sum(jnp.where(here, diag[:, :BLOCK], 0.0), axis=1, keepdims=True)
                pivot = jnp.sum(jnp.where(here, row[:, :BLOCK], 0.0), axis=1, keepdims=True)
                factor = jnp.where(rows > j, col * (1.0 / pivot), 0.0)
                diag[...] = diag[...] - factor * row
            return carry

        lax.fori_loop(0, BLOCK, step, 0)
        width = slice(low, rank + high)
        for work, diag in zip(works, diags):
            pivots = jnp.sum(
                jnp.where(rows == lanes, diag[:, :BLOCK], 0.0), axis=1, keepdims=True
            )
            inverse = diag[:, BLOCK:] * (1.0 / jnp.sqrt(pivots))
            panel = dot(inverse, work[low:high, width])
            work[low:high, width] = panel
            if high < rank:
                factors = panel[:, BLOCK : rank - low]
                work[high:, width] = work[high:, width] - dot(factors, panel, FIRST)
        between(k)
    for work, out in zip(works, outs):
        out[...] = work[:, rank:]


def products_kernel(row_count, rank, *refs):
    gram_a, gram_b, block_a, block_b, inv_a, inv_b, all_a, all_b = refs[:8]
    works, diags, sems = refs[8:10], refs[10:12], refs[12:19]
    row = lax.axis_index("row")
    barrier = pltpu.get_barrier_semaphore()
    greet_row(row, row_count, barrier)
    pl.semaphore_wait(barrier, row_count - 1)
    gather = Gather(row_count, [block_a, block_b], [all_a, all_b], sems)
    gather.start()
    early = min(rank // BLOCK, gather.depth)

    def between(k):
        if k + 1 < early:
            gather.forward(k + 1)

    factor(rank, [gram_a, gram_b], [inv_a, inv_b], works, diags, between)

    def later(d, carry):
        gather.forward(d)
        return carry

    lax.fori_loop(early, gather.depth, later, 0)
    gather.wait_side(0, 0)

    def landed(d, carry):
        @pl.when(gather.has_below(d))
        def _():
            gather.wait_side(0, d)

        @pl.when(gather.has_above(d))
        def _():
            gather.wait_side(1, d)

        return carry

    lax.fori_loop(1, gather.depth, landed, 0)
    for i in gather.each():
        gather.local(i).wait()
    gather.drain()


def products(gram_a, gram_b, block_a, block_b):
    row_count = lax.axis_size("row")
    rank = gram_a.shape[0]
    square = jax.ShapeDtypeStruct((rank, rank), jnp.float32)
    return pl.pallas_call(
        functools.partial(products_kernel, row_count, rank),
        out_shape=[square, square]
        + [jax.ShapeDtypeStruct((row_count,) + x.shape, jnp.float32) for x in (block_a, block_b)],
        in_specs=[VMEM] * 4,
        out_specs=[VMEM] * 4,
        scratch_shapes=[pltpu.VMEM((rank, 2 * rank), jnp.float32)] * 2
        + [pltpu.VMEM((BLOCK, 2 * BLOCK), jnp.float32)] * 2
        + Gather.scratch(row_count, 2),
        name="products",
        compiler_params=pltpu.CompilerParams(
            collective_id=2, has_side_effects=True, vmem_limit_bytes=60 * 2**20
        ),
    )(gram_a, gram_b, block_a, block_b)


def reduce_rows(partial_sum):
    share_count = lax.axis_size("row")
    shares = partial_sum.reshape(share_count, -1, partial_sum.shape[1])
    return jnp.sum(lax.all_to_all(shares, "row", 0, 0), axis=0)


def shards(mom_a, grad_a, basis_a, mom_b, grad_b, basis_b):
    row_count = lax.axis_size("row")
    buffer_a, buffer_b = MU * mom_a + grad_a, MU * mom_b + grad_b
    rows_a = buffer_a.shape[0]
    cut_a = buffer_a.reshape(rows_a, row_count, -1).swapaxes(0, 1)
    proj_a, proj_b, tall_a = project(basis_a, basis_b, buffer_a, buffer_b, cut_a)
    rank = proj_a.shape[0]
    share = rank // row_count

    shares_b = reduce_rows(
        jnp.concatenate([dot(proj_b, proj_b, LAST), dot(proj_b, buffer_b)], axis=1)
    )
    share_b = shares_b[:, rank:]
    all_a = lax.all_gather(proj_a, "row", axis=0)
    gram_b = lax.all_gather(shares_b[:, :rank], "row", axis=0, tiled=True)
    all_a = all_a.swapaxes(0, 1).reshape(rank, -1)
    gram_a = dot(all_a, all_a, LAST)
    block_a = dot(all_a, tall_a.reshape(-1, tall_a.shape[2]))
    inverse_a, inverse_b, product_a, product_b = products(gram_a, gram_b, block_a, share_b)
    product_a = product_a.swapaxes(0, 1).reshape(rank, -1)
    product_b = product_b.reshape(rank, -1)

    ortho_a, ortho_b = dot(proj_a, inverse_a, ((0,), (1,))), dot(proj_b, inverse_b, ((0,), (1,)))
    trans_a, trans_b = dot(inverse_a, product_a), dot(inverse_b, product_b)
    squares_a, squares_b = lax.psum(
        (
            jnp.sum(trans_a * trans_a, axis=1, keepdims=True),
            jnp.sum(trans_b * trans_b, axis=1, keepdims=True),
        ),
        "col",
    )
    start = lax.axis_index("row") * share
    first_out = finish(buffer_a, ortho_a, trans_a, squares_a, start, share)
    second_out = finish(buffer_b, ortho_b, trans_b, squares_b, start, share)
    return (*first_out, *second_out)


def finish(buffer, ortho, trans, squares, start, share):
    rank = ortho.shape[1]
    total_rows = buffer.shape[0] * lax.axis_size("row")
    total_cols = buffer.shape[1] * lax.axis_size("col")
    full_basis = trans / jnp.sqrt(squares + EPS)
    own_basis = lax.dynamic_slice_in_dim(full_basis, start, share, 0)
    new_mom = buffer - (1.0 - MU) * dot(ortho, trans)
    update = dot(ortho, full_basis) * math.sqrt(total_rows * total_cols / rank)
    return new_mom, update.astype(jnp.bfloat16), own_basis


def solution(mesh):
    spec = P("row", "col")
    return jax.shard_map(
        shards, mesh=mesh, in_specs=(spec,) * 6, out_specs=(spec,) * 6, check_vma=False
    )
```

```python
import functools
import math

import jax
import jax.numpy as jnp
from jax import lax
from jax.experimental import pallas as pl
from jax.experimental.pallas import tpu as pltpu
from jax.sharding import PartitionSpec as P

MU = 0.95
EPS = 1e-06
BLOCK = 128
HIGHEST = lax.Precision.HIGHEST
MESH = pl.DeviceIdType.MESH
VMEM = pl.BlockSpec(memory_space=pltpu.VMEM)
DMA = pltpu.SemaphoreType.DMA
LAST = ((1,), (1,))
FIRST = ((0,), (0,))
PLAIN = ((1,), (0,))
SIDES = 2


def dot(x, y, contract=PLAIN, precision=HIGHEST):
    return lax.dot_general(
        x, y, (contract, ((), ())), precision=precision, preferred_element_type=jnp.float32
    )


def halves(x):
    high = x.astype(jnp.bfloat16)
    return high, (x - high.astype(jnp.float32)).astype(jnp.bfloat16)


def narrow_dot(x, y, contract=PLAIN):
    return lax.dot_general(x, y, (contract, ((), ())), preferred_element_type=jnp.float32)


def split_dot(x, y, contract=PLAIN):
    (x_high, x_low), (y_high, y_low) = halves(x), halves(y)
    total = narrow_dot(x_high, y_low, contract) + narrow_dot(x_low, y_high, contract)
    return total + narrow_dot(x_high, y_high, contract)


def remote(src, dst, send, recv, device):
    return pltpu.make_async_remote_copy(
        src_ref=src,
        dst_ref=dst,
        send_sem=send,
        recv_sem=recv,
        device_id=device,
        device_id_type=MESH,
    )


def partner(position, bit):
    return position + bit - 2 * bit * lax.rem(position // bit, 2)


def col_bits(col_count):
    bits, bit = [], 1
    while bit < col_count:
        bits.append(bit)
        bit *= 2
    return bits


def greet_row(row, row_count, barrier):
    for k in range(1, row_count):
        peer = lax.rem(row + k, row_count)
        pl.semaphore_signal(barrier, inc=1, device_id={"row": peer}, device_id_type=MESH)


def greet_cols(col, bits, barrier):
    for bit in bits:
        peer = partner(col, bit)
        pl.semaphore_signal(barrier, inc=1, device_id={"col": peer}, device_id_type=MESH)


class Gather:
    def __init__(self, row_count, sources, outs, sems):
        self.depth = row_count // SIDES
        self.row = lax.axis_index("row")
        self.place = self.row // SIDES
        lane = lax.rem(self.row, SIDES)
        self.other = self.place * SIDES + (1 - lane)
        self.sources, self.outs = sources, outs
        self.up_s, self.up_r, self.dn_s, self.dn_r, self.side_s, self.side_r, self.own = sems
        self.has_up = self.place < self.depth - 1
        self.has_dn = self.place > 0

    @staticmethod
    def scratch(row_count, count):
        depth = row_count // SIDES
        line = DMA((count, depth))
        side = DMA((count, 2, depth))
        return [line, line, line, line, side, side, DMA((count,))]

    def up(self, i, slot, d, first=False):
        src = self.sources[i] if first else self.outs[i].at[slot]
        device = {"row": self.row + SIDES}
        return remote(src, self.outs[i].at[slot], self.up_s.at[i, d], self.up_r.at[i, d], device)

    def dn(self, i, slot, d, first=False):
        src = self.sources[i] if first else self.outs[i].at[slot]
        device = {"row": self.row - SIDES}
        return remote(src, self.outs[i].at[slot], self.dn_s.at[i, d], self.dn_r.at[i, d], device)

    def side(self, i, slot, way, d, first=False):
        src = self.sources[i] if first else self.outs[i].at[slot]
        sems = self.side_s.at[i, way, d], self.side_r.at[i, way, d]
        return remote(src, self.outs[i].at[slot], *sems, {"row": self.other})

    def local(self, i):
        return pltpu.make_async_copy(self.sources[i], self.outs[i].at[self.row], self.own.at[i])

    def each(self):
        return range(len(self.sources))

    def start(self):
        for i in self.each():

            @pl.when(self.has_up)
            def _():
                self.up(i, self.row, 0, True).start()

            @pl.when(self.has_dn)
            def _():
                self.dn(i, self.row, 0, True).start()

            self.side(i, self.row, 0, 0, True).start()
        for i in self.each():
            self.local(i).start()

    def below(self, d):
        return self.row - d * SIDES

    def above(self, d):
        return self.row + d * SIDES

    def has_below(self, d):
        return self.place - d >= 0

    def has_above(self, d):
        return self.place + d < self.depth

    def forward(self, d):
        low, high = self.below(d), self.above(d)

        @pl.when(self.has_below(d))
        def _():
            for i in self.each():
                self.up(i, low, d - 1).wait_recv()

                @pl.when(self.has_up)
                def _():
                    self.up(i, low, d).start()

                self.side(i, low, 0, d).start()

        @pl.when(self.has_above(d))
        def _():
            for i in self.each():
                self.dn(i, high, d - 1).wait_recv()

                @pl.when(self.has_dn)
                def _():
                    self.dn(i, high, d).start()

                self.side(i, high, 1, d).start()

    def across(self, way, d):
        step = d * SIDES
        return self.other + (step if way else -step)

    def wait_side(self, way, d):
        for i in self.each():
            self.side(i, self.across(way, d), way, d).wait_recv()

    def drain(self):
        for i in self.each():

            @pl.when(self.has_up)
            def _():
                self.up(i, self.row, 0, True).wait_send()

            @pl.when(self.has_dn)
            def _():
                self.dn(i, self.row, 0, True).wait_send()

            self.side(i, self.row, 0, 0, True).wait_send()

        def later(d, carry):
            for i in self.each():

                @pl.when(self.has_below(d))
                def _():
                    @pl.when(self.has_up)
                    def _():
                        self.up(i, self.below(d), d).wait_send()

                    self.side(i, self.below(d), 0, d).wait_send()

                @pl.when(self.has_above(d))
                def _():
                    @pl.when(self.has_dn)
                    def _():
                        self.dn(i, self.above(d), d).wait_send()

                    self.side(i, self.above(d), 1, d).wait_send()

            return carry

        lax.fori_loop(1, self.depth, later, 0)


class ColSum:
    def __init__(self, bits, sums, landed, send, recv):
        self.bits, self.sums, self.landed, self.send, self.recv = bits, sums, landed, send, recv
        self.col = lax.axis_index("col")

    def copy(self, stage):
        device = {"col": partner(self.col, self.bits[stage])}
        sems = self.send.at[stage], self.recv.at[stage]
        return remote(self.sums[stage], self.landed[stage], *sems, device)

    def finish(self, stage):
        self.copy(stage).wait_recv()
        self.sums[stage + 1][...] = self.sums[stage][...] + self.landed[stage][...]

    def drain(self):
        for stage in range(len(self.bits)):
            self.copy(stage).wait_send()


def project_kernel(row_count, bits, *refs):
    stages = len(bits)
    basis_a, basis_b, buffer_a, buffer_b, cut_a, out_a, out_b, tall = refs[:8]
    all_a, all_b, high_a, low_a = refs[8:12]
    refs = refs[12:]
    sums_a = list(refs[:stages]) + [out_a]
    sums_b = list(refs[stages : 2 * stages]) + [out_b]
    landed_a = refs[2 * stages : 3 * stages]
    landed_b = refs[3 * stages : 4 * stages]
    gather_sems = refs[4 * stages : 7 + 4 * stages]
    small_s, small_r, small_own, cut_s, cut_r, cut_own = refs[7 + 4 * stages : 13 + 4 * stages]
    cs_a, cr_a, cs_b, cr_b = refs[13 + 4 * stages :]
    row, col = lax.axis_index("row"), lax.axis_index("col")
    share = basis_a.shape[0]
    depth = row_count // SIDES

    barrier = pltpu.get_barrier_semaphore()
    greet_row(row, row_count, barrier)
    greet_cols(col, bits, barrier)
    pl.semaphore_wait(barrier, row_count - 1 + stages)

    def small(k):
        peer = lax.rem(row + k, row_count)
        return remote(basis_b, all_b.at[row], small_s.at[k], small_r.at[k], {"row": peer})

    def cut(k):
        peer = lax.rem(row + k, row_count)
        return remote(cut_a.at[peer], tall.at[row], cut_s.at[k], cut_r.at[k], {"row": peer})

    small_local = pltpu.make_async_copy(basis_b, all_b.at[row], small_own)
    cut_local = pltpu.make_async_copy(cut_a.at[row], tall.at[row], cut_own)
    for k in range(1, row_count):
        small(k).start()
    gather = Gather(row_count, [basis_a], [all_a], gather_sems)
    gather.start()
    small_local.start()
    cut_local.start()

    def project(slot):
        rows = pl.ds(pl.multiple_of(slot * share, share), share)
        basis_high, basis_low = halves(all_a[slot])
        total = narrow_dot(basis_high, low_a[...], LAST) + narrow_dot(basis_low, high_a[...], LAST)
        sums_a[0][rows, :] = total + narrow_dot(basis_high, high_a[...], LAST)

    high_a[...], low_a[...] = halves(buffer_a[...])

    gather.local(0).wait()
    project(row)
    small_local.wait()
    for k in range(1, row_count):
        small(k).wait_recv()
    flat_b = all_b[...].reshape(row_count * share, basis_b.shape[1])
    sums_b[0][...] = split_dot(flat_b, buffer_b[...], LAST)
    total_a = ColSum(bits, sums_a, landed_a, cs_a, cr_a)
    total_b = ColSum(bits, sums_b, landed_b, cs_b, cr_b)
    total_b.copy(0).start()

    def advance(d, carry):
        gather.forward(d)

        @pl.when(d == min(2, depth - 1))
        def _():
            for k in range(1, row_count):
                cut(k).start()

        @pl.when(gather.has_below(d - 1))
        def _():
            gather.wait_side(0, d - 1)

        @pl.when((d > 1) & gather.has_above(d - 1))
        def _():
            gather.wait_side(1, d - 1)

        def use(k, inner):
            line, way = k // 2, lax.rem(k, 2)
            step = (d - line) * (2 * way - 1)
            there = gather.place + step
            here = (there >= 0) & (there < depth) & ((way == 0) | (d - line > 0))

            @pl.when(here)
            def _():
                base = gather.row + line * (gather.other - gather.row)
                project(base + step * SIDES)

            return inner

        lax.fori_loop(0, 4, use, 0)
        return carry

    lax.fori_loop(1, depth, advance, 0)
    for stage in range(stages):
        total_b.finish(stage)
        if stage + 1 < stages:
            total_b.copy(stage + 1).start()

    def finish(way, carry):
        step = (depth - 1) * (2 * way - 1)
        there = gather.place + step

        @pl.when((there >= 0) & (there < depth))
        def _():
            project(gather.other + step * SIDES)

        return carry

    @pl.when(gather.has_below(depth - 1))
    def _():
        gather.wait_side(0, depth - 1)

    @pl.when(gather.has_above(depth - 1))
    def _():
        gather.wait_side(1, depth - 1)

    lax.fori_loop(0, 2, finish, 0)
    for stage in range(stages):
        total_a.copy(stage).start()
        total_a.finish(stage)
    cut_local.wait()
    for k in range(1, row_count):
        cut(k).wait()
        small(k).wait_send()
    gather.drain()
    total_a.drain()
    total_b.drain()


def project(basis_a, basis_b, buffer_a, buffer_b, cut_a):
    row_count, col_count = lax.axis_size("row"), lax.axis_size("col")
    bits = col_bits(col_count)
    stages = len(bits)
    share, rows_a, rows_b = basis_a.shape[0], buffer_a.shape[0], buffer_b.shape[0]
    rank = share * row_count
    float_a, float_b = (
        jax.ShapeDtypeStruct((rank, rows_a), jnp.float32),
        jax.ShapeDtypeStruct((rank, rows_b), jnp.float32),
    )
    space_a, space_b = pltpu.VMEM(float_a.shape, jnp.float32), pltpu.VMEM(float_b.shape, jnp.float32)
    return pl.pallas_call(
        functools.partial(project_kernel, row_count, bits),
        out_shape=[float_a, float_b, jax.ShapeDtypeStruct(cut_a.shape, jnp.float32)],
        in_specs=[VMEM] * 5,
        out_specs=[VMEM] * 3,
        scratch_shapes=[
            pltpu.VMEM((row_count,) + basis_a.shape, jnp.float32),
            pltpu.VMEM((row_count,) + basis_b.shape, jnp.float32),
            pltpu.VMEM(buffer_a.shape, jnp.bfloat16),
            pltpu.VMEM(buffer_a.shape, jnp.bfloat16),
        ]
        + [space_a] * stages
        + [space_b] * stages
        + [space_a] * stages
        + [space_b] * stages
        + Gather.scratch(row_count, 1)
        + [DMA((row_count,)), DMA((row_count,)), DMA(())] * 2
        + [DMA((stages,))] * 4,
        name="project",
        compiler_params=pltpu.CompilerParams(
            collective_id=1, has_side_effects=True, vmem_limit_bytes=60 * 2**20
        ),
    )(basis_a, basis_b, buffer_a, buffer_b, cut_a)


def middle_kernel(row_count, col_count, *refs):
    proj_a, proj_b, buffer_b, tall, gram_a, block_a, gram_b, share_b = refs[:8]
    all_a, part_g, part_w, land_g, land_w, own_g, quarters = refs[8:15]
    gather_sems = refs[15:22]
    twin_s, twin_r, gs, gr, ws, wr, g_own, w_own, fs, fr, f_own, qs, qr = refs[22:]
    row, col = lax.axis_index("row"), lax.axis_index("col")
    rank = proj_a.shape[0]
    share, quarter, half = rank // row_count, rank // col_count, rank // 2
    twin = partner(col, 1)
    side = lax.rem(col, 2)

    barrier = pltpu.get_barrier_semaphore()
    greet_row(row, row_count, barrier)
    for k in range(1, col_count):
        peer = lax.rem(col + k, col_count)
        pl.semaphore_signal(barrier, inc=1, device_id={"col": peer}, device_id_type=MESH)
    pl.semaphore_wait(barrier, row_count + col_count - 2)

    source = proj_a.at[pl.ds(pl.multiple_of(side * half, half), half), :]
    gather = Gather(row_count, [source], [all_a.at[side]], gather_sems)
    gather.start()

    def to_twin(slot):
        here = all_a.at[side, slot]
        return remote(here, here, twin_s.at[slot], twin_r.at[slot], {"col": twin})

    def from_twin(slot):
        there = all_a.at[1 - side, slot]
        return remote(there, there, twin_s.at[slot], twin_r.at[slot], {"col": twin})

    def rows_of(position):
        return pl.ds(pl.multiple_of(position * share, share), share)

    def send_g(k):
        peer = lax.rem(row + k, row_count)
        return remote(part_g.at[rows_of(peer), :], land_g.at[row], gs.at[k], gr.at[k], {"row": peer})

    def send_w(k):
        peer = lax.rem(row + k, row_count)
        return remote(part_w.at[rows_of(peer), :], land_w.at[row], ws.at[k], wr.at[k], {"row": peer})

    def send_f(k):
        peer = lax.rem(row + k, row_count)
        target = quarters.at[col, rows_of(row), :]
        return remote(own_g, target, fs.at[k], fr.at[k], {"row": peer})

    def send_q(k):
        peer = lax.rem(col + k, col_count)
        here = quarters.at[col]
        return remote(here, here, qs.at[k], qr.at[k], {"col": peer})

    def recv_q(k):
        peer = lax.rem(col + col_count - k, col_count)
        there = quarters.at[peer]
        return remote(there, there, qs.at[k], qr.at[k], {"col": peer})

    local_g = pltpu.make_async_copy(part_g.at[rows_of(row), :], land_g.at[row], g_own)
    local_w = pltpu.make_async_copy(part_w.at[rows_of(row), :], land_w.at[row], w_own)
    local_f = pltpu.make_async_copy(own_g, quarters.at[col, rows_of(row), :], f_own)

    some_b = proj_b[pl.ds(pl.multiple_of(col * quarter, quarter), quarter), :]
    part_g[...] = dot(proj_b[...], some_b, LAST)
    for k in range(1, row_count):
        send_g(k).start()
    local_g.start()
    part_w[...] = split_dot(proj_b[...], buffer_b[...])
    for k in range(1, row_count):
        send_w(k).start()
    local_w.start()
    gram_a[...] = jnp.zeros_like(gram_a)
    block_a[...] = jnp.zeros_like(block_a)
    gather.local(0).wait()
    to_twin(row).start()

    def use(slot):
        from_twin(slot).wait_recv()
        rows = jnp.concatenate([all_a[0, slot], all_a[1, slot]], axis=0)
        gram_a[...] += dot(rows, rows, LAST)
        block_a[...] += split_dot(rows, tall[slot])

    def advance(d, carry):
        gather.forward(d)

        @pl.when(gather.has_below(d))
        def _():
            to_twin(gather.below(d)).start()

        @pl.when(gather.has_above(d))
        def _():
            to_twin(gather.above(d)).start()

        @pl.when(gather.has_below(d - 1))
        def _():
            gather.wait_side(0, d - 1)
            to_twin(gather.across(0, d - 1)).start()

        @pl.when((d > 1) & gather.has_above(d - 1))
        def _():
            gather.wait_side(1, d - 1)
            to_twin(gather.across(1, d - 1)).start()

        @pl.when(d == min(2, gather.depth - 1))
        def _():
            reduce_g()

        def candidate(k, inner):
            line, way = k // 2, lax.rem(k, 2)
            reach = d - 1 - line
            step = reach * (2 * way - 1)
            there = gather.place + step
            here = (reach >= 0) & (there >= 0) & (there < gather.depth) & ((way == 0) | (reach > 0))

            @pl.when(here)
            def _():
                use(gather.row + line * (gather.other - gather.row) + step * SIDES)

            return inner

        lax.fori_loop(0, 4, candidate, 0)
        return carry

    def reduce_g():
        local_g.wait()
        for k in range(1, row_count):
            send_g(k).wait_recv()
        own_g[...] = jnp.sum(land_g[...], axis=0)
        for k in range(1, row_count):
            send_f(k).start()
        local_f.start()

    lax.fori_loop(1, gather.depth, advance, 0)
    last = gather.depth - 1

    @pl.when(gather.has_below(last))
    def _():
        gather.wait_side(0, last)
        to_twin(gather.across(0, last)).start()

    @pl.when(gather.has_above(last))
    def _():
        gather.wait_side(1, last)
        to_twin(gather.across(1, last)).start()

    for k in range(1, row_count):
        send_f(k).wait_recv()
    local_f.wait()
    for k in range(1, col_count):
        send_q(k).start()

    remaining_blocks = [(0, 0), (1, 1), (1, 0)]
    for line, back in remaining_blocks:
        for way in range(2):
            reach = last - back
            if reach < 0 or (way == 1 and reach == 0):
                continue
            there = gather.has_above(reach) if way else gather.has_below(reach)

            @pl.when(there)
            def _():
                base = gather.other if line else gather.row
                use(base + (reach if way else -reach) * SIDES)

    local_w.wait()
    for k in range(1, row_count):
        send_w(k).wait_recv()
    share_b[...] = jnp.sum(land_w[...], axis=0)
    for k in range(1, col_count):
        recv_q(k).wait_recv()
    for c in range(col_count):
        gram_b[:, c * quarter : (c + 1) * quarter] = quarters[c]
    for k in range(1, row_count):
        send_g(k).wait_send()
        send_w(k).wait_send()
        send_f(k).wait_send()
    for k in range(1, col_count):
        send_q(k).wait_send()

    def sent(slot, carry):
        to_twin(slot).wait_send()
        return carry

    lax.fori_loop(0, row_count, sent, 0)
    gather.drain()


def middle(proj_a, proj_b, buffer_b, tall):
    row_count, col_count = lax.axis_size("row"), lax.axis_size("col")
    rank, rows_a = proj_a.shape
    share, quarter = rank // row_count, rank // col_count
    width_a, width_b = tall.shape[2], buffer_b.shape[1]

    def array(*shape):
        return jax.ShapeDtypeStruct(shape, jnp.float32)

    def space(*shape):
        return pltpu.VMEM(shape, jnp.float32)

    rows, cols = DMA((row_count,)), DMA((col_count,))
    return pl.pallas_call(
        functools.partial(middle_kernel, row_count, col_count),
        out_shape=[array(rank, rank), array(rank, width_a), array(rank, rank), array(share, width_b)],
        in_specs=[VMEM] * 4,
        out_specs=[VMEM] * 4,
        scratch_shapes=[
            space(2, row_count, rank // 2, rows_a),
            space(rank, quarter),
            space(rank, width_b),
            space(row_count, share, quarter),
            space(row_count, share, width_b),
            space(share, quarter),
            space(col_count, rank, quarter),
        ]
        + Gather.scratch(row_count, 1)
        + [rows] * 6
        + [DMA(()), DMA(())]
        + [rows, rows, DMA(()), cols, cols],
        name="middle",
        compiler_params=pltpu.CompilerParams(
            collective_id=3, has_side_effects=True, vmem_limit_bytes=60 * 2**20
        ),
    )(proj_a, proj_b, buffer_b, tall)


def factor(rank, grams, outs, works, diags, between):
    eye_rows = lax.broadcasted_iota(jnp.int32, (rank, rank), 0)
    eye_cols = lax.broadcasted_iota(jnp.int32, (rank, rank), 1)
    for gram, work in zip(grams, works):
        work[:, :rank] = gram[...]
        work[:, rank:] = (eye_rows == eye_cols).astype(jnp.float32)
    rows = lax.broadcasted_iota(jnp.int32, (BLOCK, 1), 0)
    lanes = lax.broadcasted_iota(jnp.int32, (1, BLOCK), 1)
    for k in range(rank // BLOCK):
        low, high = k * BLOCK, (k + 1) * BLOCK
        for work, diag in zip(works, diags):
            diag[:, :BLOCK] = work[low:high, low:high]
            diag[:, BLOCK:] = (rows == lanes).astype(jnp.float32)

        def step(j, carry):
            for diag in diags:
                here = lanes == j
                row = diag[pl.ds(j, 1), :]
                col = jnp.sum(jnp.where(here, diag[:, :BLOCK], 0.0), axis=1, keepdims=True)
                pivot = jnp.sum(jnp.where(here, row[:, :BLOCK], 0.0), axis=1, keepdims=True)
                factor = jnp.where(rows > j, col * (1.0 / pivot), 0.0)
                diag[...] = diag[...] - factor * row
            return carry

        lax.fori_loop(0, BLOCK, step, 0)
        width = slice(low, rank + high)
        for work, diag in zip(works, diags):
            pivots = jnp.sum(
                jnp.where(rows == lanes, diag[:, :BLOCK], 0.0), axis=1, keepdims=True
            )
            inverse = diag[:, BLOCK:] * (1.0 / jnp.sqrt(pivots))
            panel = dot(inverse, work[low:high, width])
            work[low:high, width] = panel
            if high < rank:
                factors = panel[:, BLOCK : rank - low]
                work[high:, width] = work[high:, width] - dot(factors, panel, FIRST)
        between(k)
    for work, out in zip(works, outs):
        out[...] = work[:, rank:]


def products_kernel(row_count, rank, *refs):
    gram_a, gram_b, block_a, block_b, inv_a, inv_b, all_a, all_b = refs[:8]
    works, diags, sems = refs[8:10], refs[10:12], refs[12:19]
    row = lax.axis_index("row")
    barrier = pltpu.get_barrier_semaphore()
    greet_row(row, row_count, barrier)
    pl.semaphore_wait(barrier, row_count - 1)
    gather = Gather(row_count, [block_a, block_b], [all_a, all_b], sems)
    gather.start()
    early = min(rank // BLOCK, gather.depth)

    def between(k):
        if k + 1 < early:
            gather.forward(k + 1)

    factor(rank, [gram_a, gram_b], [inv_a, inv_b], works, diags, between)

    def later(d, carry):
        gather.forward(d)
        return carry

    lax.fori_loop(early, gather.depth, later, 0)
    gather.wait_side(0, 0)

    def landed(d, carry):
        @pl.when(gather.has_below(d))
        def _():
            gather.wait_side(0, d)

        @pl.when(gather.has_above(d))
        def _():
            gather.wait_side(1, d)

        return carry

    lax.fori_loop(1, gather.depth, landed, 0)
    for i in gather.each():
        gather.local(i).wait()
    gather.drain()


def products(gram_a, gram_b, block_a, block_b):
    row_count = lax.axis_size("row")
    rank = gram_a.shape[0]
    square = jax.ShapeDtypeStruct((rank, rank), jnp.float32)
    return pl.pallas_call(
        functools.partial(products_kernel, row_count, rank),
        out_shape=[square, square]
        + [jax.ShapeDtypeStruct((row_count,) + x.shape, jnp.float32) for x in (block_a, block_b)],
        in_specs=[VMEM] * 4,
        out_specs=[VMEM] * 4,
        scratch_shapes=[pltpu.VMEM((rank, 2 * rank), jnp.float32)] * 2
        + [pltpu.VMEM((BLOCK, 2 * BLOCK), jnp.float32)] * 2
        + Gather.scratch(row_count, 2),
        name="products",
        compiler_params=pltpu.CompilerParams(
            collective_id=2, has_side_effects=True, vmem_limit_bytes=60 * 2**20
        ),
    )(gram_a, gram_b, block_a, block_b)


def shards(mom_a, grad_a, basis_a, mom_b, grad_b, basis_b):
    row_count = lax.axis_size("row")
    buffer_a, buffer_b = MU * mom_a + grad_a, MU * mom_b + grad_b
    rows_a = buffer_a.shape[0]
    cut_a = buffer_a.reshape(rows_a, row_count, -1).swapaxes(0, 1)
    proj_a, proj_b, tall_a = project(basis_a, basis_b, buffer_a, buffer_b, cut_a)
    rank = proj_a.shape[0]
    share = rank // row_count

    gram_a, block_a, gram_b, share_b = middle(proj_a, proj_b, buffer_b, tall_a)
    inverse_a, inverse_b, product_a, product_b = products(gram_a, gram_b, block_a, share_b)
    product_a = product_a.swapaxes(0, 1).reshape(rank, -1)
    product_b = product_b.reshape(rank, -1)

    ortho_a, ortho_b = dot(proj_a, inverse_a, ((0,), (1,))), dot(proj_b, inverse_b, ((0,), (1,)))
    trans_a, trans_b = dot(inverse_a, product_a), dot(inverse_b, product_b)
    squares_a, squares_b = lax.psum(
        (
            jnp.sum(trans_a * trans_a, axis=1, keepdims=True),
            jnp.sum(trans_b * trans_b, axis=1, keepdims=True),
        ),
        "col",
    )
    start = lax.axis_index("row") * share
    first_out = finish(buffer_a, ortho_a, trans_a, squares_a, start, share)
    second_out = finish(buffer_b, ortho_b, trans_b, squares_b, start, share)
    return (*first_out, *second_out)


def finish(buffer, ortho, trans, squares, start, share):
    rank = ortho.shape[1]
    total_rows = buffer.shape[0] * lax.axis_size("row")
    total_cols = buffer.shape[1] * lax.axis_size("col")
    full_basis = trans / jnp.sqrt(squares + EPS)
    own_basis = lax.dynamic_slice_in_dim(full_basis, start, share, 0)
    new_mom = buffer - (1.0 - MU) * dot(ortho, trans)
    update = dot(ortho, full_basis) * math.sqrt(total_rows * total_cols / rank)
    return new_mom, update.astype(jnp.bfloat16), own_basis


def solution(mesh):
    spec = P("row", "col")
    return jax.shard_map(
        shards, mesh=mesh, in_specs=(spec,) * 6, out_specs=(spec,) * 6, check_vma=False
    )
```

```python
import functools
import math

import jax
import jax.numpy as jnp
from jax import lax
from jax.experimental import pallas as pl
from jax.experimental.pallas import tpu as pltpu
from jax.sharding import PartitionSpec as P

MU = 0.95
EPS = 1e-06
BLOCK = 128
HIGHEST = lax.Precision.HIGHEST
MESH = pl.DeviceIdType.MESH
VMEM = pl.BlockSpec(memory_space=pltpu.VMEM)
DMA = pltpu.SemaphoreType.DMA
LAST = ((1,), (1,))
FIRST = ((0,), (0,))
PLAIN = ((1,), (0,))
SIDES = 2


def dot(x, y, contract=PLAIN, precision=HIGHEST):
    return lax.dot_general(
        x, y, (contract, ((), ())), precision=precision, preferred_element_type=jnp.float32
    )


def halves(x):
    high = x.astype(jnp.bfloat16)
    return high, (x - high.astype(jnp.float32)).astype(jnp.bfloat16)


def narrow_dot(x, y, contract=PLAIN):
    return lax.dot_general(x, y, (contract, ((), ())), preferred_element_type=jnp.float32)


def split_dot(x, y, contract=PLAIN):
    (x_high, x_low), (y_high, y_low) = halves(x), halves(y)
    total = narrow_dot(x_high, y_low, contract) + narrow_dot(x_low, y_high, contract)
    return total + narrow_dot(x_high, y_high, contract)


def remote(src, dst, send, recv, device):
    return pltpu.make_async_remote_copy(
        src_ref=src,
        dst_ref=dst,
        send_sem=send,
        recv_sem=recv,
        device_id=device,
        device_id_type=MESH,
    )


def partner(position, bit):
    return position + bit - 2 * bit * lax.rem(position // bit, 2)


def col_bits(col_count):
    bits, bit = [], 1
    while bit < col_count:
        bits.append(bit)
        bit *= 2
    return bits


def greet_row(row, row_count, barrier):
    for k in range(1, row_count):
        peer = lax.rem(row + k, row_count)
        pl.semaphore_signal(barrier, inc=1, device_id={"row": peer}, device_id_type=MESH)


def greet_cols(col, bits, barrier):
    for bit in bits:
        peer = partner(col, bit)
        pl.semaphore_signal(barrier, inc=1, device_id={"col": peer}, device_id_type=MESH)


class Gather:
    def __init__(self, row_count, sources, outs, sems):
        self.depth = row_count // SIDES
        self.row = lax.axis_index("row")
        self.place = self.row // SIDES
        lane = lax.rem(self.row, SIDES)
        self.other = self.place * SIDES + (1 - lane)
        self.sources, self.outs = sources, outs
        self.up_s, self.up_r, self.dn_s, self.dn_r, self.side_s, self.side_r, self.own = sems
        self.has_up = self.place < self.depth - 1
        self.has_dn = self.place > 0

    @staticmethod
    def scratch(row_count, count):
        depth = row_count // SIDES
        line = DMA((count, depth))
        side = DMA((count, 2, depth))
        return [line, line, line, line, side, side, DMA((count,))]

    def up(self, i, slot, d, first=False):
        src = self.sources[i] if first else self.outs[i].at[slot]
        device = {"row": self.row + SIDES}
        return remote(src, self.outs[i].at[slot], self.up_s.at[i, d], self.up_r.at[i, d], device)

    def dn(self, i, slot, d, first=False):
        src = self.sources[i] if first else self.outs[i].at[slot]
        device = {"row": self.row - SIDES}
        return remote(src, self.outs[i].at[slot], self.dn_s.at[i, d], self.dn_r.at[i, d], device)

    def side(self, i, slot, way, d, first=False):
        src = self.sources[i] if first else self.outs[i].at[slot]
        sems = self.side_s.at[i, way, d], self.side_r.at[i, way, d]
        return remote(src, self.outs[i].at[slot], *sems, {"row": self.other})

    def local(self, i):
        return pltpu.make_async_copy(self.sources[i], self.outs[i].at[self.row], self.own.at[i])

    def each(self):
        return range(len(self.sources))

    def start(self):
        for i in self.each():

            @pl.when(self.has_up)
            def _():
                self.up(i, self.row, 0, True).start()

            @pl.when(self.has_dn)
            def _():
                self.dn(i, self.row, 0, True).start()

            self.side(i, self.row, 0, 0, True).start()
        for i in self.each():
            self.local(i).start()

    def below(self, d):
        return self.row - d * SIDES

    def above(self, d):
        return self.row + d * SIDES

    def has_below(self, d):
        return self.place - d >= 0

    def has_above(self, d):
        return self.place + d < self.depth

    def forward(self, d):
        low, high = self.below(d), self.above(d)

        @pl.when(self.has_below(d))
        def _():
            for i in self.each():
                self.up(i, low, d - 1).wait_recv()

                @pl.when(self.has_up)
                def _():
                    self.up(i, low, d).start()

                self.side(i, low, 0, d).start()

        @pl.when(self.has_above(d))
        def _():
            for i in self.each():
                self.dn(i, high, d - 1).wait_recv()

                @pl.when(self.has_dn)
                def _():
                    self.dn(i, high, d).start()

                self.side(i, high, 1, d).start()

    def across(self, way, d):
        return self.other + d * SIDES * (2 * way - 1)

    def wait_side(self, way, d):
        for i in self.each():
            self.side(i, self.across(way, d), way, d).wait_recv()

    def drain(self):
        for i in self.each():

            @pl.when(self.has_up)
            def _():
                self.up(i, self.row, 0, True).wait_send()

            @pl.when(self.has_dn)
            def _():
                self.dn(i, self.row, 0, True).wait_send()

            self.side(i, self.row, 0, 0, True).wait_send()

        def later(d, carry):
            for i in self.each():

                @pl.when(self.has_below(d))
                def _():
                    @pl.when(self.has_up)
                    def _():
                        self.up(i, self.below(d), d).wait_send()

                    self.side(i, self.below(d), 0, d).wait_send()

                @pl.when(self.has_above(d))
                def _():
                    @pl.when(self.has_dn)
                    def _():
                        self.dn(i, self.above(d), d).wait_send()

                    self.side(i, self.above(d), 1, d).wait_send()

            return carry

        lax.fori_loop(1, self.depth, later, 0)


class ColSum:
    def __init__(self, bits, sums, landed, send, recv):
        self.bits, self.sums, self.landed, self.send, self.recv = bits, sums, landed, send, recv
        self.col = lax.axis_index("col")

    def copy(self, stage):
        device = {"col": partner(self.col, self.bits[stage])}
        sems = self.send.at[stage], self.recv.at[stage]
        return remote(self.sums[stage], self.landed[stage], *sems, device)

    def finish(self, stage):
        self.copy(stage).wait_recv()
        self.sums[stage + 1][...] = self.sums[stage][...] + self.landed[stage][...]

    def drain(self):
        for stage in range(len(self.bits)):
            self.copy(stage).wait_send()


def project_kernel(row_count, bits, *refs):
    stages = len(bits)
    basis_a, basis_b, buffer_a, buffer_b, cut_a, out_a, out_b, tall = refs[:8]
    all_a, all_b, high_a, low_a = refs[8:12]
    refs = refs[12:]
    sums_a = list(refs[:stages]) + [out_a]
    sums_b = list(refs[stages : 2 * stages]) + [out_b]
    landed_a = refs[2 * stages : 3 * stages]
    landed_b = refs[3 * stages : 4 * stages]
    gather_sems = refs[4 * stages : 7 + 4 * stages]
    small_s, small_r, small_own, cut_s, cut_r, cut_own = refs[7 + 4 * stages : 13 + 4 * stages]
    cs_a, cr_a, cs_b, cr_b = refs[13 + 4 * stages :]
    row, col = lax.axis_index("row"), lax.axis_index("col")
    share = basis_a.shape[0]
    depth = row_count // SIDES

    barrier = pltpu.get_barrier_semaphore()
    greet_row(row, row_count, barrier)
    greet_cols(col, bits, barrier)
    pl.semaphore_wait(barrier, row_count - 1 + stages)

    def small(k):
        peer = lax.rem(row + k, row_count)
        return remote(basis_b, all_b.at[row], small_s.at[k], small_r.at[k], {"row": peer})

    def cut(k):
        peer = lax.rem(row + k, row_count)
        return remote(cut_a.at[peer], tall.at[row], cut_s.at[k], cut_r.at[k], {"row": peer})

    small_local = pltpu.make_async_copy(basis_b, all_b.at[row], small_own)
    cut_local = pltpu.make_async_copy(cut_a.at[row], tall.at[row], cut_own)
    for k in range(1, row_count):
        small(k).start()
    gather = Gather(row_count, [basis_a], [all_a], gather_sems)
    gather.start()
    small_local.start()
    cut_local.start()

    def project(slot):
        rows = pl.ds(pl.multiple_of(slot * share, share), share)
        basis_high, basis_low = halves(all_a[slot])
        total = narrow_dot(basis_high, low_a[...], LAST) + narrow_dot(basis_low, high_a[...], LAST)
        sums_a[0][rows, :] = total + narrow_dot(basis_high, high_a[...], LAST)

    high_a[...], low_a[...] = halves(buffer_a[...])

    gather.local(0).wait()
    project(row)
    small_local.wait()
    for k in range(1, row_count):
        small(k).wait_recv()
    flat_b = all_b[...].reshape(row_count * share, basis_b.shape[1])
    sums_b[0][...] = split_dot(flat_b, buffer_b[...], LAST)
    total_a = ColSum(bits, sums_a, landed_a, cs_a, cr_a)
    total_b = ColSum(bits, sums_b, landed_b, cs_b, cr_b)
    total_b.copy(0).start()

    def advance(d, carry):
        gather.forward(d)

        for stage in range(stages):

            @pl.when(d == min(stage + 1, depth - 1))
            def _():
                total_b.finish(stage)
                if stage + 1 < stages:
                    total_b.copy(stage + 1).start()

        @pl.when(d == min(2, depth - 1))
        def _():
            for k in range(1, row_count):
                cut(k).start()

        @pl.when(gather.has_below(d - 1))
        def _():
            gather.wait_side(0, d - 1)

        @pl.when((d > 1) & gather.has_above(d - 1))
        def _():
            gather.wait_side(1, d - 1)

        def use(k, inner):
            line, way = k // 2, lax.rem(k, 2)
            step = (d - line) * (2 * way - 1)
            there = gather.place + step
            here = (there >= 0) & (there < depth) & ((way == 0) | (d - line > 0))

            @pl.when(here)
            def _():
                base = gather.row + line * (gather.other - gather.row)
                project(base + step * SIDES)

            return inner

        lax.fori_loop(0, 4, use, 0)
        return carry

    lax.fori_loop(1, depth, advance, 0)
    def finish(way, carry):
        step = (depth - 1) * (2 * way - 1)
        there = gather.place + step

        @pl.when((there >= 0) & (there < depth))
        def _():
            project(gather.other + step * SIDES)

        return carry

    @pl.when(gather.has_below(depth - 1))
    def _():
        gather.wait_side(0, depth - 1)

    @pl.when(gather.has_above(depth - 1))
    def _():
        gather.wait_side(1, depth - 1)

    lax.fori_loop(0, 2, finish, 0)
    for stage in range(stages):
        total_a.copy(stage).start()
        total_a.finish(stage)
    cut_local.wait()
    for k in range(1, row_count):
        cut(k).wait()
        small(k).wait_send()
    gather.drain()
    total_a.drain()
    total_b.drain()


def project(basis_a, basis_b, buffer_a, buffer_b, cut_a):
    row_count, col_count = lax.axis_size("row"), lax.axis_size("col")
    bits = col_bits(col_count)
    stages = len(bits)
    share, rows_a, rows_b = basis_a.shape[0], buffer_a.shape[0], buffer_b.shape[0]
    rank = share * row_count
    float_a, float_b = (
        jax.ShapeDtypeStruct((rank, rows_a), jnp.float32),
        jax.ShapeDtypeStruct((rank, rows_b), jnp.float32),
    )
    space_a, space_b = pltpu.VMEM(float_a.shape, jnp.float32), pltpu.VMEM(float_b.shape, jnp.float32)
    return pl.pallas_call(
        functools.partial(project_kernel, row_count, bits),
        out_shape=[float_a, float_b, jax.ShapeDtypeStruct(cut_a.shape, jnp.float32)],
        in_specs=[VMEM] * 5,
        out_specs=[VMEM] * 3,
        scratch_shapes=[
            pltpu.VMEM((row_count,) + basis_a.shape, jnp.float32),
            pltpu.VMEM((row_count,) + basis_b.shape, jnp.float32),
            pltpu.VMEM(buffer_a.shape, jnp.bfloat16),
            pltpu.VMEM(buffer_a.shape, jnp.bfloat16),
        ]
        + [space_a] * stages
        + [space_b] * stages
        + [space_a] * stages
        + [space_b] * stages
        + Gather.scratch(row_count, 1)
        + [DMA((row_count,)), DMA((row_count,)), DMA(())] * 2
        + [DMA((stages,))] * 4,
        name="project",
        compiler_params=pltpu.CompilerParams(
            collective_id=1, has_side_effects=True, vmem_limit_bytes=60 * 2**20
        ),
    )(basis_a, basis_b, buffer_a, buffer_b, cut_a)


def middle_kernel(row_count, col_count, *refs):
    proj_a, proj_b, buffer_b, tall, gram_a, block_a, gram_b, share_b = refs[:8]
    all_a, part_g, part_w, land_g, land_w, own_g, quarters = refs[8:15]
    gather_sems = refs[15:22]
    twin_s, twin_r, gs, gr, ws, wr, g_own, w_own, fs, fr, f_own, qs, qr = refs[22:]
    row, col = lax.axis_index("row"), lax.axis_index("col")
    rank = proj_a.shape[0]
    share, quarter, half = rank // row_count, rank // col_count, rank // 2
    twin = partner(col, 1)
    side = lax.rem(col, 2)

    barrier = pltpu.get_barrier_semaphore()
    greet_row(row, row_count, barrier)
    for k in range(1, col_count):
        peer = lax.rem(col + k, col_count)
        pl.semaphore_signal(barrier, inc=1, device_id={"col": peer}, device_id_type=MESH)
    pl.semaphore_wait(barrier, row_count + col_count - 2)

    source = proj_a.at[pl.ds(pl.multiple_of(side * half, half), half), :]
    gather = Gather(row_count, [source], [all_a.at[side]], gather_sems)
    gather.start()

    def to_twin(slot):
        here = all_a.at[side, slot]
        return remote(here, here, twin_s.at[slot], twin_r.at[slot], {"col": twin})

    def from_twin(slot):
        there = all_a.at[1 - side, slot]
        return remote(there, there, twin_s.at[slot], twin_r.at[slot], {"col": twin})

    def rows_of(position):
        return pl.ds(pl.multiple_of(position * share, share), share)

    def send_g(k):
        peer = lax.rem(row + k, row_count)
        return remote(part_g.at[rows_of(peer), :], land_g.at[row], gs.at[k], gr.at[k], {"row": peer})

    def send_w(k):
        peer = lax.rem(row + k, row_count)
        return remote(part_w.at[rows_of(peer), :], land_w.at[row], ws.at[k], wr.at[k], {"row": peer})

    def send_f(k):
        peer = lax.rem(row + k, row_count)
        target = quarters.at[col, rows_of(row), :]
        return remote(own_g, target, fs.at[k], fr.at[k], {"row": peer})

    def send_q(k):
        peer = lax.rem(col + k, col_count)
        here = quarters.at[col]
        return remote(here, here, qs.at[k], qr.at[k], {"col": peer})

    def recv_q(k):
        peer = lax.rem(col + col_count - k, col_count)
        there = quarters.at[peer]
        return remote(there, there, qs.at[k], qr.at[k], {"col": peer})

    local_g = pltpu.make_async_copy(part_g.at[rows_of(row), :], land_g.at[row], g_own)
    local_w = pltpu.make_async_copy(part_w.at[rows_of(row), :], land_w.at[row], w_own)
    local_f = pltpu.make_async_copy(own_g, quarters.at[col, rows_of(row), :], f_own)

    some_b = proj_b[pl.ds(pl.multiple_of(col * quarter, quarter), quarter), :]
    part_g[...] = dot(proj_b[...], some_b, LAST)
    for k in range(1, row_count):
        send_g(k).start()
    local_g.start()
    part_w[...] = split_dot(proj_b[...], buffer_b[...])
    for k in range(1, row_count):
        send_w(k).start()
    local_w.start()
    gram_a[...] = jnp.zeros_like(gram_a)
    block_a[...] = jnp.zeros_like(block_a)
    gather.local(0).wait()
    to_twin(row).start()

    def use(slot):
        from_twin(slot).wait_recv()
        rows = jnp.concatenate([all_a[0, slot], all_a[1, slot]], axis=0)
        gram_a[...] += dot(rows, rows, LAST)
        block_a[...] += split_dot(rows, tall[slot])

    def advance(d, carry):
        gather.forward(d)

        @pl.when(gather.has_below(d))
        def _():
            to_twin(gather.below(d)).start()

        @pl.when(gather.has_above(d))
        def _():
            to_twin(gather.above(d)).start()

        @pl.when(gather.has_below(d - 1))
        def _():
            gather.wait_side(0, d - 1)
            to_twin(gather.across(0, d - 1)).start()

        @pl.when((d > 1) & gather.has_above(d - 1))
        def _():
            gather.wait_side(1, d - 1)
            to_twin(gather.across(1, d - 1)).start()

        @pl.when(d == min(2, gather.depth - 1))
        def _():
            reduce_g()

        def candidate(k, inner):
            line, way = k // 2, lax.rem(k, 2)
            reach = d - 1 - line
            step = reach * (2 * way - 1)
            there = gather.place + step
            here = (reach >= 0) & (there >= 0) & (there < gather.depth) & ((way == 0) | (reach > 0))

            @pl.when(here)
            def _():
                use(gather.row + line * (gather.other - gather.row) + step * SIDES)

            return inner

        lax.fori_loop(0, 4, candidate, 0)
        return carry

    def reduce_g():
        local_g.wait()
        for k in range(1, row_count):
            send_g(k).wait_recv()
        own_g[...] = jnp.sum(land_g[...], axis=0)
        for k in range(1, row_count):
            send_f(k).start()
        local_f.start()

    lax.fori_loop(1, gather.depth, advance, 0)
    last = gather.depth - 1

    @pl.when(gather.has_below(last))
    def _():
        gather.wait_side(0, last)
        to_twin(gather.across(0, last)).start()

    @pl.when(gather.has_above(last))
    def _():
        gather.wait_side(1, last)
        to_twin(gather.across(1, last)).start()

    for k in range(1, row_count):
        send_f(k).wait_recv()
    local_f.wait()
    for k in range(1, col_count):
        send_q(k).start()

    remaining_blocks = [(0, 0), (1, 1), (1, 0)]
    for line, back in remaining_blocks:
        for way in range(2):
            reach = last - back
            if reach < 0 or (way == 1 and reach == 0):
                continue
            there = gather.has_above(reach) if way else gather.has_below(reach)

            @pl.when(there)
            def _():
                base = gather.other if line else gather.row
                use(base + (reach if way else -reach) * SIDES)

    local_w.wait()
    for k in range(1, row_count):
        send_w(k).wait_recv()
    share_b[...] = jnp.sum(land_w[...], axis=0)
    for k in range(1, col_count):
        recv_q(k).wait_recv()
    for c in range(col_count):
        gram_b[:, c * quarter : (c + 1) * quarter] = quarters[c]
    for k in range(1, row_count):
        send_g(k).wait_send()
        send_w(k).wait_send()
        send_f(k).wait_send()
    for k in range(1, col_count):
        send_q(k).wait_send()

    def sent(slot, carry):
        to_twin(slot).wait_send()
        return carry

    lax.fori_loop(0, row_count, sent, 0)
    gather.drain()


def middle(proj_a, proj_b, buffer_b, tall):
    row_count, col_count = lax.axis_size("row"), lax.axis_size("col")
    rank, rows_a = proj_a.shape
    share, quarter = rank // row_count, rank // col_count
    width_a, width_b = tall.shape[2], buffer_b.shape[1]

    def array(*shape):
        return jax.ShapeDtypeStruct(shape, jnp.float32)

    def space(*shape):
        return pltpu.VMEM(shape, jnp.float32)

    rows, cols = DMA((row_count,)), DMA((col_count,))
    return pl.pallas_call(
        functools.partial(middle_kernel, row_count, col_count),
        out_shape=[array(rank, rank), array(rank, width_a), array(rank, rank), array(share, width_b)],
        in_specs=[VMEM] * 4,
        out_specs=[VMEM] * 4,
        scratch_shapes=[
            space(2, row_count, rank // 2, rows_a),
            space(rank, quarter),
            space(rank, width_b),
            space(row_count, share, quarter),
            space(row_count, share, width_b),
            space(share, quarter),
            space(col_count, rank, quarter),
        ]
        + Gather.scratch(row_count, 1)
        + [rows] * 6
        + [DMA(()), DMA(())]
        + [rows, rows, DMA(()), cols, cols],
        name="middle",
        compiler_params=pltpu.CompilerParams(
            collective_id=3, has_side_effects=True, vmem_limit_bytes=60 * 2**20
        ),
    )(proj_a, proj_b, buffer_b, tall)


def factor(rank, grams, outs, works, diags, between):
    eye_rows = lax.broadcasted_iota(jnp.int32, (rank, rank), 0)
    eye_cols = lax.broadcasted_iota(jnp.int32, (rank, rank), 1)
    for gram, work in zip(grams, works):
        work[:, :rank] = gram[...]
        work[:, rank:] = (eye_rows == eye_cols).astype(jnp.float32)
    rows = lax.broadcasted_iota(jnp.int32, (BLOCK, 1), 0)
    lanes = lax.broadcasted_iota(jnp.int32, (1, BLOCK), 1)
    for k in range(rank // BLOCK):
        low, high = k * BLOCK, (k + 1) * BLOCK
        for work, diag in zip(works, diags):
            diag[:, :BLOCK] = work[low:high, low:high]
            diag[:, BLOCK:] = (rows == lanes).astype(jnp.float32)

        def step(j, carry):
            for diag in diags:
                here = lanes == j
                row = diag[pl.ds(j, 1), :]
                col = jnp.sum(jnp.where(here, diag[:, :BLOCK], 0.0), axis=1, keepdims=True)
                pivot = jnp.sum(jnp.where(here, row[:, :BLOCK], 0.0), axis=1, keepdims=True)
                factor = jnp.where(rows > j, col * (1.0 / pivot), 0.0)
                diag[...] = diag[...] - factor * row
            return carry

        lax.fori_loop(0, BLOCK, step, 0)
        width = slice(low, rank + high)
        for work, diag in zip(works, diags):
            pivots = jnp.sum(
                jnp.where(rows == lanes, diag[:, :BLOCK], 0.0), axis=1, keepdims=True
            )
            inverse = diag[:, BLOCK:] * (1.0 / jnp.sqrt(pivots))
            panel = dot(inverse, work[low:high, width])
            work[low:high, width] = panel
            if high < rank:
                factors = panel[:, BLOCK : rank - low]
                work[high:, width] = work[high:, width] - dot(factors, panel, FIRST)
        between(k)
    for work, out in zip(works, outs):
        out[...] = work[:, rank:]


def products_kernel(row_count, col_count, rank, scales, *refs):
    gram_a, gram_b, block_a, block_b, proj_a, proj_b = refs[:6]
    trans_a, trans_b, basis_a, basis_b = refs[6:10]
    ortho_a, ortho_b, scaled_a, scaled_b = refs[10:14]
    all_a, all_b, inv_a, inv_b, high_a, low_a, wide_a, wide_b, full_a, full_b = refs[14:24]
    square_a, square_b, mine, theirs = refs[24:28]
    works, diags, sems, (sq_s, sq_r) = refs[28:30], refs[30:32], refs[32:39], refs[39:]
    row, col = lax.axis_index("row"), lax.axis_index("col")
    share = rank // row_count
    barrier = pltpu.get_barrier_semaphore()
    greet_row(row, row_count, barrier)
    for k in range(1, col_count):
        peer = lax.rem(col + k, col_count)
        pl.semaphore_signal(barrier, inc=1, device_id={"col": peer}, device_id_type=MESH)
    pl.semaphore_wait(barrier, row_count + col_count - 2)
    gather = Gather(row_count, [block_b, block_a], [all_b, all_a], sems)
    gather.start()
    early = min(rank // BLOCK, gather.depth)

    def between(k):
        if k + 1 < early:
            gather.forward(k + 1)

    factor(rank, [gram_a, gram_b], [inv_a, inv_b], works, diags, between)

    def later(d, carry):
        gather.forward(d)
        return carry

    lax.fori_loop(early, gather.depth, later, 0)
    for i in gather.each():
        gather.local(i).wait()
    high_a[...], low_a[...] = halves(inv_a[...])
    wide_a[...] = split_dot(proj_a[...].T, inv_a[...], LAST)
    wide_b[...] = split_dot(proj_b[...].T, inv_b[...], LAST)
    ortho_a[...] = wide_a[...].astype(jnp.bfloat16)
    ortho_b[...] = wide_b[...].astype(jnp.bfloat16)
    square_a[...] = jnp.zeros_like(square_a)
    own = pl.ds(pl.multiple_of(row * share, share), share)

    def use(slot):
        product_high, product_low = halves(all_a[slot])
        total = narrow_dot(high_a[...], product_low) + narrow_dot(low_a[...], product_high)
        total = total + narrow_dot(high_a[...], product_high)
        full_a[...] = total
        trans_a[slot] = total.astype(jnp.bfloat16)
        square_a[...] += jnp.sum(total * total, axis=1, keepdims=True)
        basis_a[slot] = full_a[own, :]

    def each(k, carry):
        line, d, way = k // (2 * gather.depth), lax.rem(k, 2 * gather.depth) // 2, lax.rem(k, 2)
        step = d * (2 * way - 1)
        there = gather.place + step
        here = (there >= 0) & (there < gather.depth) & ((way == 0) | (d > 0))

        @pl.when(here & (line == 1))
        def _():
            gather.wait_side(way, d)

        @pl.when(here)
        def _():
            use(gather.row + line * (gather.other - gather.row) + step * SIDES)

        return carry

    lax.fori_loop(0, 4 * gather.depth, each, 0)
    total_b = split_dot(inv_b[...], all_b[...].reshape(rank, all_b.shape[2]))
    full_b[...] = total_b
    trans_b[...] = total_b.astype(jnp.bfloat16)
    square_b[...] = jnp.sum(total_b * total_b, axis=1, keepdims=True)

    def across(column):
        return jnp.broadcast_to(column, (rank, BLOCK)).T[:8]

    def norms(k):
        peer = lax.rem(col + k, col_count)
        return remote(mine, theirs.at[col], sq_s.at[k], sq_r.at[k], {"col": peer})

    mine[0] = across(square_a[...])
    mine[1] = across(square_b[...])
    for k in range(1, col_count):
        norms(k).start()
    theirs[col] = mine[...]
    for k in range(1, col_count):
        norms(k).wait_recv()
    norm = jnp.sqrt(jnp.sum(theirs[...], axis=0) + EPS)
    norm_a, norm_b = norm[0, :1], norm[1, :1]
    scaled_a[...] = (wide_a[...] * (scales[0] / norm_a)).astype(jnp.bfloat16)
    scaled_b[...] = (wide_b[...] * (scales[1] / norm_b)).astype(jnp.bfloat16)
    ranks = lax.broadcasted_iota(jnp.int32, (share, rank), 1)
    owned = lax.broadcasted_iota(jnp.int32, (share, rank), 0) + row * share
    own_a = jnp.sum(jnp.where(ranks == owned, norm_a, 0.0), axis=1, keepdims=True)
    own_b = jnp.sum(jnp.where(ranks == owned, norm_b, 0.0), axis=1, keepdims=True)
    for k in range(row_count):
        basis_a[k] = basis_a[k] / own_a
    basis_b[...] = full_b[own, :] / own_b
    for k in range(1, col_count):
        norms(k).wait_send()
    gather.drain()


def products(gram_a, gram_b, block_a, block_b, proj_a, proj_b, scales):
    row_count, col_count = lax.axis_size("row"), lax.axis_size("col")
    rank = gram_a.shape[0]
    share = rank // row_count
    width_a, width_b = block_a.shape[1], block_b.shape[1]
    rows_a, rows_b = proj_a.shape[1], proj_b.shape[1]

    def array(kind, *shape):
        return jax.ShapeDtypeStruct(shape, kind)

    def space(*shape):
        return pltpu.VMEM(shape, jnp.float32)

    narrow, wide = jnp.bfloat16, jnp.float32
    cols = DMA((col_count,))
    return pl.pallas_call(
        functools.partial(products_kernel, row_count, col_count, rank, scales),
        out_shape=[
            array(narrow, row_count, rank, width_a),
            array(narrow, rank, width_b),
            array(wide, row_count, share, width_a),
            array(wide, share, width_b),
            array(narrow, rows_a, rank),
            array(narrow, rows_b, rank),
            array(narrow, rows_a, rank),
            array(narrow, rows_b, rank),
        ],
        in_specs=[VMEM] * 6,
        out_specs=[VMEM] * 8,
        scratch_shapes=[
            space(row_count, rank, width_a),
            space(row_count, share, width_b),
            space(rank, rank),
            space(rank, rank),
            pltpu.VMEM((rank, rank), narrow),
            pltpu.VMEM((rank, rank), narrow),
            space(rows_a, rank),
            space(rows_b, rank),
            space(rank, width_a),
            space(rank, width_b),
            space(rank, 1),
            space(rank, 1),
            space(2, 8, rank),
            space(col_count, 2, 8, rank),
        ]
        + [space(rank, 2 * rank)] * 2
        + [space(BLOCK, 2 * BLOCK)] * 2
        + Gather.scratch(row_count, 2)
        + [cols, cols],
        name="products",
        compiler_params=pltpu.CompilerParams(
            collective_id=2, has_side_effects=True, vmem_limit_bytes=60 * 2**20
        ),
    )(gram_a, gram_b, block_a, block_b, proj_a, proj_b)


def ending_kernel(*refs):
    buffer_a, trans_a, basis_a, ortho_a, scaled_a = refs[:5]
    buffer_b, trans_b, ortho_b, scaled_b = refs[5:9]
    mom_a, update_a, new_a, mom_b, update_b = refs[9:]
    mom_a[...] = buffer_a[...] - (1.0 - MU) * narrow_dot(ortho_a[...], trans_a[0])
    update_a[...] = narrow_dot(scaled_a[...], trans_a[0]).astype(jnp.bfloat16)
    new_a[...] = basis_a[0]
    mom_b[...] = buffer_b[...] - (1.0 - MU) * narrow_dot(ortho_b[...], trans_b[...])
    update_b[...] = narrow_dot(scaled_b[...], trans_b[...]).astype(jnp.bfloat16)


def ending(buffer_a, trans_a, basis_a, ortho_a, scaled_a, buffer_b, trans_b, ortho_b, scaled_b):
    steps, rank, width = trans_a.shape
    rows_a, rows_b, share = buffer_a.shape[0], buffer_b.shape[0], basis_a.shape[1]
    if width % 128 or rows_b % (16 * steps):
        flat = trans_a.swapaxes(0, 1).reshape(rank, -1)
        return (
            buffer_a - (1.0 - MU) * narrow_dot(ortho_a, flat),
            narrow_dot(scaled_a, flat).astype(jnp.bfloat16),
            basis_a.swapaxes(0, 1).reshape(share, -1),
            buffer_b - (1.0 - MU) * narrow_dot(ortho_b, trans_b),
            narrow_dot(scaled_b, trans_b).astype(jnp.bfloat16),
        )
    some = rows_b // steps
    cut = pl.BlockSpec((rows_a, width), lambda j: (0, j))
    stack = pl.BlockSpec((1, rank, width), lambda j: (j, 0, 0))
    thin = pl.BlockSpec((1, share, width), lambda j: (j, 0, 0))
    fixed_a = pl.BlockSpec((rows_a, rank), lambda j: (0, 0))
    fixed_b = pl.BlockSpec(trans_b.shape, lambda j: (0, 0))
    slab = pl.BlockSpec((some, buffer_b.shape[1]), lambda j: (j, 0))
    rows = pl.BlockSpec((some, rank), lambda j: (j, 0))
    return pl.pallas_call(
        ending_kernel,
        grid=(steps,),
        out_shape=[
            jax.ShapeDtypeStruct(buffer_a.shape, jnp.float32),
            jax.ShapeDtypeStruct(buffer_a.shape, jnp.bfloat16),
            jax.ShapeDtypeStruct((share, buffer_a.shape[1]), jnp.float32),
            jax.ShapeDtypeStruct(buffer_b.shape, jnp.float32),
            jax.ShapeDtypeStruct(buffer_b.shape, jnp.bfloat16),
        ],
        in_specs=[cut, stack, thin, fixed_a, fixed_a, slab, fixed_b, rows, rows],
        out_specs=[cut, cut, pl.BlockSpec((share, width), lambda j: (0, j)), slab, slab],
        name="ending",
    )(buffer_a, trans_a, basis_a, ortho_a, scaled_a, buffer_b, trans_b, ortho_b, scaled_b)


def shards(mom_a, grad_a, basis_a, mom_b, grad_b, basis_b):
    row_count = lax.axis_size("row")
    buffer_a, buffer_b = MU * mom_a + grad_a, MU * mom_b + grad_b
    rows_a = buffer_a.shape[0]
    cut_a = buffer_a.reshape(rows_a, row_count, -1).swapaxes(0, 1)
    proj_a, proj_b, tall_a = project(basis_a, basis_b, buffer_a, buffer_b, cut_a)
    gram_a, block_a, gram_b, share_b = middle(proj_a, proj_b, buffer_b, tall_a)
    rank = gram_a.shape[0]
    scales = [
        math.sqrt(x.shape[0] * x.shape[1] * row_count * lax.axis_size("col") / rank)
        for x in (buffer_a, buffer_b)
    ]
    trans_a, trans_b, basis_a, basis_b, ortho_a, ortho_b, scaled_a, scaled_b = products(
        gram_a, gram_b, block_a, share_b, proj_a, proj_b, scales
    )
    new_mom_a, update_a, new_basis_a, new_mom_b, update_b = ending(
        buffer_a, trans_a, basis_a, ortho_a, scaled_a, buffer_b, trans_b, ortho_b, scaled_b
    )
    return new_mom_a, update_a, new_basis_a, new_mom_b, update_b, basis_b


def solution(mesh):
    spec = P("row", "col")
    return jax.shard_map(
        shards, mesh=mesh, in_specs=(spec,) * 6, out_specs=(spec,) * 6, check_vma=False
    )
```

```python
import functools
import math

import jax
import jax.numpy as jnp
from jax import lax
from jax.experimental import pallas as pl
from jax.experimental.pallas import tpu as pltpu
from jax.sharding import PartitionSpec as P

MU = 0.95
EPS = 1e-06
BLOCK = 128
HIGHEST = lax.Precision.HIGHEST
MESH = pl.DeviceIdType.MESH
VMEM = pl.BlockSpec(memory_space=pltpu.VMEM)
DMA = pltpu.SemaphoreType.DMA
LAST = ((1,), (1,))
FIRST = ((0,), (0,))
PLAIN = ((1,), (0,))
SIDES = 2
PIECES = 2
CHUNK = 256


def dot(x, y, contract=PLAIN, precision=HIGHEST):
    return lax.dot_general(
        x, y, (contract, ((), ())), precision=precision, preferred_element_type=jnp.float32
    )


def halves(x):
    high = x.astype(jnp.bfloat16)
    return high, (x - high.astype(jnp.float32)).astype(jnp.bfloat16)


def narrow_dot(x, y, contract=PLAIN):
    return lax.dot_general(x, y, (contract, ((), ())), preferred_element_type=jnp.float32)


def split_dot(x, y, contract=PLAIN):
    (x_high, x_low), (y_high, y_low) = halves(x), halves(y)
    total = narrow_dot(x_high, y_low, contract) + narrow_dot(x_low, y_high, contract)
    return total + narrow_dot(x_high, y_high, contract)


def remote(src, dst, send, recv, device):
    return pltpu.make_async_remote_copy(
        src_ref=src,
        dst_ref=dst,
        send_sem=send,
        recv_sem=recv,
        device_id=device,
        device_id_type=MESH,
    )


def partner(position, bit):
    return position + bit - 2 * bit * lax.rem(position // bit, 2)


def col_bits(col_count):
    bits, bit = [], 1
    while bit < col_count:
        bits.append(bit)
        bit *= 2
    return bits


def greet_row(row, row_count, barrier):
    for k in range(1, row_count):
        peer = lax.rem(row + k, row_count)
        pl.semaphore_signal(barrier, inc=1, device_id={"row": peer}, device_id_type=MESH)


def greet_cols(col, bits, barrier):
    for bit in bits:
        peer = partner(col, bit)
        pl.semaphore_signal(barrier, inc=1, device_id={"col": peer}, device_id_type=MESH)


class Line:
    def __init__(self, row_count, sources, outs, sems):
        self.depth = row_count // SIDES
        self.row = lax.axis_index("row")
        self.place = self.row // SIDES
        self.sources, self.outs = sources, outs
        self.up_s, self.up_r, self.dn_s, self.dn_r = sems
        self.has_up = self.place < self.depth - 1
        self.has_dn = self.place > 0

    @staticmethod
    def scratch(row_count, count):
        return [DMA((count, row_count // SIDES))] * 4

    def up(self, i, slot, d, first=False):
        src = self.sources[i] if first else self.outs[i].at[slot]
        device = {"row": self.row + SIDES}
        return remote(src, self.outs[i].at[slot], self.up_s.at[i, d], self.up_r.at[i, d], device)

    def dn(self, i, slot, d, first=False):
        src = self.sources[i] if first else self.outs[i].at[slot]
        device = {"row": self.row - SIDES}
        return remote(src, self.outs[i].at[slot], self.dn_s.at[i, d], self.dn_r.at[i, d], device)

    def has(self, way, d):
        there = self.place + d * (2 * way - 1)
        return (d >= 0) & (there >= 0) & (there < self.depth) & ((way == 0) | (d > 0))

    def start(self, i):
        @pl.when(self.has_up)
        def _():
            self.up(i, self.place, 0, True).start()

        @pl.when(self.has_dn)
        def _():
            self.dn(i, self.place, 0, True).start()

    def forward(self, d):
        for i in range(len(self.outs)):

            @pl.when(self.has(0, d))
            def _():
                self.up(i, self.place - d, d - 1).wait_recv()

                @pl.when(self.has_up)
                def _():
                    self.up(i, self.place - d, d).start()

            @pl.when(self.has(1, d))
            def _():
                self.dn(i, self.place + d, d - 1).wait_recv()

                @pl.when(self.has_dn)
                def _():
                    self.dn(i, self.place + d, d).start()

    def drain(self):
        def sent(d, carry):
            for i in range(len(self.outs)):

                @pl.when((self.place - d >= 0) & self.has_up)
                def _():
                    self.up(i, self.place - d, d).wait_send()

                @pl.when((self.place + d < self.depth) & self.has_dn)
                def _():
                    self.dn(i, self.place + d, d).wait_send()

            return carry

        lax.fori_loop(0, self.depth, sent, 0)


def project_kernel(row_count, bits, *refs):
    basis_a, basis_b, buffer_a, buffer_b, proj_a, proj_b, pair = refs[:7]
    mine, theirs, all_b, high, low, part_b, land_b = refs[7:14]
    refs = refs[14:]
    stages = len(bits) + 1
    sums, refs = list(refs[:stages]) + [proj_a], refs[stages:]
    landed, refs = refs[:stages], refs[stages:]
    sums_b, refs = refs[: len(bits)], refs[len(bits) :]
    landed_b, refs = refs[: len(bits) - 1], refs[len(bits) - 1 :]
    line_sems, refs = refs[:4], refs[4:]
    small_s, small_r, small_own, swap_s, swap_r, swap_own, sum_s, sum_r, b_s, b_r = refs
    row, col = lax.axis_index("row"), lax.axis_index("col")
    place, lane = row // SIDES, lax.rem(row, SIDES)
    other = place * SIDES + (1 - lane)
    share, width = basis_a.shape[0], mine.shape[2]
    depth = row_count // SIDES
    rank = share * row_count
    half = rank // 2
    twin, part = partner(col, 1), lax.rem(col, 2)
    devices = [{"col": partner(col, bit)} for bit in bits] + [{"row": other}]

    barrier = pltpu.get_barrier_semaphore()
    greet_row(row, row_count, barrier)
    greet_cols(col, bits, barrier)
    pl.semaphore_wait(barrier, row_count - 1 + len(bits))

    def columns(position):
        return pl.ds(pl.multiple_of(position * width, width), width)

    def small(k):
        peer = lax.rem(row + k, row_count)
        return remote(basis_b, all_b.at[row], small_s.at[k], small_r.at[k], {"row": peer})

    swap_basis = remote(
        basis_a.at[:, columns(1 - lane)], theirs.at[place], swap_s.at[0], swap_r.at[0], {"row": other}
    )
    swap_rows = remote(
        buffer_a.at[:, columns(1 - lane)], pair.at[lane], swap_s.at[1], swap_r.at[1], {"row": other}
    )
    own_basis = pltpu.make_async_copy(basis_a.at[:, columns(lane)], mine.at[place], swap_own.at[0])
    own_rows = pltpu.make_async_copy(buffer_a.at[:, columns(lane)], pair.at[lane], swap_own.at[1])
    small_local = pltpu.make_async_copy(basis_b, all_b.at[row], small_own)
    sources = [basis_a.at[:, columns(lane)], theirs.at[place]]
    line = Line(row_count, sources, [mine, theirs], line_sems)
    swap_basis.start()
    line.start(0)
    for k in range(1, row_count):
        small(k).start()
    swap_rows.start()
    own_basis.start()
    own_rows.start()
    small_local.start()

    def unit(place_):
        return pl.ds(pl.multiple_of(place_ * SIDES * share, SIDES * share), SIDES * share)

    def summing(stage, place_):
        sems = sum_s.at[stage, place_], sum_r.at[stage, place_]
        here, there = sums[stage].at[unit(place_), :], landed[stage].at[unit(place_), :]
        return remote(here, there, *sems, devices[stage])

    def compute(place_):
        blocks = jnp.concatenate([mine[place_], theirs[place_]], axis=0)
        block_high, block_low = halves(blocks)
        total = narrow_dot(block_high, low[...], LAST) + narrow_dot(block_low, high[...], LAST)
        total = total + narrow_dot(block_high, high[...], LAST)
        for k, side in enumerate((lane, 1 - lane)):
            start = (place_ * SIDES + side) * share
            sums[0][pl.ds(pl.multiple_of(start, share), share), :] = total[k * share : (k + 1) * share]
        summing(0, place_).start()

    def step(stage, place_):
        summing(stage, place_).wait_recv()
        sums[stage + 1][unit(place_), :] = sums[stage][unit(place_), :] + landed[stage][unit(place_), :]
        if stage + 1 < stages:
            summing(stage + 1, place_).start()

    def progress(d):
        for stage in range(stages):
            for way in range(2):

                @pl.when(line.has(way, d - 1 - stage))
                def _():
                    step(stage, place + (d - 1 - stage) * (2 * way - 1))

    def half_rows(position):
        return pl.ds(pl.multiple_of(position * half, half), half)

    def scatter_b():
        return remote(part_b.at[half_rows(1 - part), :], land_b, b_s.at[0], b_r.at[0], {"col": twin})

    def exchange_b(stage):
        device = {"col": partner(col, bits[stage])}
        return remote(sums_b[stage - 1], landed_b[stage - 1], b_s.at[stage], b_r.at[stage], device)

    def return_b(position):
        rows = half_rows(position)
        index = len(bits)
        return remote(sums_b[-1], proj_b.at[rows, :], b_s.at[index], b_r.at[index], {"col": twin})

    def begin_b():
        small_local.wait()
        for k in range(1, row_count):
            small(k).wait_recv()
        flat = all_b[...].reshape(rank, basis_b.shape[1])
        part_b[...] = split_dot(flat, buffer_b[...], LAST)
        scatter_b().start()

    def second_b():
        scatter_b().wait_recv()
        sums_b[0][...] = part_b[half_rows(part), :] + land_b[...]
        if len(bits) > 1:
            exchange_b(1).start()

    def finish_b():
        for stage in range(1, len(bits)):
            exchange_b(stage).wait_recv()
            sums_b[stage][...] = sums_b[stage - 1][...] + landed_b[stage - 1][...]
            if stage + 1 < len(bits):
                exchange_b(stage + 1).start()
        return_b(part).start()
        proj_b[half_rows(part), :] = sums_b[-1][...]

    swap_basis.wait_recv()
    line.start(1)

    def advance(d, carry):
        line.forward(d)

        @pl.when(d == 1)
        def _():
            begin_b()
            own_basis.wait()
            own_rows.wait()
            swap_rows.wait_recv()
            high[...], low[...] = halves(pair[...].reshape(high.shape))
            compute(place)

        for way in range(2):

            @pl.when(line.has(way, d))
            def _():
                compute(place + d * (2 * way - 1))

        @pl.when(d == min(2, depth - 1))
        def _():
            second_b()

        progress(d)
        return carry

    lax.fori_loop(1, depth, advance, 0)
    finish_b()
    for d in range(depth, depth + stages):
        progress(d)
    return_b(1 - part).wait_recv()
    swap_basis.wait_send()
    swap_rows.wait_send()
    for k in range(1, row_count):
        small(k).wait_send()
    line.drain()

    def sent(place_, carry):
        for stage in range(stages):
            summing(stage, place_).wait_send()
        return carry

    lax.fori_loop(0, depth, sent, 0)
    scatter_b().wait_send()
    for stage in range(1, len(bits)):
        exchange_b(stage).wait_send()
    return_b(part).wait_send()


def project(basis_a, basis_b, buffer_a, buffer_b):
    row_count, col_count = lax.axis_size("row"), lax.axis_size("col")
    bits = col_bits(col_count)
    stages = len(bits) + 1
    depth = row_count // SIDES
    (share, width), rows_a, rows_b = basis_a.shape, buffer_a.shape[0], buffer_b.shape[0]
    rank, width = share * row_count, width // SIDES

    def space(*shape):
        return pltpu.VMEM(shape, jnp.float32)

    narrow = pltpu.VMEM((SIDES * rows_a, width), jnp.bfloat16)
    return pl.pallas_call(
        functools.partial(project_kernel, row_count, bits),
        out_shape=[
            jax.ShapeDtypeStruct(shape, jnp.float32)
            for shape in ((rank, SIDES * rows_a), (rank, rows_b), (SIDES, rows_a, width))
        ],
        in_specs=[VMEM] * 4,
        out_specs=[VMEM] * 3,
        scratch_shapes=[
            space(depth, share, width),
            space(depth, share, width),
            space(row_count, *basis_b.shape),
            narrow,
            narrow,
            space(rank, rows_b),
            space(rank // 2, rows_b),
        ]
        + [space(rank, SIDES * rows_a)] * (2 * stages)
        + [space(rank // 2, rows_b)] * (2 * len(bits) - 1)
        + Line.scratch(row_count, 2)
        + [DMA((row_count,)), DMA((row_count,)), DMA(()), DMA((2,)), DMA((2,)), DMA((2,))]
        + [DMA((stages, depth))] * 2
        + [DMA((len(bits) + 1,))] * 2,
        name="project",
        compiler_params=pltpu.CompilerParams(
            collective_id=1, has_side_effects=True, vmem_limit_bytes=60 * 2**20
        ),
    )(basis_a, basis_b, buffer_a, buffer_b)


def factor(rank, grams, outs, works, diags, between):
    eye_rows = lax.broadcasted_iota(jnp.int32, (rank, rank), 0)
    eye_cols = lax.broadcasted_iota(jnp.int32, (rank, rank), 1)
    for gram, work in zip(grams, works):
        work[:, :rank] = gram[...]
        work[:, rank:] = (eye_rows == eye_cols).astype(jnp.float32)
    rows = lax.broadcasted_iota(jnp.int32, (BLOCK, 1), 0)
    lanes = lax.broadcasted_iota(jnp.int32, (1, BLOCK), 1)
    for k in range(rank // BLOCK):
        low, high = k * BLOCK, (k + 1) * BLOCK
        for work, diag in zip(works, diags):
            diag[:, :BLOCK] = work[low:high, low:high]
            diag[:, BLOCK:] = (rows == lanes).astype(jnp.float32)

        def step(j, carry):
            for diag in diags:
                here = lanes == j
                row = diag[pl.ds(j, 1), :]
                col = jnp.sum(jnp.where(here, diag[:, :BLOCK], 0.0), axis=1, keepdims=True)
                pivot = jnp.sum(jnp.where(here, row[:, :BLOCK], 0.0), axis=1, keepdims=True)
                factor = jnp.where(rows > j, col * (1.0 / pivot), 0.0)
                diag[...] = diag[...] - factor * row
            return carry

        for piece in range(PIECES):
            lax.fori_loop(piece * BLOCK // PIECES, (piece + 1) * BLOCK // PIECES, step, 0)
            if piece + 1 < PIECES:
                between()
        width = slice(low, rank + high)
        for work, diag in zip(works, diags):
            pivots = jnp.sum(
                jnp.where(rows == lanes, diag[:, :BLOCK], 0.0), axis=1, keepdims=True
            )
            inverse = diag[:, BLOCK:] * (1.0 / jnp.sqrt(pivots))
            panel = dot(inverse, work[low:high, width])
            work[low:high, width] = panel
            if high < rank:
                factors = panel[:, BLOCK : rank - low]
                work[high:, width] = work[high:, width] - dot(factors, panel, FIRST)
        between()
    for work, out in zip(works, outs):
        out[...] = work[:, rank:]


class Reduce:
    def __init__(self, row_count, sems):
        depth = row_count // SIDES
        row = lax.axis_index("row")
        place, lane = row // SIDES, lax.rem(row, SIDES)
        lower = place < depth // 2
        self.place, self.lane, self.depth = place, lane, depth
        self.other = place * SIDES + (1 - lane)
        toward = jnp.where(lower, SIDES, -SIDES)
        self.inner, self.outer = {"row": row + toward}, {"row": row - toward}
        self.steps = jnp.where(lower, depth // 2 - 1 - place, place - depth // 2)
        self.middle = self.steps == 0
        self.has_outer = self.steps < depth // 2 - 1
        self.sems = sems

    @staticmethod
    def scratch(count):
        return [DMA((count,))] * 6

    def inward(self, i, part, arrive):
        return remote(part, arrive, self.sems[0].at[i], self.sems[1].at[i], self.inner)

    def swap(self, i, part, meet):
        return remote(part, meet, self.sems[2].at[i], self.sems[3].at[i], self.inner)

    def outward(self, i, final):
        return remote(final, final, self.sems[4].at[i], self.sems[5].at[i], self.outer)

    def gather(self, i, part, arrive, meet):
        @pl.when(self.has_outer)
        def _():
            self.inward(i, part, arrive).wait_recv()
            part[...] = part[...] + arrive[...]

        @pl.when(self.middle)
        def _():
            self.swap(i, part, meet).start()

        @pl.when(self.steps > 0)
        def _():
            self.inward(i, part, arrive).start()

    def spread(self, i, part, meet, final):
        @pl.when(self.middle)
        def _():
            self.swap(i, part, meet).wait_recv()
            final[...] = part[...] + meet[...]

        @pl.when(self.steps > 0)
        def _():
            self.outward(i, final).wait_recv()

        @pl.when(self.has_outer)
        def _():
            self.outward(i, final).start()

    def drain(self, i, part, arrive, meet, final):
        @pl.when(self.middle)
        def _():
            self.swap(i, part, meet).wait_send()

        @pl.when(self.steps > 0)
        def _():
            self.inward(i, part, arrive).wait_send()

        @pl.when(self.has_outer)
        def _():
            self.outward(i, final).wait_send()


def products_kernel(row_count, col_count, rank, scales, *refs):
    proj_a, proj_b, pair, buffer_b = refs[:4]
    trans_a, trans_b, basis_a, basis_b, ortho_a, ortho_b, scaled_a, scaled_b = refs[4:12]
    part_w, arrive_w, meet_w, final_w, other_w = refs[12:17]
    part_v, arrive_v, meet_v, final_v, land_v, other_v, whole_v = refs[17:24]
    piece_a, piece_b = refs[24:28], refs[28:32]
    cast_b, land_b, gram_a, gram_b, inv_a, inv_b, high_a, low_a = refs[32:40]
    rows_a, wide_a, wide_b, full_a, full_b, square_a, square_b, mine, theirs = refs[40:49]
    works, diags = refs[49:51], refs[51:53]
    reduce_sems, refs = refs[53:59], refs[59:]
    side_s, side_r, give_s, give_r, gram_s, gram_r, sq_s, sq_r = refs
    row, col = lax.axis_index("row"), lax.axis_index("col")
    line = Reduce(row_count, reduce_sems)
    lane, place, other = line.lane, line.place, line.other
    share, half = rank // row_count, rank // 2
    peers = SIDES * col_count
    piece = rank // peers
    index = lane * col_count + col
    chunks = part_w.shape[0]
    width = part_w.shape[2]

    def peer_of(k):
        target = lax.rem(index + k, peers)
        return (place * SIDES + target // col_count, lax.rem(target, col_count))

    barrier = pltpu.get_barrier_semaphore()

    pl.semaphore_signal(barrier, inc=1, device_id=line.inner, device_id_type=MESH)
    for k in range(1, peers):
        pl.semaphore_signal(barrier, inc=1, device_id=peer_of(k), device_id_type=MESH)

    @pl.when(line.has_outer)
    def _():
        pl.semaphore_signal(barrier, inc=1, device_id=line.outer, device_id_type=MESH)
        pl.semaphore_wait(barrier, peers + 1)

    @pl.when(jnp.logical_not(line.has_outer))
    def _():
        pl.semaphore_wait(barrier, peers)

    def rows_of(position, size):
        return pl.ds(pl.multiple_of(position * size, size), size)

    def give_g():
        return remote(cast_b, land_b, give_s.at[0], give_r.at[0], {"row": other})

    def give_v():
        there = whole_v.at[rows_of(1 - lane, half), :]
        return remote(there, land_v, give_s.at[1], give_r.at[1], {"row": other})

    def grams(k, which):
        source = (piece_a, piece_b)[which][3]
        target = (gram_a, gram_b)[which].at[rows_of(index, piece), :]
        return remote(source, target, gram_s.at[which, k], gram_r.at[which, k], peer_of(k))

    def aside(i, final, target):
        return remote(final, target, side_s.at[i], side_r.at[i], {"row": other})

    unit_v = (part_v, arrive_v, meet_v, final_v)

    def unit_w(k):
        return part_w.at[k], arrive_w.at[k], meet_w.at[k], final_w.at[k]

    def gather(i, unit):
        line.gather(i, unit[0], unit[1], unit[2])

    def spread(i, unit):
        line.spread(i, unit[0], unit[2], unit[3])

    theirs_index = (1 - lane) * col_count + col
    cast_b[...] = dot(proj_b[rows_of(theirs_index, piece), :], proj_b[...], LAST)
    give_g().start()
    piece_a[0][...] = dot(proj_a[rows_of(index, piece), :], proj_a[...], LAST)
    gather(0, piece_a)
    piece_b[0][...] = dot(proj_b[rows_of(index, piece), :], proj_b[...], LAST)
    give_g().wait_recv()
    piece_b[0][...] = piece_b[0][...] + land_b[...]
    gather(1, piece_b)
    rows_high, rows_low = halves(proj_a[...])

    def multiply(k):
        columns = slice(k * width, (k + 1) * width)
        block = pair[:, :, columns].reshape(proj_a.shape[1], width)
        block_high, block_low = halves(block)
        total = narrow_dot(rows_high, block_low) + narrow_dot(rows_low, block_high)
        part_w[k] = total + narrow_dot(rows_high, block_high)

    def take(k):
        gather(3 + k, unit_w(k))

    def hand(k):
        spread(3 + k, unit_w(k))
        aside(1 + k, final_w.at[k], other_w.at[k]).start()

    def take_v():
        give_v().wait_recv()
        part_v[...] = whole_v[rows_of(lane, half), :] + land_v[...]
        gather(2, unit_v)

    def hand_v():
        spread(2, unit_v)
        aside(0, final_v, other_v).start()

    multiply(0)
    for which, unit in enumerate((piece_a, piece_b)):
        spread(which, unit)
        for k in range(1, peers):
            grams(k, which).start()
    gram_a[rows_of(index, piece), :] = piece_a[3][...]
    gram_b[rows_of(index, piece), :] = piece_b[3][...]
    take(0)
    whole_v[...] = split_dot(proj_b[...], buffer_b[...])
    give_v().start()
    for k in range(1, chunks):
        multiply(k)

        @pl.when(jnp.logical_not(line.has_outer))
        def _():
            take(k)

    for which in range(2):
        for k in range(1, peers):
            grams(k, which).wait_recv()

    def later_take(k):
        @pl.when(line.has_outer)
        def _():
            take(k)

    tasks = [functools.partial(hand, 0), take_v]
    for k in range(1, chunks):
        tasks.append(functools.partial(later_take, k))
        if k == 2 or (chunks <= 2 and k == chunks - 1):
            tasks.append(hand_v)
        tasks.append(functools.partial(hand, k))
    if chunks == 1:
        tasks.append(hand_v)
    slots = rank // BLOCK * PIECES
    done = [0, 0]

    def between():
        done[0] += 1
        goal = -(-len(tasks) * done[0] // slots)
        while done[1] < min(goal, len(tasks)):
            tasks[done[1]]()
            done[1] += 1

    factor(rank, [gram_a, gram_b], [inv_a, inv_b], works, diags, between)
    high_a[...], low_a[...] = halves(inv_a[...])
    rows_a[...] = proj_a[...].T
    count_a = rows_a.shape[0] // SIDES
    wide_a[...] = split_dot(rows_a[rows_of(lane, count_a), :], inv_a[...], LAST)
    wide_b[...] = split_dot(proj_b[...].T, inv_b[...], LAST)
    ortho_a[...] = wide_a[...].astype(jnp.bfloat16)
    ortho_b[...] = wide_b[...].astype(jnp.bfloat16)
    square_a[...] = jnp.zeros_like(square_a)
    own = rows_of(row, share)

    def use(product, position):
        product_high, product_low = halves(product)
        total = narrow_dot(high_a[...], product_low) + narrow_dot(low_a[...], product_high)
        total = total + narrow_dot(high_a[...], product_high)
        full_a[...] = total
        trans_a[position] = total.astype(jnp.bfloat16)
        square_a[...] += jnp.sum(total * total, axis=1, keepdims=True)
        basis_a[position] = full_a[own, :]

    def near(k, carry):
        use(final_w[k], lane * chunks + k)
        return carry

    def far(k, carry):
        aside(1 + k, final_w.at[k], other_w.at[k]).wait_recv()
        use(other_w[k], (1 - lane) * chunks + k)
        return carry

    lax.fori_loop(0, chunks, near, 0)
    aside(0, final_v, other_v).wait_recv()
    whole_v[rows_of(lane, half), :] = final_v[...]
    give_v().wait_send()
    whole_v[rows_of(1 - lane, half), :] = other_v[...]
    total_b = split_dot(inv_b[...], whole_v[...])
    full_b[...] = total_b
    trans_b[...] = total_b.astype(jnp.bfloat16)
    square_b[...] = jnp.sum(total_b * total_b, axis=1, keepdims=True)
    lax.fori_loop(0, chunks, far, 0)

    def across(column):
        return jnp.broadcast_to(column, (rank, BLOCK)).T[:8]

    def norms(k):
        peer = lax.rem(col + k, col_count)
        return remote(mine, theirs.at[col], sq_s.at[k], sq_r.at[k], {"col": peer})

    mine[0] = across(square_a[...])
    mine[1] = across(square_b[...])
    for k in range(1, col_count):
        norms(k).start()
    theirs[col] = mine[...]
    for k in range(1, col_count):
        norms(k).wait_recv()
    norm = jnp.sqrt(jnp.sum(theirs[...], axis=0) + EPS)
    norm_a, norm_b = norm[0, :1], norm[1, :1]
    scaled_a[...] = (wide_a[...] * (scales[0] / norm_a)).astype(jnp.bfloat16)
    scaled_b[...] = (wide_b[...] * (scales[1] / norm_b)).astype(jnp.bfloat16)
    ranks = lax.broadcasted_iota(jnp.int32, (share, rank), 1)
    owned = lax.broadcasted_iota(jnp.int32, (share, rank), 0) + row * share
    own_a = jnp.sum(jnp.where(ranks == owned, norm_a, 0.0), axis=1, keepdims=True)
    own_b = jnp.sum(jnp.where(ranks == owned, norm_b, 0.0), axis=1, keepdims=True)
    for k in range(basis_a.shape[0]):
        basis_a[k] = basis_a[k] / own_a
    basis_b[...] = full_b[own, :] / own_b
    for k in range(1, col_count):
        norms(k).wait_send()
    for which in range(2):
        for k in range(1, peers):
            grams(k, which).wait_send()
    give_g().wait_send()
    aside(0, final_v, other_v).wait_send()
    for i, unit in enumerate((piece_a, piece_b, unit_v)):
        line.drain(i, *unit)

    def sent(k, carry):
        aside(1 + k, final_w.at[k], other_w.at[k]).wait_send()
        line.drain(3 + k, *unit_w(k))
        return carry

    lax.fori_loop(0, chunks, sent, 0)


def products(proj_a, proj_b, pair, buffer_b, scales):
    row_count, col_count = lax.axis_size("row"), lax.axis_size("col")
    rank = proj_a.shape[0]
    share, half, piece = rank // row_count, rank // 2, rank // (SIDES * col_count)
    side_width = pair.shape[2]
    chunk = CHUNK if side_width % CHUNK == 0 else side_width
    chunks = side_width // chunk
    width_b = buffer_b.shape[1]
    rows_a, rows_b = pair.shape[1], buffer_b.shape[0]

    def array(kind, *shape):
        return jax.ShapeDtypeStruct(shape, kind)

    def space(*shape):
        return pltpu.VMEM(shape, jnp.float32)

    narrow, wide = jnp.bfloat16, jnp.float32
    peers, cols = DMA((2, SIDES * col_count)), DMA((col_count,))
    return pl.pallas_call(
        functools.partial(products_kernel, row_count, col_count, rank, scales),
        out_shape=[
            array(narrow, SIDES * chunks, rank, chunk),
            array(narrow, rank, width_b),
            array(wide, SIDES * chunks, share, chunk),
            array(wide, share, width_b),
            array(narrow, rows_a, rank),
            array(narrow, rows_b, rank),
            array(narrow, rows_a, rank),
            array(narrow, rows_b, rank),
        ],
        in_specs=[VMEM] * 4,
        out_specs=[VMEM] * 8,
        scratch_shapes=[space(chunks, rank, chunk)] * 5
        + [space(half, width_b)] * 6
        + [space(rank, width_b)]
        + [space(piece, rank)] * 10
        + [space(rank, rank)] * 4
        + [pltpu.VMEM((rank, rank), narrow)] * 2
        + [
            space(SIDES * rows_a, rank),
            space(rows_a, rank),
            space(rows_b, rank),
            space(rank, chunk),
            space(rank, width_b),
            space(rank, 1),
            space(rank, 1),
            space(2, 8, rank),
            space(col_count, 2, 8, rank),
        ]
        + [space(rank, 2 * rank)] * 2
        + [space(BLOCK, 2 * BLOCK)] * 2
        + Reduce.scratch(3 + chunks)
        + [DMA((1 + chunks,))] * 2
        + [DMA((2,))] * 2
        + [peers, peers, cols, cols],
        name="products",
        compiler_params=pltpu.CompilerParams(
            collective_id=2, has_side_effects=True, vmem_limit_bytes=62 * 2**20
        ),
    )(proj_a, proj_b, pair, buffer_b)


def ending_kernel(slabs, *refs):
    buffer_a, trans_a, basis_a, ortho_a, scaled_a = refs[:5]
    buffer_b, trans_b, ortho_b, scaled_b = refs[5:9]
    mom_a, update_a, new_a, mom_b, update_b = refs[9:]
    mom_a[...] = buffer_a[...] - (1.0 - MU) * narrow_dot(ortho_a[...], trans_a[0])
    update_a[...] = narrow_dot(scaled_a[...], trans_a[0]).astype(jnp.bfloat16)
    new_a[...] = basis_a[0]

    @pl.when(pl.program_id(0) < slabs)
    def _():
        mom_b[...] = buffer_b[...] - (1.0 - MU) * narrow_dot(ortho_b[...], trans_b[...])
        update_b[...] = narrow_dot(scaled_b[...], trans_b[...]).astype(jnp.bfloat16)


def ending(buffer_a, trans_a, basis_a, ortho_a, scaled_a, buffer_b, trans_b, ortho_b, scaled_b):
    steps, rank, width = trans_a.shape
    rows_a, rows_b, share = buffer_a.shape[0], buffer_b.shape[0], basis_a.shape[1]
    slabs = 8
    if width % 128 or rows_b % (16 * slabs) or steps < slabs:
        flat = trans_a.swapaxes(0, 1).reshape(rank, -1)
        return (
            buffer_a - (1.0 - MU) * narrow_dot(ortho_a, flat),
            narrow_dot(scaled_a, flat).astype(jnp.bfloat16),
            basis_a.swapaxes(0, 1).reshape(share, -1),
            buffer_b - (1.0 - MU) * narrow_dot(ortho_b, trans_b),
            narrow_dot(scaled_b, trans_b).astype(jnp.bfloat16),
        )
    some = rows_b // slabs
    cut = pl.BlockSpec((rows_a, width), lambda j: (0, j))
    stack = pl.BlockSpec((1, rank, width), lambda j: (j, 0, 0))
    thin = pl.BlockSpec((1, share, width), lambda j: (j, 0, 0))
    fixed_a = pl.BlockSpec((rows_a, rank), lambda j: (0, 0))
    fixed_b = pl.BlockSpec(trans_b.shape, lambda j: (0, 0))
    slab = pl.BlockSpec((some, buffer_b.shape[1]), lambda j: (jnp.minimum(j, slabs - 1), 0))
    rows = pl.BlockSpec((some, rank), lambda j: (jnp.minimum(j, slabs - 1), 0))
    return pl.pallas_call(
        functools.partial(ending_kernel, slabs),
        grid=(steps,),
        out_shape=[
            jax.ShapeDtypeStruct(buffer_a.shape, jnp.float32),
            jax.ShapeDtypeStruct(buffer_a.shape, jnp.bfloat16),
            jax.ShapeDtypeStruct((share, buffer_a.shape[1]), jnp.float32),
            jax.ShapeDtypeStruct(buffer_b.shape, jnp.float32),
            jax.ShapeDtypeStruct(buffer_b.shape, jnp.bfloat16),
        ],
        in_specs=[cut, stack, thin, fixed_a, fixed_a, slab, fixed_b, rows, rows],
        out_specs=[cut, cut, pl.BlockSpec((share, width), lambda j: (0, j)), slab, slab],
        name="ending",
    )(buffer_a, trans_a, basis_a, ortho_a, scaled_a, buffer_b, trans_b, ortho_b, scaled_b)


def shards(mom_a, grad_a, basis_a, mom_b, grad_b, basis_b):
    row_count = lax.axis_size("row")
    buffer_a, buffer_b = MU * mom_a + grad_a, MU * mom_b + grad_b
    proj_a, proj_b, pair = project(basis_a, basis_b, buffer_a, buffer_b)
    rank = proj_a.shape[0]
    scales = [
        math.sqrt(x.shape[0] * x.shape[1] * row_count * lax.axis_size("col") / rank)
        for x in (buffer_a, buffer_b)
    ]
    trans_a, trans_b, basis_a, basis_b, ortho_a, ortho_b, scaled_a, scaled_b = products(
        proj_a, proj_b, pair, buffer_b, scales
    )
    new_mom_a, update_a, new_basis_a, new_mom_b, update_b = ending(
        buffer_a, trans_a, basis_a, ortho_a, scaled_a, buffer_b, trans_b, ortho_b, scaled_b
    )
    return new_mom_a, update_a, new_basis_a, new_mom_b, update_b, basis_b


def solution(mesh):
    spec = P("row", "col")
    return jax.shard_map(
        shards, mesh=mesh, in_specs=(spec,) * 6, out_specs=(spec,) * 6, check_vma=False
    )
```

```python
import functools
import math

import jax
import jax.numpy as jnp
from jax import lax
from jax.experimental import pallas as pl
from jax.experimental.pallas import tpu as pltpu
from jax.sharding import PartitionSpec as P

MU = 0.95
EPS = 1e-06
BLOCK = 128
HIGHEST = lax.Precision.HIGHEST
MESH = pl.DeviceIdType.MESH
VMEM = pl.BlockSpec(memory_space=pltpu.VMEM)
DMA = pltpu.SemaphoreType.DMA
LAST = ((1,), (1,))
FIRST = ((0,), (0,))
PLAIN = ((1,), (0,))
SIDES = 2
PIECES = 2
CHUNK = 128


def dot(x, y, contract=PLAIN, precision=HIGHEST):
    return lax.dot_general(
        x, y, (contract, ((), ())), precision=precision, preferred_element_type=jnp.float32
    )


def halves(x):
    high = x.astype(jnp.bfloat16)
    return high, (x - high.astype(jnp.float32)).astype(jnp.bfloat16)


def narrow_dot(x, y, contract=PLAIN):
    return lax.dot_general(x, y, (contract, ((), ())), preferred_element_type=jnp.float32)


def split_dot(x, y, contract=PLAIN):
    (x_high, x_low), (y_high, y_low) = halves(x), halves(y)
    total = narrow_dot(x_high, y_low, contract) + narrow_dot(x_low, y_high, contract)
    return total + narrow_dot(x_high, y_high, contract)


def remote(src, dst, send, recv, device):
    return pltpu.make_async_remote_copy(
        src_ref=src,
        dst_ref=dst,
        send_sem=send,
        recv_sem=recv,
        device_id=device,
        device_id_type=MESH,
    )


def partner(position, bit):
    return position + bit - 2 * bit * lax.rem(position // bit, 2)


def col_bits(col_count):
    bits, bit = [], 1
    while bit < col_count:
        bits.append(bit)
        bit *= 2
    return bits


def greet_row(row, row_count, barrier):
    for k in range(1, row_count):
        peer = lax.rem(row + k, row_count)
        pl.semaphore_signal(barrier, inc=1, device_id={"row": peer}, device_id_type=MESH)


def greet_cols(col, bits, barrier):
    for bit in bits:
        peer = partner(col, bit)
        pl.semaphore_signal(barrier, inc=1, device_id={"col": peer}, device_id_type=MESH)


class Line:
    def __init__(self, row_count, sources, outs, sems):
        self.depth = row_count // SIDES
        self.row = lax.axis_index("row")
        self.place = self.row // SIDES
        self.sources, self.outs = sources, outs
        self.up_s, self.up_r, self.dn_s, self.dn_r = sems
        self.has_up = self.place < self.depth - 1
        self.has_dn = self.place > 0

    @staticmethod
    def scratch(row_count, count):
        return [DMA((count, row_count // SIDES))] * 4

    def up(self, i, slot, d, first=False):
        src = self.sources[i] if first else self.outs[i].at[slot]
        device = {"row": self.row + SIDES}
        return remote(src, self.outs[i].at[slot], self.up_s.at[i, d], self.up_r.at[i, d], device)

    def dn(self, i, slot, d, first=False):
        src = self.sources[i] if first else self.outs[i].at[slot]
        device = {"row": self.row - SIDES}
        return remote(src, self.outs[i].at[slot], self.dn_s.at[i, d], self.dn_r.at[i, d], device)

    def has(self, way, d):
        there = self.place + d * (2 * way - 1)
        return (d >= 0) & (there >= 0) & (there < self.depth) & ((way == 0) | (d > 0))

    def start(self, i):
        @pl.when(self.has_up)
        def _():
            self.up(i, self.place, 0, True).start()

        @pl.when(self.has_dn)
        def _():
            self.dn(i, self.place, 0, True).start()

    def forward(self, d):
        for i in range(len(self.outs)):

            @pl.when(self.has(0, d))
            def _():
                self.up(i, self.place - d, d - 1).wait_recv()

                @pl.when(self.has_up)
                def _():
                    self.up(i, self.place - d, d).start()

            @pl.when(self.has(1, d))
            def _():
                self.dn(i, self.place + d, d - 1).wait_recv()

                @pl.when(self.has_dn)
                def _():
                    self.dn(i, self.place + d, d).start()

    def drain(self):
        def sent(d, carry):
            for i in range(len(self.outs)):

                @pl.when((self.place - d >= 0) & self.has_up)
                def _():
                    self.up(i, self.place - d, d).wait_send()

                @pl.when((self.place + d < self.depth) & self.has_dn)
                def _():
                    self.dn(i, self.place + d, d).wait_send()

            return carry

        lax.fori_loop(0, self.depth, sent, 0)


def project_kernel(row_count, bits, *refs):
    basis_a, basis_b, buffer_a, buffer_b, proj_a, proj_b, pair = refs[:7]
    mine, theirs, all_b, high, low, part_b, land_b = refs[7:14]
    refs = refs[14:]
    stages = len(bits) + 1
    sums, refs = list(refs[:stages]) + [proj_a], refs[stages:]
    landed, refs = refs[:stages], refs[stages:]
    sums_b, refs = refs[: len(bits)], refs[len(bits) :]
    landed_b, refs = refs[: len(bits) - 1], refs[len(bits) - 1 :]
    line_sems, refs = refs[:4], refs[4:]
    small_s, small_r, small_own, swap_s, swap_r, swap_own, sum_s, sum_r, b_s, b_r = refs
    row, col = lax.axis_index("row"), lax.axis_index("col")
    place, lane = row // SIDES, lax.rem(row, SIDES)
    other = place * SIDES + (1 - lane)
    share, width = basis_a.shape[0], mine.shape[2]
    depth = row_count // SIDES
    rank = share * row_count
    half = rank // 2
    twin, part = partner(col, 1), lax.rem(col, 2)
    devices = [{"col": partner(col, bit)} for bit in bits] + [{"row": other}]

    barrier = pltpu.get_barrier_semaphore()
    greet_row(row, row_count, barrier)
    greet_cols(col, bits, barrier)
    pl.semaphore_wait(barrier, row_count - 1 + len(bits))

    def columns(position):
        return pl.ds(pl.multiple_of(position * width, width), width)

    def small(k):
        peer = lax.rem(row + k, row_count)
        return remote(basis_b, all_b.at[row], small_s.at[k], small_r.at[k], {"row": peer})

    swap_basis = remote(
        basis_a.at[:, columns(1 - lane)], theirs.at[place], swap_s.at[0], swap_r.at[0], {"row": other}
    )
    swap_rows = remote(
        buffer_a.at[:, columns(1 - lane)], pair.at[lane], swap_s.at[1], swap_r.at[1], {"row": other}
    )
    own_basis = pltpu.make_async_copy(basis_a.at[:, columns(lane)], mine.at[place], swap_own.at[0])
    own_rows = pltpu.make_async_copy(buffer_a.at[:, columns(lane)], pair.at[lane], swap_own.at[1])
    small_local = pltpu.make_async_copy(basis_b, all_b.at[row], small_own)
    sources = [basis_a.at[:, columns(lane)], theirs.at[place]]
    line = Line(row_count, sources, [mine, theirs], line_sems)
    swap_basis.start()
    line.start(0)
    for k in range(1, row_count):
        small(k).start()
    swap_rows.start()
    own_basis.start()
    own_rows.start()
    small_local.start()

    def unit(place_):
        return pl.ds(pl.multiple_of(place_ * SIDES * share, SIDES * share), SIDES * share)

    def summing(stage, place_):
        sems = sum_s.at[stage, place_], sum_r.at[stage, place_]
        here, there = sums[stage].at[unit(place_), :], landed[stage].at[unit(place_), :]
        return remote(here, there, *sems, devices[stage])

    def compute(place_):
        blocks = jnp.concatenate([mine[place_], theirs[place_]], axis=0)
        block_high, block_low = halves(blocks)
        total = narrow_dot(block_high, low[...], LAST) + narrow_dot(block_low, high[...], LAST)
        total = total + narrow_dot(block_high, high[...], LAST)
        for k, side in enumerate((lane, 1 - lane)):
            start = (place_ * SIDES + side) * share
            sums[0][pl.ds(pl.multiple_of(start, share), share), :] = total[k * share : (k + 1) * share]
        summing(0, place_).start()

    def step(stage, place_):
        summing(stage, place_).wait_recv()
        sums[stage + 1][unit(place_), :] = sums[stage][unit(place_), :] + landed[stage][unit(place_), :]
        if stage + 1 < stages:
            summing(stage + 1, place_).start()

    def progress(d):
        for stage in range(stages):
            for way in range(2):

                @pl.when(line.has(way, d - 1 - stage))
                def _():
                    step(stage, place + (d - 1 - stage) * (2 * way - 1))

    def half_rows(position):
        return pl.ds(pl.multiple_of(position * half, half), half)

    def scatter_b():
        return remote(part_b.at[half_rows(1 - part), :], land_b, b_s.at[0], b_r.at[0], {"col": twin})

    def exchange_b(stage):
        device = {"col": partner(col, bits[stage])}
        return remote(sums_b[stage - 1], landed_b[stage - 1], b_s.at[stage], b_r.at[stage], device)

    def return_b(position):
        rows = half_rows(position)
        index = len(bits)
        return remote(sums_b[-1], proj_b.at[rows, :], b_s.at[index], b_r.at[index], {"col": twin})

    def begin_b():
        small_local.wait()
        for k in range(1, row_count):
            small(k).wait_recv()
        flat = all_b[...].reshape(rank, basis_b.shape[1])
        part_b[...] = split_dot(flat, buffer_b[...], LAST)
        scatter_b().start()

    def second_b():
        scatter_b().wait_recv()
        sums_b[0][...] = part_b[half_rows(part), :] + land_b[...]
        if len(bits) > 1:
            exchange_b(1).start()

    def finish_b():
        for stage in range(1, len(bits)):
            exchange_b(stage).wait_recv()
            sums_b[stage][...] = sums_b[stage - 1][...] + landed_b[stage - 1][...]
            if stage + 1 < len(bits):
                exchange_b(stage + 1).start()
        return_b(part).start()
        proj_b[half_rows(part), :] = sums_b[-1][...]

    swap_basis.wait_recv()
    line.start(1)

    def advance(d, carry):
        line.forward(d)

        @pl.when(d == 1)
        def _():
            begin_b()
            own_basis.wait()
            own_rows.wait()
            swap_rows.wait_recv()
            high[...], low[...] = halves(pair[...].reshape(high.shape))
            compute(place)

        for way in range(2):

            @pl.when(line.has(way, d))
            def _():
                compute(place + d * (2 * way - 1))

        @pl.when(d == min(2, depth - 1))
        def _():
            second_b()

        progress(d)
        return carry

    lax.fori_loop(1, depth, advance, 0)
    finish_b()
    for d in range(depth, depth + stages):
        progress(d)
    return_b(1 - part).wait_recv()
    swap_basis.wait_send()
    swap_rows.wait_send()
    for k in range(1, row_count):
        small(k).wait_send()
    line.drain()

    def sent(place_, carry):
        for stage in range(stages):
            summing(stage, place_).wait_send()
        return carry

    lax.fori_loop(0, depth, sent, 0)
    scatter_b().wait_send()
    for stage in range(1, len(bits)):
        exchange_b(stage).wait_send()
    return_b(part).wait_send()


def project(basis_a, basis_b, buffer_a, buffer_b):
    row_count, col_count = lax.axis_size("row"), lax.axis_size("col")
    bits = col_bits(col_count)
    stages = len(bits) + 1
    depth = row_count // SIDES
    (share, width), rows_a, rows_b = basis_a.shape, buffer_a.shape[0], buffer_b.shape[0]
    rank, width = share * row_count, width // SIDES

    def space(*shape):
        return pltpu.VMEM(shape, jnp.float32)

    narrow = pltpu.VMEM((SIDES * rows_a, width), jnp.bfloat16)
    return pl.pallas_call(
        functools.partial(project_kernel, row_count, bits),
        out_shape=[
            jax.ShapeDtypeStruct(shape, jnp.float32)
            for shape in ((rank, SIDES * rows_a), (rank, rows_b), (SIDES, rows_a, width))
        ],
        in_specs=[VMEM] * 4,
        out_specs=[VMEM] * 3,
        scratch_shapes=[
            space(depth, share, width),
            space(depth, share, width),
            space(row_count, *basis_b.shape),
            narrow,
            narrow,
            space(rank, rows_b),
            space(rank // 2, rows_b),
        ]
        + [space(rank, SIDES * rows_a)] * (2 * stages)
        + [space(rank // 2, rows_b)] * (2 * len(bits) - 1)
        + Line.scratch(row_count, 2)
        + [DMA((row_count,)), DMA((row_count,)), DMA(()), DMA((2,)), DMA((2,)), DMA((2,))]
        + [DMA((stages, depth))] * 2
        + [DMA((len(bits) + 1,))] * 2,
        name="project",
        compiler_params=pltpu.CompilerParams(
            collective_id=1, has_side_effects=True, vmem_limit_bytes=60 * 2**20
        ),
    )(basis_a, basis_b, buffer_a, buffer_b)


def factor(rank, grams, outs, works, diags, between):
    eye_rows = lax.broadcasted_iota(jnp.int32, (rank, rank), 0)
    eye_cols = lax.broadcasted_iota(jnp.int32, (rank, rank), 1)
    for gram, work in zip(grams, works):
        work[:, :rank] = gram[...]
        work[:, rank:] = (eye_rows == eye_cols).astype(jnp.float32)
    rows = lax.broadcasted_iota(jnp.int32, (BLOCK, 1), 0)
    lanes = lax.broadcasted_iota(jnp.int32, (1, BLOCK), 1)
    for k in range(rank // BLOCK):
        low, high = k * BLOCK, (k + 1) * BLOCK
        for work, diag in zip(works, diags):
            diag[:, :BLOCK] = work[low:high, low:high]
            diag[:, BLOCK:] = (rows == lanes).astype(jnp.float32)

        def step(j, carry):
            for diag in diags:
                here = lanes == j
                row = diag[pl.ds(j, 1), :]
                col = jnp.sum(jnp.where(here, diag[:, :BLOCK], 0.0), axis=1, keepdims=True)
                pivot = jnp.sum(jnp.where(here, row[:, :BLOCK], 0.0), axis=1, keepdims=True)
                factor = jnp.where(rows > j, col * (1.0 / pivot), 0.0)
                diag[...] = diag[...] - factor * row
            return carry

        for piece in range(PIECES):
            lax.fori_loop(piece * BLOCK // PIECES, (piece + 1) * BLOCK // PIECES, step, 0)
            if piece + 1 < PIECES:
                between()
        width = slice(low, rank + high)
        for work, diag in zip(works, diags):
            pivots = jnp.sum(
                jnp.where(rows == lanes, diag[:, :BLOCK], 0.0), axis=1, keepdims=True
            )
            inverse = diag[:, BLOCK:] * (1.0 / jnp.sqrt(pivots))
            panel = dot(inverse, work[low:high, width])
            work[low:high, width] = panel
            if high < rank:
                factors = panel[:, BLOCK : rank - low]
                work[high:, width] = work[high:, width] - dot(factors, panel, FIRST)
        between()
    for work, out in zip(works, outs):
        out[...] = work[:, rank:]


class Reduce:
    def __init__(self, row_count, sems):
        depth = row_count // SIDES
        row = lax.axis_index("row")
        place, lane = row // SIDES, lax.rem(row, SIDES)
        lower = place < depth // 2
        self.place, self.lane, self.depth = place, lane, depth
        self.other = place * SIDES + (1 - lane)
        toward = jnp.where(lower, SIDES, -SIDES)
        self.inner, self.outer = {"row": row + toward}, {"row": row - toward}
        self.steps = jnp.where(lower, depth // 2 - 1 - place, place - depth // 2)
        self.middle = self.steps == 0
        self.has_outer = self.steps < depth // 2 - 1
        self.sems = sems

    @staticmethod
    def scratch(count):
        return [DMA((count,))] * 6

    def inward(self, i, part, arrive):
        return remote(part, arrive, self.sems[0].at[i], self.sems[1].at[i], self.inner)

    def swap(self, i, part, meet):
        return remote(part, meet, self.sems[2].at[i], self.sems[3].at[i], self.inner)

    def outward(self, i, final):
        return remote(final, final, self.sems[4].at[i], self.sems[5].at[i], self.outer)

    def gather(self, i, part, arrive, meet):
        @pl.when(self.has_outer)
        def _():
            self.inward(i, part, arrive).wait_recv()
            part[...] = part[...] + arrive[...]

        @pl.when(self.middle)
        def _():
            self.swap(i, part, meet).start()

        @pl.when(self.steps > 0)
        def _():
            self.inward(i, part, arrive).start()

    def spread(self, i, part, meet, final):
        @pl.when(self.middle)
        def _():
            self.swap(i, part, meet).wait_recv()
            final[...] = part[...] + meet[...]

        @pl.when(self.steps > 0)
        def _():
            self.outward(i, final).wait_recv()

        @pl.when(self.has_outer)
        def _():
            self.outward(i, final).start()

    def drain(self, i, part, arrive, meet, final):
        @pl.when(self.middle)
        def _():
            self.swap(i, part, meet).wait_send()

        @pl.when(self.steps > 0)
        def _():
            self.inward(i, part, arrive).wait_send()

        @pl.when(self.has_outer)
        def _():
            self.outward(i, final).wait_send()


def products_kernel(row_count, col_count, rank, joined, scales, *refs):
    proj_a, proj_b, pair, buffer_b = refs[:4]
    trans_a, trans_b, basis_a, basis_b, ortho_a, ortho_b, scaled_a, scaled_b = refs[4:12]
    part_w, arrive_w, meet_w, final_w, other_w = refs[12:17]
    part_v, arrive_v, meet_v, final_v, land_v, other_v, whole_v = refs[17:24]
    piece_a, piece_b = refs[24:28], refs[28:32]
    cast_b, land_b, gram_a, gram_b, inv_a, inv_b, high_a, low_a = refs[32:40]
    rows_a, wide_a, wide_b, full_a, full_b, square_a, square_b, mine, theirs = refs[40:49]
    works, diags = refs[49:51], refs[51:53]
    reduce_sems, refs = refs[53:59], refs[59:]
    side_s, side_r, give_s, give_r, gram_s, gram_r, sq_s, sq_r = refs
    row, col = lax.axis_index("row"), lax.axis_index("col")
    line = Reduce(row_count, reduce_sems)
    lane, place, other = line.lane, line.place, line.other
    share, half = rank // row_count, rank // 2
    peers = SIDES * col_count
    piece = rank // peers
    index = lane * col_count + col
    chunks = part_w.shape[0]
    width = part_w.shape[2]

    def peer_of(k):
        target = lax.rem(index + k, peers)
        return (place * SIDES + target // col_count, lax.rem(target, col_count))

    barrier = pltpu.get_barrier_semaphore()

    pl.semaphore_signal(barrier, inc=1, device_id=line.inner, device_id_type=MESH)
    for k in range(1, peers):
        pl.semaphore_signal(barrier, inc=1, device_id=peer_of(k), device_id_type=MESH)

    @pl.when(line.has_outer)
    def _():
        pl.semaphore_signal(barrier, inc=1, device_id=line.outer, device_id_type=MESH)
        pl.semaphore_wait(barrier, peers + 1)

    @pl.when(jnp.logical_not(line.has_outer))
    def _():
        pl.semaphore_wait(barrier, peers)

    def rows_of(position, size):
        return pl.ds(pl.multiple_of(position * size, size), size)

    def give_g():
        return remote(cast_b, land_b, give_s.at[0], give_r.at[0], {"row": other})

    def give_v():
        there = whole_v.at[rows_of(1 - lane, half), :]
        return remote(there, land_v, give_s.at[1], give_r.at[1], {"row": other})

    def grams(k, which):
        source = (piece_a, piece_b)[which][3]
        target = (gram_a, gram_b)[which].at[rows_of(index, piece), :]
        return remote(source, target, gram_s.at[which, k], gram_r.at[which, k], peer_of(k))

    def aside(i, final, target):
        return remote(final, target, side_s.at[i], side_r.at[i], {"row": other})

    unit_v = (part_v, arrive_v, meet_v, final_v)

    def unit_w(k):
        return part_w.at[k], arrive_w.at[k], meet_w.at[k], final_w.at[k]

    def gather(i, unit):
        line.gather(i, unit[0], unit[1], unit[2])

    def spread(i, unit):
        line.spread(i, unit[0], unit[2], unit[3])

    theirs_index = (1 - lane) * col_count + col
    cast_b[...] = dot(proj_b[rows_of(theirs_index, piece), :], proj_b[...], LAST)
    give_g().start()
    piece_a[0][...] = dot(proj_a[rows_of(index, piece), :], proj_a[...], LAST)
    gather(0, piece_a)
    piece_b[0][...] = dot(proj_b[rows_of(index, piece), :], proj_b[...], LAST)
    give_g().wait_recv()
    piece_b[0][...] = piece_b[0][...] + land_b[...]
    gather(1, piece_b)
    rows_high, rows_low = halves(proj_a[...])

    def multiply(k):
        columns = slice(k * width, (k + 1) * width)
        block = pair[:, :, columns].reshape(proj_a.shape[1], width)
        block_high, block_low = halves(block)
        total = narrow_dot(rows_high, block_low) + narrow_dot(rows_low, block_high)
        part_w[k] = total + narrow_dot(rows_high, block_high)

    def take(k):
        gather(3 + k, unit_w(k))

    def hand(k):
        spread(3 + k, unit_w(k))
        aside(1 + k, final_w.at[k], other_w.at[k]).start()

    def take_v():
        give_v().wait_recv()
        part_v[...] = whole_v[rows_of(lane, half), :] + land_v[...]
        gather(2, unit_v)

    def hand_v():
        spread(2, unit_v)
        aside(0, final_v, other_v).start()

    def later_take(k):
        @pl.when(line.has_outer)
        def _():
            take(k)

    def later_take_v():
        @pl.when(line.has_outer)
        def _():
            take_v()

    early = jnp.logical_not(line.has_outer)
    multiply(0)

    @pl.when(early)
    def _():
        take(0)

    for which, unit in enumerate((piece_a, piece_b)):
        spread(which, unit)
        for k in range(1, peers):
            grams(k, which).start()
    gram_a[rows_of(index, piece), :] = piece_a[3][...]
    gram_b[rows_of(index, piece), :] = piece_b[3][...]
    whole_v[...] = split_dot(proj_b[...], buffer_b[...])
    give_v().start()
    for k in range(1, chunks):
        multiply(k)

        @pl.when(early)
        def _():
            take(k)

        if k == min(2, chunks - 1):

            @pl.when(early)
            def _():
                take_v()

    tasks = []
    for k in range(chunks):
        tasks.append(functools.partial(later_take, k))
        if k > 0:
            tasks.append(functools.partial(hand, k - 1))
        if k == min(2, chunks - 1):
            tasks.append(later_take_v)
        if k == min(3, chunks - 1):
            tasks.append(hand_v)
    tasks.append(functools.partial(hand, chunks - 1))
    first = min(4, len(tasks))
    for task in tasks[:first]:
        task()
    tasks = tasks[first:]
    for which in range(2):
        for k in range(1, peers):
            grams(k, which).wait_recv()
    slots = rank // BLOCK * PIECES
    done = [0, 0]

    def between():
        done[0] += 1
        goal = -(-len(tasks) * done[0] // slots)
        while done[1] < min(goal, len(tasks)):
            tasks[done[1]]()
            done[1] += 1

    factor(rank, [gram_a, gram_b], [inv_a, inv_b], works, diags, between)
    high_a[...], low_a[...] = halves(inv_a[...])
    rows_a[...] = proj_a[...].T
    count_a = rows_a.shape[0] // SIDES
    wide_a[...] = split_dot(rows_a[rows_of(lane, count_a), :], inv_a[...], LAST)
    wide_b[...] = split_dot(proj_b[...].T, inv_b[...], LAST)
    ortho_a[...] = wide_a[...].astype(jnp.bfloat16)
    ortho_b[...] = wide_b[...].astype(jnp.bfloat16)
    square_a[...] = jnp.zeros_like(square_a)
    own = rows_of(row, share)

    def use(product, position):
        product_high, product_low = halves(product)
        total = narrow_dot(high_a[...], product_low) + narrow_dot(low_a[...], product_high)
        total = total + narrow_dot(high_a[...], product_high)
        full_a[...] = total
        trans_a[position] = total.astype(jnp.bfloat16)
        square_a[...] += jnp.sum(total * total, axis=1, keepdims=True)
        basis_a[position] = full_a[own, :]

    groups = chunks // joined

    def group(source, k):
        return jnp.concatenate([source[k * joined + i] for i in range(joined)], axis=1)

    def near(k, carry):
        use(group(final_w, k), lane * groups + k)
        return carry

    def far(k, carry):
        for i in range(joined):
            j = k * joined + i
            aside(1 + j, final_w.at[j], other_w.at[j]).wait_recv()
        use(group(other_w, k), (1 - lane) * groups + k)
        return carry

    lax.fori_loop(0, groups, near, 0)
    aside(0, final_v, other_v).wait_recv()
    whole_v[rows_of(lane, half), :] = final_v[...]
    give_v().wait_send()
    whole_v[rows_of(1 - lane, half), :] = other_v[...]
    total_b = split_dot(inv_b[...], whole_v[...])
    full_b[...] = total_b
    trans_b[...] = total_b.astype(jnp.bfloat16)
    square_b[...] = jnp.sum(total_b * total_b, axis=1, keepdims=True)
    lax.fori_loop(0, groups, far, 0)

    def across(column):
        return jnp.broadcast_to(column, (rank, BLOCK)).T[:8]

    def norms(k):
        peer = lax.rem(col + k, col_count)
        return remote(mine, theirs.at[col], sq_s.at[k], sq_r.at[k], {"col": peer})

    mine[0] = across(square_a[...])
    mine[1] = across(square_b[...])
    for k in range(1, col_count):
        norms(k).start()
    theirs[col] = mine[...]
    for k in range(1, col_count):
        norms(k).wait_recv()
    norm = jnp.sqrt(jnp.sum(theirs[...], axis=0) + EPS)
    norm_a, norm_b = norm[0, :1], norm[1, :1]
    scaled_a[...] = (wide_a[...] * (scales[0] / norm_a)).astype(jnp.bfloat16)
    scaled_b[...] = (wide_b[...] * (scales[1] / norm_b)).astype(jnp.bfloat16)
    ranks = lax.broadcasted_iota(jnp.int32, (share, rank), 1)
    owned = lax.broadcasted_iota(jnp.int32, (share, rank), 0) + row * share
    own_a = jnp.sum(jnp.where(ranks == owned, norm_a, 0.0), axis=1, keepdims=True)
    own_b = jnp.sum(jnp.where(ranks == owned, norm_b, 0.0), axis=1, keepdims=True)
    for k in range(basis_a.shape[0]):
        basis_a[k] = basis_a[k] / own_a
    basis_b[...] = full_b[own, :] / own_b
    for k in range(1, col_count):
        norms(k).wait_send()
    for which in range(2):
        for k in range(1, peers):
            grams(k, which).wait_send()
    give_g().wait_send()
    aside(0, final_v, other_v).wait_send()
    for i, unit in enumerate((piece_a, piece_b, unit_v)):
        line.drain(i, *unit)

    def sent(k, carry):
        aside(1 + k, final_w.at[k], other_w.at[k]).wait_send()
        line.drain(3 + k, *unit_w(k))
        return carry

    lax.fori_loop(0, chunks, sent, 0)


def products(proj_a, proj_b, pair, buffer_b, scales):
    row_count, col_count = lax.axis_size("row"), lax.axis_size("col")
    rank = proj_a.shape[0]
    share, half, piece = rank // row_count, rank // 2, rank // (SIDES * col_count)
    side_width = pair.shape[2]
    chunk = CHUNK if side_width % CHUNK == 0 else side_width
    chunks = side_width // chunk
    joined = 2 if chunks % 2 == 0 else 1
    groups, wide_chunk = chunks // joined, chunk * joined
    width_b = buffer_b.shape[1]
    rows_a, rows_b = pair.shape[1], buffer_b.shape[0]

    def array(kind, *shape):
        return jax.ShapeDtypeStruct(shape, kind)

    def space(*shape):
        return pltpu.VMEM(shape, jnp.float32)

    narrow, wide = jnp.bfloat16, jnp.float32
    peers, cols = DMA((2, SIDES * col_count)), DMA((col_count,))
    return pl.pallas_call(
        functools.partial(products_kernel, row_count, col_count, rank, joined, scales),
        out_shape=[
            array(narrow, SIDES * groups, rank, wide_chunk),
            array(narrow, rank, width_b),
            array(wide, SIDES * groups, share, wide_chunk),
            array(wide, share, width_b),
            array(narrow, rows_a, rank),
            array(narrow, rows_b, rank),
            array(narrow, rows_a, rank),
            array(narrow, rows_b, rank),
        ],
        in_specs=[VMEM] * 4,
        out_specs=[VMEM] * 8,
        scratch_shapes=[space(chunks, rank, chunk)] * 5
        + [space(half, width_b)] * 6
        + [space(rank, width_b)]
        + [space(piece, rank)] * 10
        + [space(rank, rank)] * 4
        + [pltpu.VMEM((rank, rank), narrow)] * 2
        + [
            space(SIDES * rows_a, rank),
            space(rows_a, rank),
            space(rows_b, rank),
            space(rank, wide_chunk),
            space(rank, width_b),
            space(rank, 1),
            space(rank, 1),
            space(2, 8, rank),
            space(col_count, 2, 8, rank),
        ]
        + [space(rank, 2 * rank)] * 2
        + [space(BLOCK, 2 * BLOCK)] * 2
        + Reduce.scratch(3 + chunks)
        + [DMA((1 + chunks,))] * 2
        + [DMA((2,))] * 2
        + [peers, peers, cols, cols],
        name="products",
        compiler_params=pltpu.CompilerParams(
            collective_id=2, has_side_effects=True, vmem_limit_bytes=62 * 2**20
        ),
    )(proj_a, proj_b, pair, buffer_b)


def ending_kernel(slabs, *refs):
    buffer_a, trans_a, basis_a, ortho_a, scaled_a = refs[:5]
    buffer_b, trans_b, ortho_b, scaled_b = refs[5:9]
    mom_a, update_a, new_a, mom_b, update_b = refs[9:]
    mom_a[...] = buffer_a[...] - (1.0 - MU) * narrow_dot(ortho_a[...], trans_a[0])
    update_a[...] = narrow_dot(scaled_a[...], trans_a[0]).astype(jnp.bfloat16)
    new_a[...] = basis_a[0]

    @pl.when(pl.program_id(0) < slabs)
    def _():
        mom_b[...] = buffer_b[...] - (1.0 - MU) * narrow_dot(ortho_b[...], trans_b[...])
        update_b[...] = narrow_dot(scaled_b[...], trans_b[...]).astype(jnp.bfloat16)


def ending(buffer_a, trans_a, basis_a, ortho_a, scaled_a, buffer_b, trans_b, ortho_b, scaled_b):
    steps, rank, width = trans_a.shape
    rows_a, rows_b, share = buffer_a.shape[0], buffer_b.shape[0], basis_a.shape[1]
    slabs = 8
    if width % 128 or rows_b % (16 * slabs) or steps < slabs:
        flat = trans_a.swapaxes(0, 1).reshape(rank, -1)
        return (
            buffer_a - (1.0 - MU) * narrow_dot(ortho_a, flat),
            narrow_dot(scaled_a, flat).astype(jnp.bfloat16),
            basis_a.swapaxes(0, 1).reshape(share, -1),
            buffer_b - (1.0 - MU) * narrow_dot(ortho_b, trans_b),
            narrow_dot(scaled_b, trans_b).astype(jnp.bfloat16),
        )
    some = rows_b // slabs
    cut = pl.BlockSpec((rows_a, width), lambda j: (0, j))
    stack = pl.BlockSpec((1, rank, width), lambda j: (j, 0, 0))
    thin = pl.BlockSpec((1, share, width), lambda j: (j, 0, 0))
    fixed_a = pl.BlockSpec((rows_a, rank), lambda j: (0, 0))
    fixed_b = pl.BlockSpec(trans_b.shape, lambda j: (0, 0))
    slab = pl.BlockSpec((some, buffer_b.shape[1]), lambda j: (jnp.minimum(j, slabs - 1), 0))
    rows = pl.BlockSpec((some, rank), lambda j: (jnp.minimum(j, slabs - 1), 0))
    return pl.pallas_call(
        functools.partial(ending_kernel, slabs),
        grid=(steps,),
        out_shape=[
            jax.ShapeDtypeStruct(buffer_a.shape, jnp.float32),
            jax.ShapeDtypeStruct(buffer_a.shape, jnp.bfloat16),
            jax.ShapeDtypeStruct((share, buffer_a.shape[1]), jnp.float32),
            jax.ShapeDtypeStruct(buffer_b.shape, jnp.float32),
            jax.ShapeDtypeStruct(buffer_b.shape, jnp.bfloat16),
        ],
        in_specs=[cut, stack, thin, fixed_a, fixed_a, slab, fixed_b, rows, rows],
        out_specs=[cut, cut, pl.BlockSpec((share, width), lambda j: (0, j)), slab, slab],
        name="ending",
    )(buffer_a, trans_a, basis_a, ortho_a, scaled_a, buffer_b, trans_b, ortho_b, scaled_b)


def shards(mom_a, grad_a, basis_a, mom_b, grad_b, basis_b):
    row_count = lax.axis_size("row")
    buffer_a, buffer_b = MU * mom_a + grad_a, MU * mom_b + grad_b
    proj_a, proj_b, pair = project(basis_a, basis_b, buffer_a, buffer_b)
    rank = proj_a.shape[0]
    scales = [
        math.sqrt(x.shape[0] * x.shape[1] * row_count * lax.axis_size("col") / rank)
        for x in (buffer_a, buffer_b)
    ]
    trans_a, trans_b, basis_a, basis_b, ortho_a, ortho_b, scaled_a, scaled_b = products(
        proj_a, proj_b, pair, buffer_b, scales
    )
    new_mom_a, update_a, new_basis_a, new_mom_b, update_b = ending(
        buffer_a, trans_a, basis_a, ortho_a, scaled_a, buffer_b, trans_b, ortho_b, scaled_b
    )
    return new_mom_a, update_a, new_basis_a, new_mom_b, update_b, basis_b


def solution(mesh):
    spec = P("row", "col")
    return jax.shard_map(
        shards, mesh=mesh, in_specs=(spec,) * 6, out_specs=(spec,) * 6, check_vma=False
    )
```

```python
import functools
import math

import jax
import jax.numpy as jnp
from jax import lax
from jax.experimental import pallas as pl
from jax.experimental.pallas import tpu as pltpu
from jax.sharding import PartitionSpec as P

MU = 0.95
EPS = 1e-06
BLOCK = 128
HIGHEST = lax.Precision.HIGHEST
MESH = pl.DeviceIdType.MESH
VMEM = pl.BlockSpec(memory_space=pltpu.VMEM)
DMA = pltpu.SemaphoreType.DMA
LAST = ((1,), (1,))
FIRST = ((0,), (0,))
PLAIN = ((1,), (0,))
SIDES = 2
PIECES = 4
PIVOTS = 4
CHUNK = 128


def dot(x, y, contract=PLAIN, precision=HIGHEST):
    return lax.dot_general(
        x, y, (contract, ((), ())), precision=precision, preferred_element_type=jnp.float32
    )


def halves(x):
    high = x.astype(jnp.bfloat16)
    return high, (x - high.astype(jnp.float32)).astype(jnp.bfloat16)


def narrow_dot(x, y, contract=PLAIN):
    return lax.dot_general(x, y, (contract, ((), ())), preferred_element_type=jnp.float32)


def split_dot(x, y, contract=PLAIN):
    (x_high, x_low), (y_high, y_low) = halves(x), halves(y)
    total = narrow_dot(x_high, y_low, contract) + narrow_dot(x_low, y_high, contract)
    return total + narrow_dot(x_high, y_high, contract)


def remote(src, dst, send, recv, device):
    return pltpu.make_async_remote_copy(
        src_ref=src,
        dst_ref=dst,
        send_sem=send,
        recv_sem=recv,
        device_id=device,
        device_id_type=MESH,
    )


def partner(position, bit):
    return position + bit - 2 * bit * lax.rem(position // bit, 2)


def col_bits(col_count):
    bits, bit = [], 1
    while bit < col_count:
        bits.append(bit)
        bit *= 2
    return bits


def greet_row(row, row_count, barrier):
    for k in range(1, row_count):
        peer = lax.rem(row + k, row_count)
        pl.semaphore_signal(barrier, inc=1, device_id={"row": peer}, device_id_type=MESH)


def greet_cols(col, bits, barrier):
    for bit in bits:
        peer = partner(col, bit)
        pl.semaphore_signal(barrier, inc=1, device_id={"col": peer}, device_id_type=MESH)


class Line:
    def __init__(self, row_count, sources, outs, sems):
        self.depth = row_count // SIDES
        self.row = lax.axis_index("row")
        self.place = self.row // SIDES
        self.sources, self.outs = sources, outs
        self.up_s, self.up_r, self.dn_s, self.dn_r = sems
        self.has_up = self.place < self.depth - 1
        self.has_dn = self.place > 0

    @staticmethod
    def scratch(row_count, count):
        return [DMA((count, row_count // SIDES))] * 4

    def up(self, i, slot, d, first=False):
        src = self.sources[i] if first else self.outs[i].at[slot]
        device = {"row": self.row + SIDES}
        return remote(src, self.outs[i].at[slot], self.up_s.at[i, d], self.up_r.at[i, d], device)

    def dn(self, i, slot, d, first=False):
        src = self.sources[i] if first else self.outs[i].at[slot]
        device = {"row": self.row - SIDES}
        return remote(src, self.outs[i].at[slot], self.dn_s.at[i, d], self.dn_r.at[i, d], device)

    def has(self, way, d):
        there = self.place + d * (2 * way - 1)
        return (d >= 0) & (there >= 0) & (there < self.depth) & ((way == 0) | (d > 0))

    def start(self, i):
        @pl.when(self.has_up)
        def _():
            self.up(i, self.place, 0, True).start()

        @pl.when(self.has_dn)
        def _():
            self.dn(i, self.place, 0, True).start()

    def forward(self, d):
        for i in range(len(self.outs)):

            @pl.when(self.has(0, d))
            def _():
                self.up(i, self.place - d, d - 1).wait_recv()

                @pl.when(self.has_up)
                def _():
                    self.up(i, self.place - d, d).start()

            @pl.when(self.has(1, d))
            def _():
                self.dn(i, self.place + d, d - 1).wait_recv()

                @pl.when(self.has_dn)
                def _():
                    self.dn(i, self.place + d, d).start()

    def drain(self):
        def sent(d, carry):
            for i in range(len(self.outs)):

                @pl.when((self.place - d >= 0) & self.has_up)
                def _():
                    self.up(i, self.place - d, d).wait_send()

                @pl.when((self.place + d < self.depth) & self.has_dn)
                def _():
                    self.dn(i, self.place + d, d).wait_send()

            return carry

        lax.fori_loop(0, self.depth, sent, 0)


def project_kernel(row_count, bits, *refs):
    basis_a, basis_b, buffer_a, buffer_b, proj_a, proj_b, pair = refs[:7]
    mine, theirs, all_b, high, low, part_b, land_b = refs[7:14]
    refs = refs[14:]
    stages = len(bits) + 1
    sums, refs = list(refs[:stages]) + [proj_a], refs[stages:]
    landed, refs = refs[:stages], refs[stages:]
    sums_b, refs = refs[: len(bits)], refs[len(bits) :]
    landed_b, refs = refs[: len(bits) - 1], refs[len(bits) - 1 :]
    line_sems, refs = refs[:4], refs[4:]
    small_s, small_r, small_own, swap_s, swap_r, swap_own, sum_s, sum_r, b_s, b_r = refs
    row, col = lax.axis_index("row"), lax.axis_index("col")
    place, lane = row // SIDES, lax.rem(row, SIDES)
    other = place * SIDES + (1 - lane)
    share, width = basis_a.shape[0], mine.shape[2]
    depth = row_count // SIDES
    rank = share * row_count
    half = rank // 2
    twin, part = partner(col, 1), lax.rem(col, 2)
    devices = [{"col": partner(col, bit)} for bit in bits] + [{"row": other}]

    barrier = pltpu.get_barrier_semaphore()
    greet_row(row, row_count, barrier)
    greet_cols(col, bits, barrier)
    pl.semaphore_wait(barrier, row_count - 1 + len(bits))

    def columns(position):
        return pl.ds(pl.multiple_of(position * width, width), width)

    def small(k):
        peer = lax.rem(place + k, depth) * SIDES + lane
        return remote(basis_b, all_b.at[row], small_s.at[k], small_r.at[k], {"row": peer})

    def beside(k):
        slot = lax.rem(place + depth - k, depth) * SIDES + lane
        source = basis_b if k == 0 else all_b.at[slot]
        sems = small_s.at[depth + k], small_r.at[depth + k]
        return remote(source, all_b.at[slot], *sems, {"row": other})

    swap_basis = remote(
        basis_a.at[:, columns(1 - lane)], theirs.at[place], swap_s.at[0], swap_r.at[0], {"row": other}
    )
    swap_rows = remote(
        buffer_a.at[:, columns(1 - lane)], pair.at[lane], swap_s.at[1], swap_r.at[1], {"row": other}
    )
    own_basis = pltpu.make_async_copy(basis_a.at[:, columns(lane)], mine.at[place], swap_own.at[0])
    own_rows = pltpu.make_async_copy(buffer_a.at[:, columns(lane)], pair.at[lane], swap_own.at[1])
    small_local = pltpu.make_async_copy(basis_b, all_b.at[row], small_own)
    sources = [basis_a.at[:, columns(lane)], theirs.at[place]]
    line = Line(row_count, sources, [mine, theirs], line_sems)
    swap_basis.start()
    line.start(0)
    for k in range(1, depth):
        small(k).start()
    beside(0).start()
    swap_rows.start()
    own_basis.start()
    own_rows.start()
    small_local.start()

    def strip(place_, position):
        return pl.ds(pl.multiple_of((place_ * SIDES + position) * share, share), share)

    def summing(stage, place_):
        sems = sum_s.at[stage, place_], sum_r.at[stage, place_]
        rows = strip(place_, part if stage else 1 - part)
        here, there = sums[stage].at[rows, :], landed[stage].at[rows, :]
        return remote(here, there, *sems, devices[stage])

    def giving(place_, position):
        here = proj_a.at[strip(place_, position), :]
        return remote(here, here, sum_s.at[stages, place_], sum_r.at[stages, place_], {"col": twin})

    def compute(place_):
        blocks = jnp.concatenate([mine[place_], theirs[place_]], axis=0)
        block_high, block_low = halves(blocks)
        total = narrow_dot(block_high, low[...], LAST) + narrow_dot(block_low, high[...], LAST)
        total = total + narrow_dot(block_high, high[...], LAST)
        for k, side in enumerate((lane, 1 - lane)):
            start = (place_ * SIDES + side) * share
            sums[0][pl.ds(pl.multiple_of(start, share), share), :] = total[k * share : (k + 1) * share]
        summing(0, place_).start()

    def step(stage, place_):
        summing(stage, place_).wait_recv()
        rows = strip(place_, part)
        sums[stage + 1][rows, :] = sums[stage][rows, :] + landed[stage][rows, :]
        if stage + 1 < stages:
            summing(stage + 1, place_).start()
        else:
            giving(place_, part).start()

    begin = min(2, depth - 1)

    def progress(turn):
        for stage in range(stages):
            d = turn - stage
            for near in range(begin):
                for way in range(2):

                    @pl.when((d == begin) & line.has(way, near))
                    def _():
                        step(stage, place + near * (2 * way - 1))

            for way in range(2):

                @pl.when((d >= begin) & line.has(way, d))
                def _():
                    step(stage, place + d * (2 * way - 1))

    def half_rows(position):
        return pl.ds(pl.multiple_of(position * half, half), half)

    def scatter_b():
        return remote(part_b.at[half_rows(1 - part), :], land_b, b_s.at[0], b_r.at[0], {"col": twin})

    def exchange_b(stage):
        device = {"col": partner(col, bits[stage])}
        return remote(sums_b[stage - 1], landed_b[stage - 1], b_s.at[stage], b_r.at[stage], device)

    def return_b(position):
        rows = half_rows(position)
        index = len(bits)
        return remote(sums_b[-1], proj_b.at[rows, :], b_s.at[index], b_r.at[index], {"col": twin})

    def pass_b():
        for k in range(1, depth):
            small(k).wait_recv()
            beside(k).start()

    def begin_b():
        small_local.wait()
        for k in range(depth):
            beside(k).wait_recv()
        flat = all_b[...].reshape(rank, basis_b.shape[1])
        part_b[...] = split_dot(flat, buffer_b[...], LAST)
        scatter_b().start()

    def second_b():
        scatter_b().wait_recv()
        sums_b[0][...] = part_b[half_rows(part), :] + land_b[...]
        if len(bits) > 1:
            exchange_b(1).start()

    def finish_b():
        for stage in range(1, len(bits)):
            exchange_b(stage).wait_recv()
            sums_b[stage][...] = sums_b[stage - 1][...] + landed_b[stage - 1][...]
            if stage + 1 < len(bits):
                exchange_b(stage + 1).start()
        return_b(part).start()
        proj_b[half_rows(part), :] = sums_b[-1][...]

    swap_basis.wait_recv()
    line.start(1)

    def units(d):
        for way in range(2):

            @pl.when(line.has(way, d))
            def _():
                compute(place + d * (2 * way - 1))

    def advance(d, carry):
        line.forward(d)

        @pl.when(d == 1)
        def _():
            pass_b()
            begin_b()
            if depth > 2:
                second_b()

        @pl.when(d == begin)
        def _():
            own_basis.wait()
            own_rows.wait()
            swap_rows.wait_recv()
            high[...], low[...] = halves(pair[...].reshape(high.shape))
            if depth == 2:
                second_b()

        def catch_up(near, inner):
            units(near)
            return inner

        lax.fori_loop(jnp.where(d == begin, 0, d), jnp.where(d < begin, 0, d + 1), catch_up, 0)
        progress(d)
        return carry

    lax.fori_loop(1, depth, advance, 0)
    progress(depth)
    finish_b()
    for d in range(depth + 1, depth + stages - 1):
        progress(d)
    return_b(1 - part).wait_recv()
    swap_basis.wait_send()
    swap_rows.wait_send()
    for k in range(depth):
        beside(k).wait_send()
    for k in range(1, depth):
        small(k).wait_send()
    line.drain()

    def sent(place_, carry):
        giving(place_, 1 - part).wait_recv()
        giving(place_, part).wait_send()
        for stage in range(stages):
            summing(stage, place_).wait_send()
        return carry

    lax.fori_loop(0, depth, sent, 0)
    scatter_b().wait_send()
    for stage in range(1, len(bits)):
        exchange_b(stage).wait_send()
    return_b(part).wait_send()


def project(basis_a, basis_b, buffer_a, buffer_b):
    row_count, col_count = lax.axis_size("row"), lax.axis_size("col")
    bits = col_bits(col_count)
    stages = len(bits) + 1
    depth = row_count // SIDES
    (share, width), rows_a, rows_b = basis_a.shape, buffer_a.shape[0], buffer_b.shape[0]
    rank, width = share * row_count, width // SIDES

    def space(*shape):
        return pltpu.VMEM(shape, jnp.float32)

    narrow = pltpu.VMEM((SIDES * rows_a, width), jnp.bfloat16)
    return pl.pallas_call(
        functools.partial(project_kernel, row_count, bits),
        out_shape=[
            jax.ShapeDtypeStruct(shape, jnp.float32)
            for shape in ((rank, SIDES * rows_a), (rank, rows_b), (SIDES, rows_a, width))
        ],
        in_specs=[VMEM] * 4,
        out_specs=[VMEM] * 3,
        scratch_shapes=[
            space(depth, share, width),
            space(depth, share, width),
            space(row_count, *basis_b.shape),
            narrow,
            narrow,
            space(rank, rows_b),
            space(rank // 2, rows_b),
        ]
        + [space(rank, SIDES * rows_a)] * (2 * stages)
        + [space(rank // 2, rows_b)] * (2 * len(bits) - 1)
        + Line.scratch(row_count, 2)
        + [DMA((row_count,)), DMA((row_count,)), DMA(()), DMA((2,)), DMA((2,)), DMA((2,))]
        + [DMA((stages + 1, depth))] * 2
        + [DMA((len(bits) + 1,))] * 2,
        name="project",
        compiler_params=pltpu.CompilerParams(
            collective_id=1, has_side_effects=True, vmem_limit_bytes=60 * 2**20
        ),
    )(basis_a, basis_b, buffer_a, buffer_b)


def factor(rank, grams, outs, works, diags, between):
    eye_rows = lax.broadcasted_iota(jnp.int32, (rank, rank), 0)
    eye_cols = lax.broadcasted_iota(jnp.int32, (rank, rank), 1)
    for gram, work in zip(grams, works):
        work[:, :rank] = gram[...]
        work[:, rank:] = (eye_rows == eye_cols).astype(jnp.float32)
    rows = lax.broadcasted_iota(jnp.int32, (BLOCK, 1), 0)
    lanes = lax.broadcasted_iota(jnp.int32, (1, BLOCK), 1)
    for k in range(rank // BLOCK):
        low, high = k * BLOCK, (k + 1) * BLOCK
        for work, diag in zip(works, diags):
            diag[:, :BLOCK] = work[low:high, low:high]
            diag[:, BLOCK:] = (rows == lanes).astype(jnp.float32)

        def step(base, i, carry):
            j = PIVOTS * i
            for diag in diags:
                square = diag[base:, :BLOCK]
                tops = [diag[pl.ds(j + p, 1), :] for p in range(PIVOTS)]

                def pick(some, p):
                    kept = jnp.where(lanes == j + p, some[:, :BLOCK], 0.0)
                    return jnp.sum(kept, axis=1, keepdims=True)

                cols = [pick(square, p) for p in range(PIVOTS)]
                cells = [[pick(top, p) for p in range(PIVOTS)] for top in tops]
                total = diag[base:, :]
                for p in range(PIVOTS):
                    scale = 1.0 / cells[p][p]
                    weights = jnp.where(rows[base:] > j + p, cols[p] * scale, 0.0)
                    for q in range(p + 1, PIVOTS):
                        ratio = cells[q][p] * scale
                        tops[q] = tops[q] - ratio * tops[p]
                        cols[q] = cols[q] - weights * cells[p][q]
                        cells[q] = [cells[q][r] - ratio * cells[p][r] for r in range(PIVOTS)]
                    total = total - weights * tops[p]
                diag[base:, :] = total
            return carry

        for piece in range(PIECES):
            steps = BLOCK // PIVOTS // PIECES
            some = functools.partial(step, piece * BLOCK // PIECES)
            lax.fori_loop(piece * steps, (piece + 1) * steps, some, 0)
            if piece + 1 < PIECES:
                between()
        width = slice(low, rank + high)
        for work, diag in zip(works, diags):
            pivots = jnp.sum(
                jnp.where(rows == lanes, diag[:, :BLOCK], 0.0), axis=1, keepdims=True
            )
            inverse = diag[:, BLOCK:] * (1.0 / jnp.sqrt(pivots))
            panel = dot(inverse, work[low:high, width])
            work[low:high, width] = panel
            if high < rank:
                factors = panel[:, BLOCK : rank - low]
                work[high:, width] = work[high:, width] - dot(factors, panel, FIRST)
        between()
    for work, out in zip(works, outs):
        out[...] = work[:, rank:]


class Reduce:
    def __init__(self, row_count, sems):
        depth = row_count // SIDES
        row = lax.axis_index("row")
        place, lane = row // SIDES, lax.rem(row, SIDES)
        lower = place < depth // 2
        self.place, self.lane, self.depth = place, lane, depth
        self.other = place * SIDES + (1 - lane)
        toward = jnp.where(lower, SIDES, -SIDES)
        self.inner, self.outer = {"row": row + toward}, {"row": row - toward}
        self.steps = jnp.where(lower, depth // 2 - 1 - place, place - depth // 2)
        self.middle = self.steps == 0
        self.has_outer = self.steps < depth // 2 - 1
        self.sems = sems

    @staticmethod
    def scratch(count):
        return [DMA((count,))] * 6

    def inward(self, i, part, arrive):
        return remote(part, arrive, self.sems[0].at[i], self.sems[1].at[i], self.inner)

    def swap(self, i, part, meet):
        return remote(part, meet, self.sems[2].at[i], self.sems[3].at[i], self.inner)

    def outward(self, i, final):
        return remote(final, final, self.sems[4].at[i], self.sems[5].at[i], self.outer)

    def gather(self, i, part, arrive, meet):
        @pl.when(self.has_outer)
        def _():
            self.inward(i, part, arrive).wait_recv()
            part[...] = part[...] + arrive[...]

        @pl.when(self.middle)
        def _():
            self.swap(i, part, meet).start()

        @pl.when(self.steps > 0)
        def _():
            self.inward(i, part, arrive).start()

    def spread(self, i, part, meet, final):
        @pl.when(self.middle)
        def _():
            self.swap(i, part, meet).wait_recv()
            final[...] = part[...] + meet[...]

        @pl.when(self.steps > 0)
        def _():
            self.outward(i, final).wait_recv()

        @pl.when(self.has_outer)
        def _():
            self.outward(i, final).start()

    def drain(self, i, part, arrive, meet, final):
        @pl.when(self.middle)
        def _():
            self.swap(i, part, meet).wait_send()

        @pl.when(self.steps > 0)
        def _():
            self.inward(i, part, arrive).wait_send()

        @pl.when(self.has_outer)
        def _():
            self.outward(i, final).wait_send()


def products_kernel(row_count, col_count, rank, joined, scales, *refs):
    proj_a, proj_b, pair, buffer_b = refs[:4]
    trans_a, trans_b, basis_a, basis_b, ortho_a, ortho_b, scaled_a, scaled_b = refs[4:12]
    part_w, arrive_w, meet_w, final_w, other_w = refs[12:17]
    part_v, arrive_v, meet_v, final_v, land_v, other_v, whole_v = refs[17:24]
    piece_a, piece_b = refs[24:28], refs[28:32]
    cast_b, land_b, gram_a, gram_b, inv_a, inv_b, high_a, low_a = refs[32:40]
    rows_a, wide_a, wide_b, full_a, full_b, square_a, square_b, mine, theirs = refs[40:49]
    works, diags = refs[49:51], refs[51:53]
    reduce_sems, refs = refs[53:59], refs[59:]
    side_s, side_r, give_s, give_r, gram_s, gram_r, sq_s, sq_r = refs
    row, col = lax.axis_index("row"), lax.axis_index("col")
    line = Reduce(row_count, reduce_sems)
    lane, place, other = line.lane, line.place, line.other
    share, half = rank // row_count, rank // 2
    peers = SIDES * col_count
    piece = rank // peers
    index = lane * col_count + col
    chunks = part_w.shape[0]
    width = part_w.shape[2]

    def peer_of(k):
        target = lax.rem(index + k, peers)
        return (place * SIDES + target // col_count, lax.rem(target, col_count))

    barrier = pltpu.get_barrier_semaphore()

    pl.semaphore_signal(barrier, inc=1, device_id=line.inner, device_id_type=MESH)
    for k in range(1, peers):
        pl.semaphore_signal(barrier, inc=1, device_id=peer_of(k), device_id_type=MESH)

    @pl.when(line.has_outer)
    def _():
        pl.semaphore_signal(barrier, inc=1, device_id=line.outer, device_id_type=MESH)
        pl.semaphore_wait(barrier, peers + 1)

    @pl.when(jnp.logical_not(line.has_outer))
    def _():
        pl.semaphore_wait(barrier, peers)

    def rows_of(position, size):
        return pl.ds(pl.multiple_of(position * size, size), size)

    def give_g():
        return remote(cast_b, land_b, give_s.at[0], give_r.at[0], {"row": other})

    def give_v():
        there = whole_v.at[rows_of(1 - lane, half), :]
        return remote(there, land_v, give_s.at[1], give_r.at[1], {"row": other})

    bits = col_bits(col_count)[::-1]

    def held(stage):
        columns = [col]
        for bit in bits[: max(stage - 1, 0)]:
            columns += [partner(c, bit) for c in columns]
        sides = [lane] if stage == 0 else [lane, 1 - lane]
        return [side * col_count + c for side in sides for c in columns]

    def grams(stage):
        device = {"row": other} if stage == 0 else {"col": partner(col, bits[stage - 1])}
        copies = []
        for k, position in enumerate(held(stage)):
            for which, gram in enumerate((gram_a, gram_b)):
                here = gram.at[rows_of(position, piece), :]
                sems = gram_s.at[which, stage, k], gram_r.at[which, stage, k]
                copies.append(remote(here, here, *sems, device))
        return copies

    def send_grams(stage):
        for copy in grams(stage):
            copy.start()

    def await_grams(stage):
        for copy in grams(stage):
            copy.wait_recv()

    def aside(i, final, target):
        return remote(final, target, side_s.at[i], side_r.at[i], {"row": other})

    unit_v = (part_v, arrive_v, meet_v, final_v)

    def unit_w(k):
        return part_w.at[k], arrive_w.at[k], meet_w.at[k], final_w.at[k]

    def gather(i, unit):
        line.gather(i, unit[0], unit[1], unit[2])

    def spread(i, unit):
        line.spread(i, unit[0], unit[2], unit[3])

    theirs_index = (1 - lane) * col_count + col
    cast_b[...] = dot(proj_b[rows_of(theirs_index, piece), :], proj_b[...], LAST)
    give_g().start()
    piece_a[0][...] = dot(proj_a[rows_of(index, piece), :], proj_a[...], LAST)
    gather(0, piece_a)
    piece_b[0][...] = dot(proj_b[rows_of(index, piece), :], proj_b[...], LAST)
    give_g().wait_recv()
    piece_b[0][...] = piece_b[0][...] + land_b[...]
    gather(1, piece_b)
    rows_high, rows_low = halves(proj_a[...])

    def multiply(k):
        columns = slice(k * width, (k + 1) * width)
        block = pair[:, :, columns].reshape(proj_a.shape[1], width)
        block_high, block_low = halves(block)
        total = narrow_dot(rows_high, block_low) + narrow_dot(rows_low, block_high)
        part_w[k] = total + narrow_dot(rows_high, block_high)

    def take(k):
        gather(3 + k, unit_w(k))

    def hand(k):
        spread(3 + k, unit_w(k))
        aside(1 + k, final_w.at[k], other_w.at[k]).start()

    def take_v():
        give_v().wait_recv()
        part_v[...] = whole_v[rows_of(lane, half), :] + land_v[...]
        gather(2, unit_v)

    def hand_v():
        spread(2, unit_v)
        aside(0, final_v, other_v).start()

    def later_take(k):
        @pl.when(line.has_outer)
        def _():
            take(k)

    def later_take_v():
        @pl.when(line.has_outer)
        def _():
            take_v()

    early = jnp.logical_not(line.has_outer)
    multiply(0)

    @pl.when(early)
    def _():
        take(0)

    for which, unit in enumerate((piece_a, piece_b)):
        spread(which, unit)
    gram_a[rows_of(index, piece), :] = piece_a[3][...]
    gram_b[rows_of(index, piece), :] = piece_b[3][...]
    send_grams(0)
    whole_v[...] = split_dot(proj_b[...], buffer_b[...])
    give_v().start()
    for k in range(1, chunks):
        multiply(k)

        @pl.when(early)
        def _():
            take(k)

        if k == min(2, chunks - 1):

            @pl.when(early)
            def _():
                take_v()

            await_grams(0)
            send_grams(1)
        if k == min(3, chunks - 1):
            later_take(0)

    tasks = []
    for k in range(chunks):
        if k > 0:
            tasks.append(functools.partial(later_take, k))
            tasks.append(functools.partial(hand, k - 1))
        if k == min(2, chunks - 1):
            tasks.append(later_take_v)
        if k == min(3, chunks - 1):
            tasks.append(hand_v)
    tasks.append(functools.partial(hand, chunks - 1))
    for stage in range(1, len(bits) + 1):
        for _ in range(min(2, len(tasks))):
            tasks.pop(0)()
        await_grams(stage)
        if stage < len(bits):
            send_grams(stage + 1)
    slots = rank // BLOCK * PIECES
    done = [0, 0]

    def between():
        done[0] += 1
        goal = -(-len(tasks) * done[0] // slots)
        while done[1] < min(goal, len(tasks)):
            tasks[done[1]]()
            done[1] += 1

    factor(rank, [gram_a, gram_b], [inv_a, inv_b], works, diags, between)
    high_a[...], low_a[...] = halves(inv_a[...])
    rows_a[...] = proj_a[...].T
    count_a = rows_a.shape[0] // SIDES
    wide_a[...] = split_dot(rows_a[rows_of(lane, count_a), :], inv_a[...], LAST)
    wide_b[...] = split_dot(proj_b[...].T, inv_b[...], LAST)
    ortho_a[...] = wide_a[...].astype(jnp.bfloat16)
    ortho_b[...] = wide_b[...].astype(jnp.bfloat16)
    square_a[...] = jnp.zeros_like(square_a)
    own = rows_of(row, share)

    def use(product, position):
        product_high, product_low = halves(product)
        total = narrow_dot(high_a[...], product_low) + narrow_dot(low_a[...], product_high)
        total = total + narrow_dot(high_a[...], product_high)
        full_a[...] = total
        trans_a[position] = total.astype(jnp.bfloat16)
        square_a[...] += jnp.sum(total * total, axis=1, keepdims=True)
        basis_a[position] = full_a[own, :]

    groups = chunks // joined

    def group(source, k):
        return jnp.concatenate([source[k * joined + i] for i in range(joined)], axis=1)

    def near(k, carry):
        use(group(final_w, k), lane * groups + k)
        return carry

    def far(k, carry):
        for i in range(joined):
            j = k * joined + i
            aside(1 + j, final_w.at[j], other_w.at[j]).wait_recv()
        use(group(other_w, k), (1 - lane) * groups + k)
        return carry

    lax.fori_loop(0, groups, near, 0)
    aside(0, final_v, other_v).wait_recv()
    whole_v[rows_of(lane, half), :] = final_v[...]
    give_v().wait_send()
    whole_v[rows_of(1 - lane, half), :] = other_v[...]
    total_b = split_dot(inv_b[...], whole_v[...])
    full_b[...] = total_b
    trans_b[...] = total_b.astype(jnp.bfloat16)
    square_b[...] = jnp.sum(total_b * total_b, axis=1, keepdims=True)
    lax.fori_loop(0, groups, far, 0)

    def across(column):
        return jnp.broadcast_to(column, (rank, BLOCK)).T[:8]

    def norms(k):
        peer = lax.rem(col + k, col_count)
        return remote(mine, theirs.at[col], sq_s.at[k], sq_r.at[k], {"col": peer})

    mine[0] = across(square_a[...])
    mine[1] = across(square_b[...])
    for k in range(1, col_count):
        norms(k).start()
    theirs[col] = mine[...]
    for k in range(1, col_count):
        norms(k).wait_recv()
    norm = jnp.sqrt(jnp.sum(theirs[...], axis=0) + EPS)
    norm_a, norm_b = norm[0, :1], norm[1, :1]
    scaled_a[...] = (wide_a[...] * (scales[0] / norm_a)).astype(jnp.bfloat16)
    scaled_b[...] = (wide_b[...] * (scales[1] / norm_b)).astype(jnp.bfloat16)
    ranks = lax.broadcasted_iota(jnp.int32, (share, rank), 1)
    owned = lax.broadcasted_iota(jnp.int32, (share, rank), 0) + row * share
    own_a = jnp.sum(jnp.where(ranks == owned, norm_a, 0.0), axis=1, keepdims=True)
    own_b = jnp.sum(jnp.where(ranks == owned, norm_b, 0.0), axis=1, keepdims=True)
    for k in range(basis_a.shape[0]):
        basis_a[k] = basis_a[k] / own_a
    basis_b[...] = full_b[own, :] / own_b
    for k in range(1, col_count):
        norms(k).wait_send()
    for stage in range(len(bits) + 1):
        for copy in grams(stage):
            copy.wait_send()
    give_g().wait_send()
    aside(0, final_v, other_v).wait_send()
    for i, unit in enumerate((piece_a, piece_b, unit_v)):
        line.drain(i, *unit)

    def sent(k, carry):
        aside(1 + k, final_w.at[k], other_w.at[k]).wait_send()
        line.drain(3 + k, *unit_w(k))
        return carry

    lax.fori_loop(0, chunks, sent, 0)


def products(proj_a, proj_b, pair, buffer_b, scales):
    row_count, col_count = lax.axis_size("row"), lax.axis_size("col")
    rank = proj_a.shape[0]
    share, half, piece = rank // row_count, rank // 2, rank // (SIDES * col_count)
    side_width = pair.shape[2]
    chunk = CHUNK if side_width % CHUNK == 0 else side_width
    chunks = side_width // chunk
    joined = 2 if chunks % 2 == 0 else 1
    groups, wide_chunk = chunks // joined, chunk * joined
    width_b = buffer_b.shape[1]
    rows_a, rows_b = pair.shape[1], buffer_b.shape[0]

    def array(kind, *shape):
        return jax.ShapeDtypeStruct(shape, kind)

    def space(*shape):
        return pltpu.VMEM(shape, jnp.float32)

    narrow, wide = jnp.bfloat16, jnp.float32
    grams = DMA((2, len(col_bits(col_count)) + 1, SIDES * col_count))
    cols = DMA((col_count,))
    return pl.pallas_call(
        functools.partial(products_kernel, row_count, col_count, rank, joined, scales),
        out_shape=[
            array(narrow, SIDES * groups, rank, wide_chunk),
            array(narrow, rank, width_b),
            array(wide, SIDES * groups, share, wide_chunk),
            array(wide, share, width_b),
            array(narrow, rows_a, rank),
            array(narrow, rows_b, rank),
            array(narrow, rows_a, rank),
            array(narrow, rows_b, rank),
        ],
        in_specs=[VMEM] * 4,
        out_specs=[VMEM] * 8,
        scratch_shapes=[space(chunks, rank, chunk)] * 5
        + [space(half, width_b)] * 6
        + [space(rank, width_b)]
        + [space(piece, rank)] * 10
        + [space(rank, rank)] * 4
        + [pltpu.VMEM((rank, rank), narrow)] * 2
        + [
            space(SIDES * rows_a, rank),
            space(rows_a, rank),
            space(rows_b, rank),
            space(rank, wide_chunk),
            space(rank, width_b),
            space(rank, 1),
            space(rank, 1),
            space(2, 8, rank),
            space(col_count, 2, 8, rank),
        ]
        + [space(rank, 2 * rank)] * 2
        + [space(BLOCK, 2 * BLOCK)] * 2
        + Reduce.scratch(3 + chunks)
        + [DMA((1 + chunks,))] * 2
        + [DMA((2,))] * 2
        + [grams, grams, cols, cols],
        name="products",
        compiler_params=pltpu.CompilerParams(
            collective_id=2, has_side_effects=True, vmem_limit_bytes=62 * 2**20
        ),
    )(proj_a, proj_b, pair, buffer_b)


def ending_kernel(slabs, *refs):
    buffer_a, trans_a, basis_a, ortho_a, scaled_a = refs[:5]
    buffer_b, trans_b, ortho_b, scaled_b = refs[5:9]
    mom_a, update_a, new_a, mom_b, update_b = refs[9:]
    mom_a[...] = buffer_a[...] - (1.0 - MU) * narrow_dot(ortho_a[...], trans_a[0])
    update_a[...] = narrow_dot(scaled_a[...], trans_a[0]).astype(jnp.bfloat16)
    new_a[...] = basis_a[0]

    @pl.when(pl.program_id(0) < slabs)
    def _():
        mom_b[...] = buffer_b[...] - (1.0 - MU) * narrow_dot(ortho_b[...], trans_b[...])
        update_b[...] = narrow_dot(scaled_b[...], trans_b[...]).astype(jnp.bfloat16)


def ending(buffer_a, trans_a, basis_a, ortho_a, scaled_a, buffer_b, trans_b, ortho_b, scaled_b):
    steps, rank, width = trans_a.shape
    rows_a, rows_b, share = buffer_a.shape[0], buffer_b.shape[0], basis_a.shape[1]
    slabs = 8
    if width % 128 or rows_b % (16 * slabs) or steps < slabs:
        flat = trans_a.swapaxes(0, 1).reshape(rank, -1)
        return (
            buffer_a - (1.0 - MU) * narrow_dot(ortho_a, flat),
            narrow_dot(scaled_a, flat).astype(jnp.bfloat16),
            basis_a.swapaxes(0, 1).reshape(share, -1),
            buffer_b - (1.0 - MU) * narrow_dot(ortho_b, trans_b),
            narrow_dot(scaled_b, trans_b).astype(jnp.bfloat16),
        )
    some = rows_b // slabs
    cut = pl.BlockSpec((rows_a, width), lambda j: (0, j))
    stack = pl.BlockSpec((1, rank, width), lambda j: (j, 0, 0))
    thin = pl.BlockSpec((1, share, width), lambda j: (j, 0, 0))
    fixed_a = pl.BlockSpec((rows_a, rank), lambda j: (0, 0))
    fixed_b = pl.BlockSpec(trans_b.shape, lambda j: (0, 0))
    slab = pl.BlockSpec((some, buffer_b.shape[1]), lambda j: (jnp.minimum(j, slabs - 1), 0))
    rows = pl.BlockSpec((some, rank), lambda j: (jnp.minimum(j, slabs - 1), 0))
    return pl.pallas_call(
        functools.partial(ending_kernel, slabs),
        grid=(steps,),
        out_shape=[
            jax.ShapeDtypeStruct(buffer_a.shape, jnp.float32),
            jax.ShapeDtypeStruct(buffer_a.shape, jnp.bfloat16),
            jax.ShapeDtypeStruct((share, buffer_a.shape[1]), jnp.float32),
            jax.ShapeDtypeStruct(buffer_b.shape, jnp.float32),
            jax.ShapeDtypeStruct(buffer_b.shape, jnp.bfloat16),
        ],
        in_specs=[cut, stack, thin, fixed_a, fixed_a, slab, fixed_b, rows, rows],
        out_specs=[cut, cut, pl.BlockSpec((share, width), lambda j: (0, j)), slab, slab],
        name="ending",
    )(buffer_a, trans_a, basis_a, ortho_a, scaled_a, buffer_b, trans_b, ortho_b, scaled_b)


def shards(mom_a, grad_a, basis_a, mom_b, grad_b, basis_b):
    row_count = lax.axis_size("row")
    buffer_a, buffer_b = MU * mom_a + grad_a, MU * mom_b + grad_b
    proj_a, proj_b, pair = project(basis_a, basis_b, buffer_a, buffer_b)
    rank = proj_a.shape[0]
    scales = [
        math.sqrt(x.shape[0] * x.shape[1] * row_count * lax.axis_size("col") / rank)
        for x in (buffer_a, buffer_b)
    ]
    trans_a, trans_b, basis_a, basis_b, ortho_a, ortho_b, scaled_a, scaled_b = products(
        proj_a, proj_b, pair, buffer_b, scales
    )
    new_mom_a, update_a, new_basis_a, new_mom_b, update_b = ending(
        buffer_a, trans_a, basis_a, ortho_a, scaled_a, buffer_b, trans_b, ortho_b, scaled_b
    )
    return new_mom_a, update_a, new_basis_a, new_mom_b, update_b, basis_b


def solution(mesh):
    spec = P("row", "col")
    return jax.shard_map(
        shards, mesh=mesh, in_specs=(spec,) * 6, out_specs=(spec,) * 6, check_vma=False
    )
```

```python
import functools
import math

import jax
import jax.numpy as jnp
from jax import lax
from jax.experimental import pallas as pl
from jax.experimental.pallas import tpu as pltpu
from jax.sharding import PartitionSpec as P

MU = 0.95
EPS = 1e-06
BLOCK = 128
HIGHEST = lax.Precision.HIGHEST
MESH = pl.DeviceIdType.MESH
VMEM = pl.BlockSpec(memory_space=pltpu.VMEM)
DMA = pltpu.SemaphoreType.DMA
LAST = ((1,), (1,))
FIRST = ((0,), (0,))
PLAIN = ((1,), (0,))
SIDES = 2
PIECES = 4
PIVOTS = 4
CHUNK = 128


def dot(x, y, contract=PLAIN, precision=HIGHEST):
    return lax.dot_general(
        x, y, (contract, ((), ())), precision=precision, preferred_element_type=jnp.float32
    )


def halves(x):
    high = x.astype(jnp.bfloat16)
    return high, (x - high.astype(jnp.float32)).astype(jnp.bfloat16)


def narrow_dot(x, y, contract=PLAIN):
    return lax.dot_general(x, y, (contract, ((), ())), preferred_element_type=jnp.float32)


def split_dot(x, y, contract=PLAIN):
    (x_high, x_low), (y_high, y_low) = halves(x), halves(y)
    total = narrow_dot(x_high, y_low, contract) + narrow_dot(x_low, y_high, contract)
    return total + narrow_dot(x_high, y_high, contract)


def remote(src, dst, send, recv, device):
    return pltpu.make_async_remote_copy(
        src_ref=src,
        dst_ref=dst,
        send_sem=send,
        recv_sem=recv,
        device_id=device,
        device_id_type=MESH,
    )


def partner(position, bit):
    return position + bit - 2 * bit * lax.rem(position // bit, 2)


def col_bits(col_count):
    bits, bit = [], 1
    while bit < col_count:
        bits.append(bit)
        bit *= 2
    return bits


def greet_row(row, row_count, barrier):
    for k in range(1, row_count):
        peer = lax.rem(row + k, row_count)
        pl.semaphore_signal(barrier, inc=1, device_id={"row": peer}, device_id_type=MESH)


def greet_cols(col, bits, barrier):
    for bit in bits:
        peer = partner(col, bit)
        pl.semaphore_signal(barrier, inc=1, device_id={"col": peer}, device_id_type=MESH)


class Line:
    def __init__(self, row_count, sources, outs, sems):
        self.depth = row_count // SIDES
        self.row = lax.axis_index("row")
        self.place = self.row // SIDES
        self.sources, self.outs = sources, outs
        self.up_s, self.up_r, self.dn_s, self.dn_r = sems
        self.has_up = self.place < self.depth - 1
        self.has_dn = self.place > 0

    @staticmethod
    def scratch(row_count, count):
        return [DMA((count, row_count // SIDES))] * 4

    def up(self, i, slot, d, first=False):
        src = self.sources[i] if first else self.outs[i].at[slot]
        device = {"row": self.row + SIDES}
        return remote(src, self.outs[i].at[slot], self.up_s.at[i, d], self.up_r.at[i, d], device)

    def dn(self, i, slot, d, first=False):
        src = self.sources[i] if first else self.outs[i].at[slot]
        device = {"row": self.row - SIDES}
        return remote(src, self.outs[i].at[slot], self.dn_s.at[i, d], self.dn_r.at[i, d], device)

    def has(self, way, d):
        there = self.place + d * (2 * way - 1)
        return (d >= 0) & (there >= 0) & (there < self.depth) & ((way == 0) | (d > 0))

    def start(self, i):
        @pl.when(self.has_up)
        def _():
            self.up(i, self.place, 0, True).start()

        @pl.when(self.has_dn)
        def _():
            self.dn(i, self.place, 0, True).start()

    def forward(self, d):
        for i in range(len(self.outs)):

            @pl.when(self.has(0, d))
            def _():
                self.up(i, self.place - d, d - 1).wait_recv()

                @pl.when(self.has_up)
                def _():
                    self.up(i, self.place - d, d).start()

            @pl.when(self.has(1, d))
            def _():
                self.dn(i, self.place + d, d - 1).wait_recv()

                @pl.when(self.has_dn)
                def _():
                    self.dn(i, self.place + d, d).start()

    def drain(self):
        def sent(d, carry):
            for i in range(len(self.outs)):

                @pl.when((self.place - d >= 0) & self.has_up)
                def _():
                    self.up(i, self.place - d, d).wait_send()

                @pl.when((self.place + d < self.depth) & self.has_dn)
                def _():
                    self.dn(i, self.place + d, d).wait_send()

            return carry

        lax.fori_loop(0, self.depth, sent, 0)


def project_kernel(row_count, bits, *refs):
    basis_a, basis_b, buffer_a, buffer_b, proj_a, proj_b, pair = refs[:7]
    mine, theirs, all_b, high, low, part_b, land_b = refs[7:14]
    refs = refs[14:]
    stages = len(bits) + 1
    sums, refs = list(refs[:stages]) + [proj_a], refs[stages:]
    landed, refs = refs[:stages], refs[stages:]
    sums_b, refs = refs[: len(bits)], refs[len(bits) :]
    landed_b, refs = refs[: len(bits) - 1], refs[len(bits) - 1 :]
    line_sems, refs = refs[:4], refs[4:]
    small_s, small_r, small_own, swap_s, swap_r, swap_own, sum_s, sum_r, b_s, b_r = refs
    row, col = lax.axis_index("row"), lax.axis_index("col")
    place, lane = row // SIDES, lax.rem(row, SIDES)
    other = place * SIDES + (1 - lane)
    share, width = basis_a.shape[0], mine.shape[2]
    depth = row_count // SIDES
    rank = share * row_count
    half = rank // 2
    twin, part = partner(col, 1), lax.rem(col, 2)
    devices = [{"col": partner(col, bit)} for bit in bits] + [{"row": other}]

    barrier = pltpu.get_barrier_semaphore()
    greet_row(row, row_count, barrier)
    greet_cols(col, bits, barrier)
    pl.semaphore_wait(barrier, row_count - 1 + len(bits))

    def columns(position):
        return pl.ds(pl.multiple_of(position * width, width), width)

    def small(k):
        peer = lax.rem(place + k, depth) * SIDES + lane
        return remote(basis_b, all_b.at[row], small_s.at[k], small_r.at[k], {"row": peer})

    def beside(k):
        slot = lax.rem(place + depth - k, depth) * SIDES + lane
        source = basis_b if k == 0 else all_b.at[slot]
        sems = small_s.at[depth + k], small_r.at[depth + k]
        return remote(source, all_b.at[slot], *sems, {"row": other})

    swap_basis = remote(
        basis_a.at[:, columns(1 - lane)], theirs.at[place], swap_s.at[0], swap_r.at[0], {"row": other}
    )
    swap_rows = remote(
        buffer_a.at[:, columns(1 - lane)], pair.at[lane], swap_s.at[1], swap_r.at[1], {"row": other}
    )
    own_basis = pltpu.make_async_copy(basis_a.at[:, columns(lane)], mine.at[place], swap_own.at[0])
    own_rows = pltpu.make_async_copy(buffer_a.at[:, columns(lane)], pair.at[lane], swap_own.at[1])
    small_local = pltpu.make_async_copy(basis_b, all_b.at[row], small_own)
    sources = [basis_a.at[:, columns(lane)], theirs.at[place]]
    line = Line(row_count, sources, [mine, theirs], line_sems)
    swap_basis.start()
    line.start(0)
    for k in range(1, depth):
        small(k).start()
    beside(0).start()
    swap_rows.start()
    own_basis.start()
    own_rows.start()
    small_local.start()

    def strip(place_, position):
        return pl.ds(pl.multiple_of((place_ * SIDES + position) * share, share), share)

    def summing(stage, place_):
        sems = sum_s.at[stage, place_], sum_r.at[stage, place_]
        rows = strip(place_, part if stage else 1 - part)
        here, there = sums[stage].at[rows, :], landed[stage].at[rows, :]
        return remote(here, there, *sems, devices[stage])

    def giving(place_, position):
        here = proj_a.at[strip(place_, position), :]
        return remote(here, here, sum_s.at[stages, place_], sum_r.at[stages, place_], {"col": twin})

    def compute(place_):
        blocks = jnp.concatenate([mine[place_], theirs[place_]], axis=0)
        block_high, block_low = halves(blocks)
        total = narrow_dot(block_high, low[...], LAST) + narrow_dot(block_low, high[...], LAST)
        total = total + narrow_dot(block_high, high[...], LAST)
        for k, side in enumerate((lane, 1 - lane)):
            start = (place_ * SIDES + side) * share
            sums[0][pl.ds(pl.multiple_of(start, share), share), :] = total[k * share : (k + 1) * share]
        summing(0, place_).start()

    def step(stage, place_):
        summing(stage, place_).wait_recv()
        rows = strip(place_, part)
        sums[stage + 1][rows, :] = sums[stage][rows, :] + landed[stage][rows, :]
        if stage + 1 < stages:
            summing(stage + 1, place_).start()
        else:
            giving(place_, part).start()

    begin = min(2, depth - 1)

    def progress(turn):
        for stage in range(stages):
            d = turn - stage
            for near in range(begin):
                for way in range(2):

                    @pl.when((d == begin) & line.has(way, near))
                    def _():
                        step(stage, place + near * (2 * way - 1))

            for way in range(2):

                @pl.when((d >= begin) & line.has(way, d))
                def _():
                    step(stage, place + d * (2 * way - 1))

    def half_rows(position):
        return pl.ds(pl.multiple_of(position * half, half), half)

    def scatter_b():
        return remote(part_b.at[half_rows(1 - part), :], land_b, b_s.at[0], b_r.at[0], {"col": twin})

    def exchange_b(stage):
        device = {"col": partner(col, bits[stage])}
        return remote(sums_b[stage - 1], landed_b[stage - 1], b_s.at[stage], b_r.at[stage], device)

    def return_b(position):
        rows = half_rows(position)
        index = len(bits)
        return remote(sums_b[-1], proj_b.at[rows, :], b_s.at[index], b_r.at[index], {"col": twin})

    def pass_b():
        for k in range(1, depth):
            small(k).wait_recv()
            beside(k).start()

    def begin_b():
        small_local.wait()
        for k in range(depth):
            beside(k).wait_recv()
        flat = all_b[...].reshape(rank, basis_b.shape[1])
        part_b[...] = split_dot(flat, buffer_b[...], LAST)
        scatter_b().start()

    def second_b():
        scatter_b().wait_recv()
        sums_b[0][...] = part_b[half_rows(part), :] + land_b[...]
        if len(bits) > 1:
            exchange_b(1).start()

    def finish_b():
        for stage in range(1, len(bits)):
            exchange_b(stage).wait_recv()
            sums_b[stage][...] = sums_b[stage - 1][...] + landed_b[stage - 1][...]
            if stage + 1 < len(bits):
                exchange_b(stage + 1).start()
        return_b(part).start()
        proj_b[half_rows(part), :] = sums_b[-1][...]

    swap_basis.wait_recv()
    line.start(1)

    def units(d):
        for way in range(2):

            @pl.when(line.has(way, d))
            def _():
                compute(place + d * (2 * way - 1))

    def advance(d, carry):
        line.forward(d)

        @pl.when(d == 1)
        def _():
            pass_b()
            begin_b()
            if depth > 2:
                second_b()

        @pl.when(d == begin)
        def _():
            own_basis.wait()
            own_rows.wait()
            swap_rows.wait_recv()
            high[...], low[...] = halves(pair[...].reshape(high.shape))
            if depth == 2:
                second_b()

        def catch_up(near, inner):
            units(near)
            return inner

        lax.fori_loop(jnp.where(d == begin, 0, d), jnp.where(d < begin, 0, d + 1), catch_up, 0)
        progress(d)
        return carry

    lax.fori_loop(1, depth, advance, 0)
    progress(depth)
    finish_b()
    for d in range(depth + 1, depth + stages - 1):
        progress(d)
    return_b(1 - part).wait_recv()
    swap_basis.wait_send()
    swap_rows.wait_send()
    for k in range(depth):
        beside(k).wait_send()
    for k in range(1, depth):
        small(k).wait_send()
    line.drain()

    def sent(place_, carry):
        giving(place_, 1 - part).wait_recv()
        giving(place_, part).wait_send()
        for stage in range(stages):
            summing(stage, place_).wait_send()
        return carry

    lax.fori_loop(0, depth, sent, 0)
    scatter_b().wait_send()
    for stage in range(1, len(bits)):
        exchange_b(stage).wait_send()
    return_b(part).wait_send()


def project(basis_a, basis_b, buffer_a, buffer_b):
    row_count, col_count = lax.axis_size("row"), lax.axis_size("col")
    bits = col_bits(col_count)
    stages = len(bits) + 1
    depth = row_count // SIDES
    (share, width), rows_a, rows_b = basis_a.shape, buffer_a.shape[0], buffer_b.shape[0]
    rank, width = share * row_count, width // SIDES

    def space(*shape):
        return pltpu.VMEM(shape, jnp.float32)

    narrow = pltpu.VMEM((SIDES * rows_a, width), jnp.bfloat16)
    return pl.pallas_call(
        functools.partial(project_kernel, row_count, bits),
        out_shape=[
            jax.ShapeDtypeStruct(shape, jnp.float32)
            for shape in ((rank, SIDES * rows_a), (rank, rows_b), (SIDES, rows_a, width))
        ],
        in_specs=[VMEM] * 4,
        out_specs=[VMEM] * 3,
        scratch_shapes=[
            space(depth, share, width),
            space(depth, share, width),
            space(row_count, *basis_b.shape),
            narrow,
            narrow,
            space(rank, rows_b),
            space(rank // 2, rows_b),
        ]
        + [space(rank, SIDES * rows_a)] * (2 * stages)
        + [space(rank // 2, rows_b)] * (2 * len(bits) - 1)
        + Line.scratch(row_count, 2)
        + [DMA((row_count,)), DMA((row_count,)), DMA(()), DMA((2,)), DMA((2,)), DMA((2,))]
        + [DMA((stages + 1, depth))] * 2
        + [DMA((len(bits) + 1,))] * 2,
        name="project",
        compiler_params=pltpu.CompilerParams(
            collective_id=1, has_side_effects=True, vmem_limit_bytes=60 * 2**20
        ),
    )(basis_a, basis_b, buffer_a, buffer_b)


def factor(rank, grams, outs, works, diags, between):
    eye_rows = lax.broadcasted_iota(jnp.int32, (rank, rank), 0)
    eye_cols = lax.broadcasted_iota(jnp.int32, (rank, rank), 1)
    for gram, work in zip(grams, works):
        work[:, :rank] = gram[...]
        work[:, rank:] = (eye_rows == eye_cols).astype(jnp.float32)
    rows = lax.broadcasted_iota(jnp.int32, (BLOCK, 1), 0)
    lanes = lax.broadcasted_iota(jnp.int32, (1, BLOCK), 1)
    for k in range(rank // BLOCK):
        low, high = k * BLOCK, (k + 1) * BLOCK
        for work, diag in zip(works, diags):
            diag[:, :BLOCK] = work[low:high, low:high]
            diag[:, BLOCK:] = (rows == lanes).astype(jnp.float32)

        def step(base, i, carry):
            j = PIVOTS * i
            for diag in diags:
                square = diag[base:, :BLOCK]
                tops = [diag[pl.ds(j + p, 1), :] for p in range(PIVOTS)]

                def pick(some, p):
                    kept = jnp.where(lanes == j + p, some[:, :BLOCK], 0.0)
                    return jnp.sum(kept, axis=1, keepdims=True)

                cols = [pick(square, p) for p in range(PIVOTS)]
                cells = [[pick(top, p) for p in range(PIVOTS)] for top in tops]
                total = diag[base:, :]
                for p in range(PIVOTS):
                    scale = 1.0 / cells[p][p]
                    weights = jnp.where(rows[base:] > j + p, cols[p] * scale, 0.0)
                    for q in range(p + 1, PIVOTS):
                        ratio = cells[q][p] * scale
                        tops[q] = tops[q] - ratio * tops[p]
                        cols[q] = cols[q] - weights * cells[p][q]
                        cells[q] = [cells[q][r] - ratio * cells[p][r] for r in range(PIVOTS)]
                    total = total - weights * tops[p]
                diag[base:, :] = total
            return carry

        for piece in range(PIECES):
            steps = BLOCK // PIVOTS // PIECES
            some = functools.partial(step, piece * BLOCK // PIECES)
            lax.fori_loop(piece * steps, (piece + 1) * steps, some, 0)
            if piece + 1 < PIECES:
                between()
        width = slice(low, rank + high)
        for work, diag in zip(works, diags):
            pivots = jnp.sum(
                jnp.where(rows == lanes, diag[:, :BLOCK], 0.0), axis=1, keepdims=True
            )
            inverse = diag[:, BLOCK:] * (1.0 / jnp.sqrt(pivots))
            panel = dot(inverse, work[low:high, width])
            work[low:high, width] = panel
            if high < rank:
                factors = panel[:, BLOCK : rank - low]
                work[high:, width] = work[high:, width] - dot(factors, panel, FIRST)
        between()
    for work, out in zip(works, outs):
        out[...] = work[:, rank:]


class Reduce:
    def __init__(self, row_count, sems):
        depth = row_count // SIDES
        row = lax.axis_index("row")
        place, lane = row // SIDES, lax.rem(row, SIDES)
        lower = place < depth // 2
        self.place, self.lane, self.depth = place, lane, depth
        self.other = place * SIDES + (1 - lane)
        toward = jnp.where(lower, SIDES, -SIDES)
        self.inner, self.outer = {"row": row + toward}, {"row": row - toward}
        self.steps = jnp.where(lower, depth // 2 - 1 - place, place - depth // 2)
        self.middle = self.steps == 0
        self.has_outer = self.steps < depth // 2 - 1
        self.sems = sems

    @staticmethod
    def scratch(count):
        return [DMA((count,))] * 6

    def inward(self, i, part, arrive):
        return remote(part, arrive, self.sems[0].at[i], self.sems[1].at[i], self.inner)

    def swap(self, i, part, meet):
        return remote(part, meet, self.sems[2].at[i], self.sems[3].at[i], self.inner)

    def outward(self, i, final):
        return remote(final, final, self.sems[4].at[i], self.sems[5].at[i], self.outer)

    def gather(self, i, part, arrive, meet):
        @pl.when(self.has_outer)
        def _():
            self.inward(i, part, arrive).wait_recv()
            part[...] = part[...] + arrive[...]

        @pl.when(self.middle)
        def _():
            self.swap(i, part, meet).start()

        @pl.when(self.steps > 0)
        def _():
            self.inward(i, part, arrive).start()

    def spread(self, i, part, meet, final):
        @pl.when(self.middle)
        def _():
            self.swap(i, part, meet).wait_recv()
            final[...] = part[...] + meet[...]

        @pl.when(self.steps > 0)
        def _():
            self.outward(i, final).wait_recv()

        @pl.when(self.has_outer)
        def _():
            self.outward(i, final).start()

    def drain(self, i, part, arrive, meet, final):
        @pl.when(self.middle)
        def _():
            self.swap(i, part, meet).wait_send()

        @pl.when(self.steps > 0)
        def _():
            self.inward(i, part, arrive).wait_send()

        @pl.when(self.has_outer)
        def _():
            self.outward(i, final).wait_send()


def products_kernel(row_count, col_count, rank, joined, scales, *refs):
    proj_a, proj_b, pair, buffer_b = refs[:4]
    trans_a, trans_b, basis_a, basis_b, ortho_a, ortho_b, scaled_a, scaled_b = refs[4:12]
    part_w, arrive_w, meet_w, final_w, other_w = refs[12:17]
    part_v, arrive_v, meet_v, final_v, land_v, other_v, whole_v = refs[17:24]
    piece_a, piece_b = refs[24:28], refs[28:32]
    cast_b, land_b, gram_a, gram_b, inv_a, inv_b, high_a, low_a = refs[32:40]
    rows_a, wide_a, wide_b, full_a, full_b, square_a, square_b, mine, theirs = refs[40:49]
    works, diags = refs[49:51], refs[51:53]
    reduce_sems, refs = refs[53:59], refs[59:]
    side_s, side_r, give_s, give_r, gram_s, gram_r, sq_s, sq_r = refs
    row, col = lax.axis_index("row"), lax.axis_index("col")
    line = Reduce(row_count, reduce_sems)
    lane, place, other = line.lane, line.place, line.other
    share, half = rank // row_count, rank // 2
    peers = SIDES * col_count
    piece = rank // peers
    index = lane * col_count + col
    chunks = part_w.shape[0]
    width = part_w.shape[2]

    def peer_of(k):
        target = lax.rem(index + k, peers)
        return (place * SIDES + target // col_count, lax.rem(target, col_count))

    barrier = pltpu.get_barrier_semaphore()

    pl.semaphore_signal(barrier, inc=1, device_id=line.inner, device_id_type=MESH)
    for k in range(1, peers):
        pl.semaphore_signal(barrier, inc=1, device_id=peer_of(k), device_id_type=MESH)

    @pl.when(line.has_outer)
    def _():
        pl.semaphore_signal(barrier, inc=1, device_id=line.outer, device_id_type=MESH)
        pl.semaphore_wait(barrier, peers + 1)

    @pl.when(jnp.logical_not(line.has_outer))
    def _():
        pl.semaphore_wait(barrier, peers)

    def rows_of(position, size):
        return pl.ds(pl.multiple_of(position * size, size), size)

    def give_g():
        return remote(cast_b, land_b, give_s.at[0], give_r.at[0], {"row": other})

    def give_v():
        there = whole_v.at[rows_of(1 - lane, half), :]
        return remote(there, land_v, give_s.at[1], give_r.at[1], {"row": other})

    bits = col_bits(col_count)[::-1]

    def held(stage):
        columns = [col]
        for bit in bits[: max(stage - 1, 0)]:
            columns += [partner(c, bit) for c in columns]
        sides = [lane] if stage == 0 else [lane, 1 - lane]
        return [side * col_count + c for side in sides for c in columns]

    def grams(stage):
        device = {"row": other} if stage == 0 else {"col": partner(col, bits[stage - 1])}
        copies = []
        for k, position in enumerate(held(stage)):
            for which, gram in enumerate((gram_a, gram_b)):
                here = gram.at[rows_of(position, piece), :]
                sems = gram_s.at[which, stage, k], gram_r.at[which, stage, k]
                copies.append(remote(here, here, *sems, device))
        return copies

    def send_grams(stage):
        for copy in grams(stage):
            copy.start()

    def await_grams(stage):
        for copy in grams(stage):
            copy.wait_recv()

    def aside(i, final, target):
        return remote(final, target, side_s.at[i], side_r.at[i], {"row": other})

    unit_v = (part_v, arrive_v, meet_v, final_v)

    def unit_w(k):
        return part_w.at[k], arrive_w.at[k], meet_w.at[k], final_w.at[k]

    def gather(i, unit):
        line.gather(i, unit[0], unit[1], unit[2])

    def spread(i, unit):
        line.spread(i, unit[0], unit[2], unit[3])

    theirs_index = (1 - lane) * col_count + col
    cast_b[...] = dot(proj_b[rows_of(theirs_index, piece), :], proj_b[...], LAST)
    give_g().start()
    rows_high, rows_low = halves(proj_a[...])

    def multiply(k):
        columns = slice(k * width, (k + 1) * width)
        block = pair[:, :, columns].reshape(proj_a.shape[1], width)
        block_high, block_low = halves(block)
        total = narrow_dot(rows_high, block_low) + narrow_dot(rows_low, block_high)
        part_w[k] = total + narrow_dot(rows_high, block_high)

    def take(k):
        gather(3 + k, unit_w(k))

    def hand(k):
        spread(3 + k, unit_w(k))
        aside(1 + k, final_w.at[k], other_w.at[k]).start()

    def take_v():
        give_v().wait_recv()
        part_v[...] = whole_v[rows_of(lane, half), :] + land_v[...]
        gather(2, unit_v)

    def hand_v():
        spread(2, unit_v)
        aside(0, final_v, other_v).start()

    def later_take(k):
        @pl.when(line.has_outer)
        def _():
            take(k)

    def later_take_v():
        @pl.when(line.has_outer)
        def _():
            take_v()

    early = jnp.logical_not(line.has_outer)
    piece_a[0][...] = dot(proj_a[rows_of(index, piece), :], proj_a[...], LAST)
    gather(0, piece_a)

    def produce(k):
        multiply(k)

        @pl.when(early)
        def _():
            take(k)

    ahead = min(3, chunks)
    produce(0)
    piece_b[0][...] = dot(proj_b[rows_of(index, piece), :], proj_b[...], LAST)
    give_g().wait_recv()
    piece_b[0][...] = piece_b[0][...] + land_b[...]
    gather(1, piece_b)
    for k in range(1, ahead):
        produce(k)
    for which, unit in enumerate((piece_a, piece_b)):
        spread(which, unit)
    gram_a[rows_of(index, piece), :] = piece_a[3][...]
    gram_b[rows_of(index, piece), :] = piece_b[3][...]
    send_grams(0)
    whole_v[...] = split_dot(proj_b[...], buffer_b[...])
    give_v().start()
    if ahead < chunks:
        produce(ahead)
    await_grams(0)
    send_grams(1)

    @pl.when(early)
    def _():
        take_v()

    later_take(0)
    for k in range(ahead + 1, chunks):
        produce(k)

    tasks = []
    for k in range(chunks):
        if k > 0:
            tasks.append(functools.partial(later_take, k))
            tasks.append(functools.partial(hand, k - 1))
        if k == min(3, chunks - 1):
            tasks.append(later_take_v)
        if k == min(4, chunks - 1):
            tasks.append(hand_v)
    tasks.append(functools.partial(hand, chunks - 1))
    for stage in range(1, len(bits) + 1):
        for _ in range(min(2, len(tasks))):
            tasks.pop(0)()
        await_grams(stage)
        if stage < len(bits):
            send_grams(stage + 1)
    slots = rank // BLOCK * PIECES
    done = [0, 0]

    def between():
        done[0] += 1
        goal = -(-len(tasks) * done[0] // slots)
        while done[1] < min(goal, len(tasks)):
            tasks[done[1]]()
            done[1] += 1

    factor(rank, [gram_a, gram_b], [inv_a, inv_b], works, diags, between)
    high_a[...], low_a[...] = halves(inv_a[...])
    rows_a[...] = proj_a[...].T
    count_a = rows_a.shape[0] // SIDES
    wide_a[...] = split_dot(rows_a[rows_of(lane, count_a), :], inv_a[...], LAST)
    wide_b[...] = split_dot(proj_b[...].T, inv_b[...], LAST)
    ortho_a[...] = wide_a[...].astype(jnp.bfloat16)
    ortho_b[...] = wide_b[...].astype(jnp.bfloat16)
    square_a[...] = jnp.zeros_like(square_a)
    own = rows_of(row, share)

    def use(product, position):
        product_high, product_low = halves(product)
        total = narrow_dot(high_a[...], product_low) + narrow_dot(low_a[...], product_high)
        total = total + narrow_dot(high_a[...], product_high)
        full_a[...] = total
        trans_a[position] = total.astype(jnp.bfloat16)
        square_a[...] += jnp.sum(total * total, axis=1, keepdims=True)
        basis_a[position] = full_a[own, :]

    groups = chunks // joined

    def group(source, k):
        return jnp.concatenate([source[k * joined + i] for i in range(joined)], axis=1)

    def near(k, carry):
        use(group(final_w, k), lane * groups + k)
        return carry

    def far(k, carry):
        for i in range(joined):
            j = k * joined + i
            aside(1 + j, final_w.at[j], other_w.at[j]).wait_recv()
        use(group(other_w, k), (1 - lane) * groups + k)
        return carry

    lax.fori_loop(0, groups, near, 0)
    aside(0, final_v, other_v).wait_recv()
    whole_v[rows_of(lane, half), :] = final_v[...]
    give_v().wait_send()
    whole_v[rows_of(1 - lane, half), :] = other_v[...]
    total_b = split_dot(inv_b[...], whole_v[...])
    full_b[...] = total_b
    trans_b[...] = total_b.astype(jnp.bfloat16)
    square_b[...] = jnp.sum(total_b * total_b, axis=1, keepdims=True)
    lax.fori_loop(0, groups, far, 0)

    def across(column):
        return jnp.broadcast_to(column, (rank, BLOCK)).T[:8]

    def norms(k):
        peer = lax.rem(col + k, col_count)
        return remote(mine, theirs.at[col], sq_s.at[k], sq_r.at[k], {"col": peer})

    mine[0] = across(square_a[...])
    mine[1] = across(square_b[...])
    for k in range(1, col_count):
        norms(k).start()
    theirs[col] = mine[...]
    for k in range(1, col_count):
        norms(k).wait_recv()
    norm = jnp.sqrt(jnp.sum(theirs[...], axis=0) + EPS)
    norm_a, norm_b = norm[0, :1], norm[1, :1]
    scaled_a[...] = (wide_a[...] * (scales[0] / norm_a)).astype(jnp.bfloat16)
    scaled_b[...] = (wide_b[...] * (scales[1] / norm_b)).astype(jnp.bfloat16)
    ranks = lax.broadcasted_iota(jnp.int32, (share, rank), 1)
    owned = lax.broadcasted_iota(jnp.int32, (share, rank), 0) + row * share
    own_a = jnp.sum(jnp.where(ranks == owned, norm_a, 0.0), axis=1, keepdims=True)
    own_b = jnp.sum(jnp.where(ranks == owned, norm_b, 0.0), axis=1, keepdims=True)
    for k in range(basis_a.shape[0]):
        basis_a[k] = basis_a[k] / own_a
    basis_b[...] = full_b[own, :] / own_b
    for k in range(1, col_count):
        norms(k).wait_send()
    for stage in range(len(bits) + 1):
        for copy in grams(stage):
            copy.wait_send()
    give_g().wait_send()
    aside(0, final_v, other_v).wait_send()
    for i, unit in enumerate((piece_a, piece_b, unit_v)):
        line.drain(i, *unit)

    def sent(k, carry):
        aside(1 + k, final_w.at[k], other_w.at[k]).wait_send()
        line.drain(3 + k, *unit_w(k))
        return carry

    lax.fori_loop(0, chunks, sent, 0)


def products(proj_a, proj_b, pair, buffer_b, scales):
    row_count, col_count = lax.axis_size("row"), lax.axis_size("col")
    rank = proj_a.shape[0]
    share, half, piece = rank // row_count, rank // 2, rank // (SIDES * col_count)
    side_width = pair.shape[2]
    chunk = CHUNK if side_width % CHUNK == 0 else side_width
    chunks = side_width // chunk
    joined = 2 if chunks % 2 == 0 else 1
    groups, wide_chunk = chunks // joined, chunk * joined
    width_b = buffer_b.shape[1]
    rows_a, rows_b = pair.shape[1], buffer_b.shape[0]

    def array(kind, *shape):
        return jax.ShapeDtypeStruct(shape, kind)

    def space(*shape):
        return pltpu.VMEM(shape, jnp.float32)

    narrow, wide = jnp.bfloat16, jnp.float32
    grams = DMA((2, len(col_bits(col_count)) + 1, SIDES * col_count))
    cols = DMA((col_count,))
    return pl.pallas_call(
        functools.partial(products_kernel, row_count, col_count, rank, joined, scales),
        out_shape=[
            array(narrow, SIDES * groups, rank, wide_chunk),
            array(narrow, rank, width_b),
            array(wide, SIDES * groups, share, wide_chunk),
            array(wide, share, width_b),
            array(narrow, rows_a, rank),
            array(narrow, rows_b, rank),
            array(narrow, rows_a, rank),
            array(narrow, rows_b, rank),
        ],
        in_specs=[VMEM] * 4,
        out_specs=[VMEM] * 8,
        scratch_shapes=[space(chunks, rank, chunk)] * 5
        + [space(half, width_b)] * 6
        + [space(rank, width_b)]
        + [space(piece, rank)] * 10
        + [space(rank, rank)] * 4
        + [pltpu.VMEM((rank, rank), narrow)] * 2
        + [
            space(SIDES * rows_a, rank),
            space(rows_a, rank),
            space(rows_b, rank),
            space(rank, wide_chunk),
            space(rank, width_b),
            space(rank, 1),
            space(rank, 1),
            space(2, 8, rank),
            space(col_count, 2, 8, rank),
        ]
        + [space(rank, 2 * rank)] * 2
        + [space(BLOCK, 2 * BLOCK)] * 2
        + Reduce.scratch(3 + chunks)
        + [DMA((1 + chunks,))] * 2
        + [DMA((2,))] * 2
        + [grams, grams, cols, cols],
        name="products",
        compiler_params=pltpu.CompilerParams(
            collective_id=2, has_side_effects=True, vmem_limit_bytes=62 * 2**20
        ),
    )(proj_a, proj_b, pair, buffer_b)


def ending_kernel(slabs, *refs):
    buffer_a, trans_a, basis_a, ortho_a, scaled_a = refs[:5]
    buffer_b, trans_b, ortho_b, scaled_b = refs[5:9]
    mom_a, update_a, new_a, mom_b, update_b = refs[9:]
    width = trans_a.shape[2]
    for k in range(trans_a.shape[0]):
        columns = slice(k * width, (k + 1) * width)
        change = narrow_dot(ortho_a[...], trans_a[k])
        mom_a[:, columns] = buffer_a[:, columns] - (1.0 - MU) * change
        update_a[:, columns] = narrow_dot(scaled_a[...], trans_a[k]).astype(jnp.bfloat16)
        new_a[:, columns] = basis_a[k]

    @pl.when(pl.program_id(0) < slabs)
    def _():
        mom_b[...] = buffer_b[...] - (1.0 - MU) * narrow_dot(ortho_b[...], trans_b[...])
        update_b[...] = narrow_dot(scaled_b[...], trans_b[...]).astype(jnp.bfloat16)


def ending(buffer_a, trans_a, basis_a, ortho_a, scaled_a, buffer_b, trans_b, ortho_b, scaled_b):
    steps, rank, width = trans_a.shape
    rows_a, rows_b, share = buffer_a.shape[0], buffer_b.shape[0], basis_a.shape[1]
    slabs = 4
    if width % 128 or rows_b % (16 * slabs) or steps % 2 or steps < 2 * slabs:
        flat = trans_a.swapaxes(0, 1).reshape(rank, -1)
        return (
            buffer_a - (1.0 - MU) * narrow_dot(ortho_a, flat),
            narrow_dot(scaled_a, flat).astype(jnp.bfloat16),
            basis_a.swapaxes(0, 1).reshape(share, -1),
            buffer_b - (1.0 - MU) * narrow_dot(ortho_b, trans_b),
            narrow_dot(scaled_b, trans_b).astype(jnp.bfloat16),
        )
    some = rows_b // slabs
    cut = pl.BlockSpec((rows_a, 2 * width), lambda j: (0, j))
    stack = pl.BlockSpec((2, rank, width), lambda j: (j, 0, 0))
    thin = pl.BlockSpec((2, share, width), lambda j: (j, 0, 0))
    fixed_a = pl.BlockSpec((rows_a, rank), lambda j: (0, 0))
    fixed_b = pl.BlockSpec(trans_b.shape, lambda j: (0, 0))
    slab = pl.BlockSpec((some, buffer_b.shape[1]), lambda j: (jnp.minimum(j, slabs - 1), 0))
    rows = pl.BlockSpec((some, rank), lambda j: (jnp.minimum(j, slabs - 1), 0))
    return pl.pallas_call(
        functools.partial(ending_kernel, slabs),
        grid=(steps // 2,),
        out_shape=[
            jax.ShapeDtypeStruct(buffer_a.shape, jnp.float32),
            jax.ShapeDtypeStruct(buffer_a.shape, jnp.bfloat16),
            jax.ShapeDtypeStruct((share, buffer_a.shape[1]), jnp.float32),
            jax.ShapeDtypeStruct(buffer_b.shape, jnp.float32),
            jax.ShapeDtypeStruct(buffer_b.shape, jnp.bfloat16),
        ],
        in_specs=[cut, stack, thin, fixed_a, fixed_a, slab, fixed_b, rows, rows],
        out_specs=[cut, cut, pl.BlockSpec((share, 2 * width), lambda j: (0, j)), slab, slab],
        name="ending",
    )(buffer_a, trans_a, basis_a, ortho_a, scaled_a, buffer_b, trans_b, ortho_b, scaled_b)


def shards(mom_a, grad_a, basis_a, mom_b, grad_b, basis_b):
    row_count = lax.axis_size("row")
    buffer_a, buffer_b = MU * mom_a + grad_a, MU * mom_b + grad_b
    proj_a, proj_b, pair = project(basis_a, basis_b, buffer_a, buffer_b)
    rank = proj_a.shape[0]
    scales = [
        math.sqrt(x.shape[0] * x.shape[1] * row_count * lax.axis_size("col") / rank)
        for x in (buffer_a, buffer_b)
    ]
    trans_a, trans_b, basis_a, basis_b, ortho_a, ortho_b, scaled_a, scaled_b = products(
        proj_a, proj_b, pair, buffer_b, scales
    )
    new_mom_a, update_a, new_basis_a, new_mom_b, update_b = ending(
        buffer_a, trans_a, basis_a, ortho_a, scaled_a, buffer_b, trans_b, ortho_b, scaled_b
    )
    return new_mom_a, update_a, new_basis_a, new_mom_b, update_b, basis_b


def solution(mesh):
    spec = P("row", "col")
    return jax.shard_map(
        shards, mesh=mesh, in_specs=(spec,) * 6, out_specs=(spec,) * 6, check_vma=False
    )
```

```python
import functools
import math

import jax
import jax.numpy as jnp
from jax import lax
from jax.experimental import pallas as pl
from jax.experimental.pallas import tpu as pltpu
from jax.sharding import PartitionSpec as P

MU = 0.95
EPS = 1e-06
BLOCK = 128
HIGHEST = lax.Precision.HIGHEST
MESH = pl.DeviceIdType.MESH
VMEM = pl.BlockSpec(memory_space=pltpu.VMEM)
DMA = pltpu.SemaphoreType.DMA
LAST = ((1,), (1,))
FIRST = ((0,), (0,))
PLAIN = ((1,), (0,))
SIDES = 2
PIECES = 4
PIVOTS = 4
CHUNK = 128


def dot(x, y, contract=PLAIN, precision=HIGHEST):
    return lax.dot_general(
        x, y, (contract, ((), ())), precision=precision, preferred_element_type=jnp.float32
    )


def halves(x):
    high = x.astype(jnp.bfloat16)
    return high, (x - high.astype(jnp.float32)).astype(jnp.bfloat16)


def narrow_dot(x, y, contract=PLAIN):
    return lax.dot_general(x, y, (contract, ((), ())), preferred_element_type=jnp.float32)


def split_dot(x, y, contract=PLAIN):
    (x_high, x_low), (y_high, y_low) = halves(x), halves(y)
    total = narrow_dot(x_high, y_low, contract) + narrow_dot(x_low, y_high, contract)
    return total + narrow_dot(x_high, y_high, contract)


def remote(src, dst, send, recv, device):
    return pltpu.make_async_remote_copy(
        src_ref=src,
        dst_ref=dst,
        send_sem=send,
        recv_sem=recv,
        device_id=device,
        device_id_type=MESH,
    )


def partner(position, bit):
    return position + bit - 2 * bit * lax.rem(position // bit, 2)


def col_bits(col_count):
    bits, bit = [], 1
    while bit < col_count:
        bits.append(bit)
        bit *= 2
    return bits


def greet_row(row, row_count, barrier):
    for k in range(1, row_count):
        peer = lax.rem(row + k, row_count)
        pl.semaphore_signal(barrier, inc=1, device_id={"row": peer}, device_id_type=MESH)


def greet_cols(col, bits, barrier):
    for bit in bits:
        peer = partner(col, bit)
        pl.semaphore_signal(barrier, inc=1, device_id={"col": peer}, device_id_type=MESH)


class Line:
    def __init__(self, row_count, sources, outs, sems):
        self.depth = row_count // SIDES
        self.row = lax.axis_index("row")
        self.place = self.row // SIDES
        self.sources, self.outs = sources, outs
        self.up_s, self.up_r, self.dn_s, self.dn_r = sems
        self.has_up = self.place < self.depth - 1
        self.has_dn = self.place > 0

    @staticmethod
    def scratch(row_count, count):
        return [DMA((count, row_count // SIDES))] * 4

    def up(self, i, slot, d, first=False):
        src = self.sources[i] if first else self.outs[i].at[slot]
        device = {"row": self.row + SIDES}
        return remote(src, self.outs[i].at[slot], self.up_s.at[i, d], self.up_r.at[i, d], device)

    def dn(self, i, slot, d, first=False):
        src = self.sources[i] if first else self.outs[i].at[slot]
        device = {"row": self.row - SIDES}
        return remote(src, self.outs[i].at[slot], self.dn_s.at[i, d], self.dn_r.at[i, d], device)

    def has(self, way, d):
        there = self.place + d * (2 * way - 1)
        return (d >= 0) & (there >= 0) & (there < self.depth) & ((way == 0) | (d > 0))

    def start(self, i):
        @pl.when(self.has_up)
        def _():
            self.up(i, self.place, 0, True).start()

        @pl.when(self.has_dn)
        def _():
            self.dn(i, self.place, 0, True).start()

    def forward(self, d):
        for i in range(len(self.outs)):

            @pl.when(self.has(0, d))
            def _():
                self.up(i, self.place - d, d - 1).wait_recv()

                @pl.when(self.has_up)
                def _():
                    self.up(i, self.place - d, d).start()

            @pl.when(self.has(1, d))
            def _():
                self.dn(i, self.place + d, d - 1).wait_recv()

                @pl.when(self.has_dn)
                def _():
                    self.dn(i, self.place + d, d).start()

    def drain(self):
        def sent(d, carry):
            for i in range(len(self.outs)):

                @pl.when((self.place - d >= 0) & self.has_up)
                def _():
                    self.up(i, self.place - d, d).wait_send()

                @pl.when((self.place + d < self.depth) & self.has_dn)
                def _():
                    self.dn(i, self.place + d, d).wait_send()

            return carry

        lax.fori_loop(0, self.depth, sent, 0)


def project_kernel(row_count, bits, *refs):
    basis_a, basis_b, buffer_a, buffer_b, proj_a, proj_b, pair = refs[:7]
    mine, theirs, all_b, high, low, part_b, land_b = refs[7:14]
    refs = refs[14:]
    stages = len(bits) + 1
    sums, refs = list(refs[:stages]) + [proj_a], refs[stages:]
    landed, refs = refs[:stages], refs[stages:]
    sums_b, refs = refs[: len(bits)], refs[len(bits) :]
    landed_b, refs = refs[: len(bits) - 1], refs[len(bits) - 1 :]
    line_sems, refs = refs[:4], refs[4:]
    small_s, small_r, small_own, swap_s, swap_r, swap_own, sum_s, sum_r, b_s, b_r = refs
    row, col = lax.axis_index("row"), lax.axis_index("col")
    place, lane = row // SIDES, lax.rem(row, SIDES)
    other = place * SIDES + (1 - lane)
    share, width = basis_a.shape[0], mine.shape[2]
    depth = row_count // SIDES
    rank = share * row_count
    half = rank // 2
    twin, part = partner(col, 1), lax.rem(col, 2)
    devices = [{"col": partner(col, bit)} for bit in bits] + [{"row": other}]

    barrier = pltpu.get_barrier_semaphore()
    greet_row(row, row_count, barrier)
    greet_cols(col, bits, barrier)
    pl.semaphore_wait(barrier, row_count - 1 + len(bits))

    def columns(position):
        return pl.ds(pl.multiple_of(position * width, width), width)

    def small(k):
        peer = lax.rem(place + k, depth) * SIDES + lane
        return remote(basis_b, all_b.at[row], small_s.at[k], small_r.at[k], {"row": peer})

    def beside(k):
        slot = lax.rem(place + depth - k, depth) * SIDES + lane
        source = basis_b if k == 0 else all_b.at[slot]
        sems = small_s.at[depth + k], small_r.at[depth + k]
        return remote(source, all_b.at[slot], *sems, {"row": other})

    swap_basis = remote(
        basis_a.at[:, columns(1 - lane)], theirs.at[place], swap_s.at[0], swap_r.at[0], {"row": other}
    )
    swap_rows = remote(
        buffer_a.at[:, columns(1 - lane)], pair.at[lane], swap_s.at[1], swap_r.at[1], {"row": other}
    )
    own_basis = pltpu.make_async_copy(basis_a.at[:, columns(lane)], mine.at[place], swap_own.at[0])
    own_rows = pltpu.make_async_copy(buffer_a.at[:, columns(lane)], pair.at[lane], swap_own.at[1])
    small_local = pltpu.make_async_copy(basis_b, all_b.at[row], small_own)
    sources = [basis_a.at[:, columns(lane)], theirs.at[place]]
    line = Line(row_count, sources, [mine, theirs], line_sems)
    swap_basis.start()
    line.start(0)
    for k in range(1, depth):
        small(k).start()
    beside(0).start()
    swap_rows.start()
    own_basis.start()
    own_rows.start()
    small_local.start()

    def strip(place_, position):
        return pl.ds(pl.multiple_of((place_ * SIDES + position) * share, share), share)

    def summing(stage, place_):
        sems = sum_s.at[stage, place_], sum_r.at[stage, place_]
        rows = strip(place_, part if stage else 1 - part)
        here, there = sums[stage].at[rows, :], landed[stage].at[rows, :]
        return remote(here, there, *sems, devices[stage])

    def giving(place_, position):
        here = proj_a.at[strip(place_, position), :]
        return remote(here, here, sum_s.at[stages, place_], sum_r.at[stages, place_], {"col": twin})

    def compute(place_):
        blocks = jnp.concatenate([mine[place_], theirs[place_]], axis=0)
        block_high, block_low = halves(blocks)
        total = narrow_dot(block_high, low[...], LAST) + narrow_dot(block_low, high[...], LAST)
        total = total + narrow_dot(block_high, high[...], LAST)
        for k, side in enumerate((lane, 1 - lane)):
            start = (place_ * SIDES + side) * share
            sums[0][pl.ds(pl.multiple_of(start, share), share), :] = total[k * share : (k + 1) * share]
        summing(0, place_).start()

    def step(stage, place_):
        summing(stage, place_).wait_recv()
        rows = strip(place_, part)
        sums[stage + 1][rows, :] = sums[stage][rows, :] + landed[stage][rows, :]
        if stage + 1 < stages:
            summing(stage + 1, place_).start()
        else:
            giving(place_, part).start()

    begin = min(2, depth - 1)

    def progress(turn):
        for stage in range(stages):
            d = turn - stage
            for near in range(begin):
                for way in range(2):

                    @pl.when((d == begin) & line.has(way, near))
                    def _():
                        step(stage, place + near * (2 * way - 1))

            for way in range(2):

                @pl.when((d >= begin) & line.has(way, d))
                def _():
                    step(stage, place + d * (2 * way - 1))

    def half_rows(position):
        return pl.ds(pl.multiple_of(position * half, half), half)

    def scatter_b():
        return remote(part_b.at[half_rows(1 - part), :], land_b, b_s.at[0], b_r.at[0], {"col": twin})

    def exchange_b(stage):
        device = {"col": partner(col, bits[stage])}
        return remote(sums_b[stage - 1], landed_b[stage - 1], b_s.at[stage], b_r.at[stage], device)

    def return_b(position):
        rows = half_rows(position)
        index = len(bits)
        return remote(sums_b[-1], proj_b.at[rows, :], b_s.at[index], b_r.at[index], {"col": twin})

    def pass_b():
        for k in range(1, depth):
            small(k).wait_recv()
            beside(k).start()

    def begin_b():
        small_local.wait()
        for k in range(depth):
            beside(k).wait_recv()
        flat = all_b[...].reshape(rank, basis_b.shape[1])
        part_b[...] = split_dot(flat, buffer_b[...], LAST)
        scatter_b().start()

    def second_b():
        scatter_b().wait_recv()
        sums_b[0][...] = part_b[half_rows(part), :] + land_b[...]
        if len(bits) > 1:
            exchange_b(1).start()

    def finish_b():
        for stage in range(1, len(bits)):
            exchange_b(stage).wait_recv()
            sums_b[stage][...] = sums_b[stage - 1][...] + landed_b[stage - 1][...]
            if stage + 1 < len(bits):
                exchange_b(stage + 1).start()
        return_b(part).start()
        proj_b[half_rows(part), :] = sums_b[-1][...]

    swap_basis.wait_recv()
    line.start(1)

    def units(d):
        for way in range(2):

            @pl.when(line.has(way, d))
            def _():
                compute(place + d * (2 * way - 1))

    def advance(d, carry):
        line.forward(d)

        @pl.when(d == 1)
        def _():
            pass_b()
            begin_b()
            if depth > 2:
                second_b()

        @pl.when(d == begin)
        def _():
            own_basis.wait()
            own_rows.wait()
            swap_rows.wait_recv()
            high[...], low[...] = halves(pair[...].reshape(high.shape))
            if depth == 2:
                second_b()

        def catch_up(near, inner):
            units(near)
            return inner

        lax.fori_loop(jnp.where(d == begin, 0, d), jnp.where(d < begin, 0, d + 1), catch_up, 0)
        progress(d)
        return carry

    lax.fori_loop(1, depth, advance, 0)
    progress(depth)
    finish_b()
    for d in range(depth + 1, depth + stages - 1):
        progress(d)
    return_b(1 - part).wait_recv()
    swap_basis.wait_send()
    swap_rows.wait_send()
    for k in range(depth):
        beside(k).wait_send()
    for k in range(1, depth):
        small(k).wait_send()
    line.drain()

    def sent(place_, carry):
        giving(place_, 1 - part).wait_recv()
        giving(place_, part).wait_send()
        for stage in range(stages):
            summing(stage, place_).wait_send()
        return carry

    lax.fori_loop(0, depth, sent, 0)
    scatter_b().wait_send()
    for stage in range(1, len(bits)):
        exchange_b(stage).wait_send()
    return_b(part).wait_send()


def project(basis_a, basis_b, buffer_a, buffer_b):
    row_count, col_count = lax.axis_size("row"), lax.axis_size("col")
    bits = col_bits(col_count)
    stages = len(bits) + 1
    depth = row_count // SIDES
    (share, width), rows_a, rows_b = basis_a.shape, buffer_a.shape[0], buffer_b.shape[0]
    rank, width = share * row_count, width // SIDES

    def space(*shape):
        return pltpu.VMEM(shape, jnp.float32)

    narrow = pltpu.VMEM((SIDES * rows_a, width), jnp.bfloat16)
    return pl.pallas_call(
        functools.partial(project_kernel, row_count, bits),
        out_shape=[
            jax.ShapeDtypeStruct(shape, jnp.float32)
            for shape in ((rank, SIDES * rows_a), (rank, rows_b), (SIDES, rows_a, width))
        ],
        in_specs=[VMEM] * 4,
        out_specs=[VMEM] * 3,
        scratch_shapes=[
            space(depth, share, width),
            space(depth, share, width),
            space(row_count, *basis_b.shape),
            narrow,
            narrow,
            space(rank, rows_b),
            space(rank // 2, rows_b),
        ]
        + [space(rank, SIDES * rows_a)] * (2 * stages)
        + [space(rank // 2, rows_b)] * (2 * len(bits) - 1)
        + Line.scratch(row_count, 2)
        + [DMA((row_count,)), DMA((row_count,)), DMA(()), DMA((2,)), DMA((2,)), DMA((2,))]
        + [DMA((stages + 1, depth))] * 2
        + [DMA((len(bits) + 1,))] * 2,
        name="project",
        compiler_params=pltpu.CompilerParams(
            collective_id=1, has_side_effects=True, vmem_limit_bytes=60 * 2**20
        ),
    )(basis_a, basis_b, buffer_a, buffer_b)


def factor(rank, grams, outs, works, diags, between):
    eye_rows = lax.broadcasted_iota(jnp.int32, (rank, rank), 0)
    eye_cols = lax.broadcasted_iota(jnp.int32, (rank, rank), 1)
    for gram, work in zip(grams, works):
        work[:, :rank] = gram[...]
        work[:, rank:] = (eye_rows == eye_cols).astype(jnp.float32)
    rows = lax.broadcasted_iota(jnp.int32, (BLOCK, 1), 0)
    lanes = lax.broadcasted_iota(jnp.int32, (1, BLOCK), 1)
    for k in range(rank // BLOCK):
        low, high = k * BLOCK, (k + 1) * BLOCK
        for work, diag in zip(works, diags):
            diag[:, :BLOCK] = work[low:high, low:high]
            diag[:, BLOCK:] = (rows == lanes).astype(jnp.float32)

        def step(base, i, carry):
            j = PIVOTS * i
            for diag in diags:
                square = diag[base:, :BLOCK]
                tops = [diag[pl.ds(j + p, 1), :] for p in range(PIVOTS)]

                def pick(some, p):
                    kept = jnp.where(lanes == j + p, some[:, :BLOCK], 0.0)
                    return jnp.sum(kept, axis=1, keepdims=True)

                cols = [pick(square, p) for p in range(PIVOTS)]
                cells = [[pick(top, p) for p in range(PIVOTS)] for top in tops]
                total = diag[base:, :]
                for p in range(PIVOTS):
                    scale = 1.0 / cells[p][p]
                    weights = jnp.where(rows[base:] > j + p, cols[p] * scale, 0.0)
                    for q in range(p + 1, PIVOTS):
                        ratio = cells[q][p] * scale
                        tops[q] = tops[q] - ratio * tops[p]
                        cols[q] = cols[q] - weights * cells[p][q]
                        cells[q] = [cells[q][r] - ratio * cells[p][r] for r in range(PIVOTS)]
                    total = total - weights * tops[p]
                diag[base:, :] = total
            return carry

        for piece in range(PIECES):
            steps = BLOCK // PIVOTS // PIECES
            some = functools.partial(step, piece * BLOCK // PIECES)
            lax.fori_loop(piece * steps, (piece + 1) * steps, some, 0)
            if piece + 1 < PIECES:
                between()
        width = slice(low, rank + high)
        for work, diag in zip(works, diags):
            pivots = jnp.sum(
                jnp.where(rows == lanes, diag[:, :BLOCK], 0.0), axis=1, keepdims=True
            )
            inverse = diag[:, BLOCK:] * (1.0 / jnp.sqrt(pivots))
            panel = dot(inverse, work[low:high, width])
            work[low:high, width] = panel
            if high < rank:
                factors = panel[:, BLOCK : rank - low]
                work[high:, width] = work[high:, width] - dot(factors, panel, FIRST)
        between()
    for work, out in zip(works, outs):
        out[...] = work[:, rank:]


class Reduce:
    def __init__(self, row_count, sems):
        depth = row_count // SIDES
        row = lax.axis_index("row")
        place, lane = row // SIDES, lax.rem(row, SIDES)
        lower = place < depth // 2
        self.place, self.lane, self.depth = place, lane, depth
        self.other = place * SIDES + (1 - lane)
        toward = jnp.where(lower, SIDES, -SIDES)
        self.inner, self.outer = {"row": row + toward}, {"row": row - toward}
        self.steps = jnp.where(lower, depth // 2 - 1 - place, place - depth // 2)
        self.middle = self.steps == 0
        self.has_outer = self.steps < depth // 2 - 1
        self.sems = sems

    @staticmethod
    def scratch(count):
        return [DMA((count,))] * 6

    def inward(self, i, part, arrive):
        return remote(part, arrive, self.sems[0].at[i], self.sems[1].at[i], self.inner)

    def swap(self, i, part, meet):
        return remote(part, meet, self.sems[2].at[i], self.sems[3].at[i], self.inner)

    def outward(self, i, final):
        return remote(final, final, self.sems[4].at[i], self.sems[5].at[i], self.outer)

    def gather(self, i, part, arrive, meet):
        @pl.when(self.has_outer)
        def _():
            self.inward(i, part, arrive).wait_recv()
            part[...] = part[...] + arrive[...]

        @pl.when(self.middle)
        def _():
            self.swap(i, part, meet).start()

        @pl.when(self.steps > 0)
        def _():
            self.inward(i, part, arrive).start()

    def spread(self, i, part, meet, final):
        @pl.when(self.middle)
        def _():
            self.swap(i, part, meet).wait_recv()
            final[...] = part[...] + meet[...]

        @pl.when(self.steps > 0)
        def _():
            self.outward(i, final).wait_recv()

        @pl.when(self.has_outer)
        def _():
            self.outward(i, final).start()

    def drain(self, i, part, arrive, meet, final):
        @pl.when(self.middle)
        def _():
            self.swap(i, part, meet).wait_send()

        @pl.when(self.steps > 0)
        def _():
            self.inward(i, part, arrive).wait_send()

        @pl.when(self.has_outer)
        def _():
            self.outward(i, final).wait_send()


def products_kernel(row_count, col_count, rank, joined, scales, *refs):
    proj_a, proj_b, pair, buffer_b = refs[:4]
    trans_a, trans_b, basis_a, basis_b, ortho_a, ortho_b, scaled_a, scaled_b = refs[4:12]
    part_w, arrive_w, meet_w, final_w, other_w = refs[12:17]
    part_v, arrive_v, meet_v, final_v, land_v, other_v, whole_v = refs[17:24]
    piece_a, piece_b = refs[24:28], refs[28:32]
    cast_b, land_b, gram_a, gram_b, inv_a, inv_b, high_a, low_a = refs[32:40]
    rows_a, wide_a, wide_b, full_a, full_b, square_a, square_b, mine, theirs = refs[40:49]
    works, diags = refs[49:51], refs[51:53]
    reduce_sems, refs = refs[53:59], refs[59:]
    side_s, side_r, give_s, give_r, gram_s, gram_r, sq_s, sq_r = refs
    row, col = lax.axis_index("row"), lax.axis_index("col")
    line = Reduce(row_count, reduce_sems)
    lane, place, other = line.lane, line.place, line.other
    share, half = rank // row_count, rank // 2
    peers = SIDES * col_count
    piece = rank // peers
    index = lane * col_count + col
    chunks = part_w.shape[0]
    width = part_w.shape[2]

    def peer_of(k):
        target = lax.rem(index + k, peers)
        return (place * SIDES + target // col_count, lax.rem(target, col_count))

    barrier = pltpu.get_barrier_semaphore()

    pl.semaphore_signal(barrier, inc=1, device_id=line.inner, device_id_type=MESH)
    for k in range(1, peers):
        pl.semaphore_signal(barrier, inc=1, device_id=peer_of(k), device_id_type=MESH)

    @pl.when(line.has_outer)
    def _():
        pl.semaphore_signal(barrier, inc=1, device_id=line.outer, device_id_type=MESH)
        pl.semaphore_wait(barrier, peers + 1)

    @pl.when(jnp.logical_not(line.has_outer))
    def _():
        pl.semaphore_wait(barrier, peers)

    def rows_of(position, size):
        return pl.ds(pl.multiple_of(position * size, size), size)

    def give_g():
        return remote(cast_b, land_b, give_s.at[0], give_r.at[0], {"row": other})

    def give_v():
        there = whole_v.at[rows_of(1 - lane, half), :]
        return remote(there, land_v, give_s.at[1], give_r.at[1], {"row": other})

    bits = col_bits(col_count)[::-1]

    def held(stage):
        columns = [col]
        for bit in bits[: max(stage - 1, 0)]:
            columns += [partner(c, bit) for c in columns]
        sides = [lane] if stage == 0 else [lane, 1 - lane]
        return [side * col_count + c for side in sides for c in columns]

    def grams(stage):
        device = {"row": other} if stage == 0 else {"col": partner(col, bits[stage - 1])}
        copies = []
        for k, position in enumerate(held(stage)):
            for which, gram in enumerate((gram_a, gram_b)):
                here = gram.at[rows_of(position, piece), :]
                sems = gram_s.at[which, stage, k], gram_r.at[which, stage, k]
                copies.append(remote(here, here, *sems, device))
        return copies

    def send_grams(stage):
        for copy in grams(stage):
            copy.start()

    def await_grams(stage):
        for copy in grams(stage):
            copy.wait_recv()

    def aside(i, final, target):
        return remote(final, target, side_s.at[i], side_r.at[i], {"row": other})

    unit_v = (part_v, arrive_v, meet_v, final_v)

    def unit_w(k):
        return part_w.at[k], arrive_w.at[k], meet_w.at[k], final_w.at[k]

    def gather(i, unit):
        line.gather(i, unit[0], unit[1], unit[2])

    def spread(i, unit):
        line.spread(i, unit[0], unit[2], unit[3])

    theirs_index = (1 - lane) * col_count + col
    cast_b[...] = dot(proj_b[rows_of(theirs_index, piece), :], proj_b[...], LAST)
    give_g().start()
    piece_a[0][...] = dot(proj_a[rows_of(index, piece), :], proj_a[...], LAST)
    gather(0, piece_a)
    piece_b[0][...] = dot(proj_b[rows_of(index, piece), :], proj_b[...], LAST)
    give_g().wait_recv()
    piece_b[0][...] = piece_b[0][...] + land_b[...]
    gather(1, piece_b)
    rows_high, rows_low = halves(proj_a[...])

    def multiply(k):
        columns = slice(k * width, (k + 1) * width)
        block = pair[:, :, columns].reshape(proj_a.shape[1], width)
        block_high, block_low = halves(block)
        total = narrow_dot(rows_high, block_low) + narrow_dot(rows_low, block_high)
        part_w[k] = total + narrow_dot(rows_high, block_high)

    def take(k):
        gather(3 + k, unit_w(k))

    def hand(k):
        spread(3 + k, unit_w(k))
        aside(1 + k, final_w.at[k], other_w.at[k]).start()

    def take_v():
        give_v().wait_recv()
        part_v[...] = whole_v[rows_of(lane, half), :] + land_v[...]
        gather(2, unit_v)

    def hand_v():
        spread(2, unit_v)
        aside(0, final_v, other_v).start()

    def later_take(k):
        @pl.when(line.has_outer)
        def _():
            take(k)

    def later_take_v():
        @pl.when(line.has_outer)
        def _():
            take_v()

    early = jnp.logical_not(line.has_outer)
    multiply(0)

    @pl.when(early)
    def _():
        take(0)

    for which, unit in enumerate((piece_a, piece_b)):
        spread(which, unit)
    gram_a[rows_of(index, piece), :] = piece_a[3][...]
    gram_b[rows_of(index, piece), :] = piece_b[3][...]
    send_grams(0)
    whole_v[...] = split_dot(proj_b[...], buffer_b[...])
    give_v().start()
    for k in range(1, chunks):
        multiply(k)

        @pl.when(early)
        def _():
            take(k)

        if k == min(2, chunks - 1):

            @pl.when(early)
            def _():
                take_v()

            await_grams(0)
            send_grams(1)
        if k == min(3, chunks - 1):
            later_take(0)

    tasks = []
    for k in range(chunks):
        if k > 0:
            tasks.append(functools.partial(later_take, k))
            tasks.append(functools.partial(hand, k - 1))
        if k == min(2, chunks - 1):
            tasks.append(later_take_v)
        if k == min(3, chunks - 1):
            tasks.append(hand_v)
    tasks.append(functools.partial(hand, chunks - 1))
    for stage in range(1, len(bits) + 1):
        for _ in range(min(2, len(tasks))):
            tasks.pop(0)()
        await_grams(stage)
        if stage < len(bits):
            send_grams(stage + 1)
    slots = rank // BLOCK * PIECES
    done = [0, 0]

    def between():
        done[0] += 1
        goal = -(-len(tasks) * done[0] // slots)
        while done[1] < min(goal, len(tasks)):
            tasks[done[1]]()
            done[1] += 1

    factor(rank, [gram_a, gram_b], [inv_a, inv_b], works, diags, between)
    high_a[...], low_a[...] = halves(inv_a[...])
    rows_a[...] = proj_a[...].T
    count_a = rows_a.shape[0] // SIDES
    wide_a[...] = split_dot(rows_a[rows_of(lane, count_a), :], inv_a[...], LAST)
    wide_b[...] = split_dot(proj_b[...].T, inv_b[...], LAST)
    ortho_a[...] = wide_a[...].astype(jnp.bfloat16)
    ortho_b[...] = wide_b[...].astype(jnp.bfloat16)
    square_a[...] = jnp.zeros_like(square_a)
    own = rows_of(row, share)

    def use(product, position):
        product_high, product_low = halves(product)
        total = narrow_dot(high_a[...], product_low) + narrow_dot(low_a[...], product_high)
        total = total + narrow_dot(high_a[...], product_high)
        full_a[...] = total
        trans_a[position] = total.astype(jnp.bfloat16)
        square_a[...] += jnp.sum(total * total, axis=1, keepdims=True)
        basis_a[position] = full_a[own, :]

    groups = chunks // joined

    def group(source, k):
        return jnp.concatenate([source[k * joined + i] for i in range(joined)], axis=1)

    def near(k, carry):
        use(group(final_w, k), lane * groups + k)
        return carry

    def far(k, carry):
        for i in range(joined):
            j = k * joined + i
            aside(1 + j, final_w.at[j], other_w.at[j]).wait_recv()
        use(group(other_w, k), (1 - lane) * groups + k)
        return carry

    lax.fori_loop(0, groups, near, 0)
    aside(0, final_v, other_v).wait_recv()
    whole_v[rows_of(lane, half), :] = final_v[...]
    give_v().wait_send()
    whole_v[rows_of(1 - lane, half), :] = other_v[...]
    total_b = split_dot(inv_b[...], whole_v[...])
    full_b[...] = total_b
    trans_b[...] = total_b.astype(jnp.bfloat16)
    square_b[...] = jnp.sum(total_b * total_b, axis=1, keepdims=True)
    lax.fori_loop(0, groups, far, 0)

    def across(column):
        return jnp.broadcast_to(column, (rank, BLOCK)).T[:8]

    def norms(k):
        peer = lax.rem(col + k, col_count)
        return remote(mine, theirs.at[col], sq_s.at[k], sq_r.at[k], {"col": peer})

    mine[0] = across(square_a[...])
    mine[1] = across(square_b[...])
    for k in range(1, col_count):
        norms(k).start()
    theirs[col] = mine[...]
    for k in range(1, col_count):
        norms(k).wait_recv()
    norm = jnp.sqrt(jnp.sum(theirs[...], axis=0) + EPS)
    norm_a, norm_b = norm[0, :1], norm[1, :1]
    scaled_a[...] = (wide_a[...] * (scales[0] / norm_a)).astype(jnp.bfloat16)
    scaled_b[...] = (wide_b[...] * (scales[1] / norm_b)).astype(jnp.bfloat16)
    ranks = lax.broadcasted_iota(jnp.int32, (share, rank), 1)
    owned = lax.broadcasted_iota(jnp.int32, (share, rank), 0) + row * share
    own_a = jnp.sum(jnp.where(ranks == owned, norm_a, 0.0), axis=1, keepdims=True)
    own_b = jnp.sum(jnp.where(ranks == owned, norm_b, 0.0), axis=1, keepdims=True)
    for k in range(basis_a.shape[0]):
        basis_a[k] = basis_a[k] / own_a
    basis_b[...] = full_b[own, :] / own_b
    for k in range(1, col_count):
        norms(k).wait_send()
    for stage in range(len(bits) + 1):
        for copy in grams(stage):
            copy.wait_send()
    give_g().wait_send()
    aside(0, final_v, other_v).wait_send()
    for i, unit in enumerate((piece_a, piece_b, unit_v)):
        line.drain(i, *unit)

    def sent(k, carry):
        aside(1 + k, final_w.at[k], other_w.at[k]).wait_send()
        line.drain(3 + k, *unit_w(k))
        return carry

    lax.fori_loop(0, chunks, sent, 0)


def products(proj_a, proj_b, pair, buffer_b, scales):
    row_count, col_count = lax.axis_size("row"), lax.axis_size("col")
    rank = proj_a.shape[0]
    share, half, piece = rank // row_count, rank // 2, rank // (SIDES * col_count)
    side_width = pair.shape[2]
    chunk = CHUNK if side_width % CHUNK == 0 else side_width
    chunks = side_width // chunk
    joined = 2 if chunks % 2 == 0 else 1
    groups, wide_chunk = chunks // joined, chunk * joined
    width_b = buffer_b.shape[1]
    rows_a, rows_b = pair.shape[1], buffer_b.shape[0]

    def array(kind, *shape):
        return jax.ShapeDtypeStruct(shape, kind)

    def space(*shape):
        return pltpu.VMEM(shape, jnp.float32)

    narrow, wide = jnp.bfloat16, jnp.float32
    grams = DMA((2, len(col_bits(col_count)) + 1, SIDES * col_count))
    cols = DMA((col_count,))
    return pl.pallas_call(
        functools.partial(products_kernel, row_count, col_count, rank, joined, scales),
        out_shape=[
            array(narrow, SIDES * groups, rank, wide_chunk),
            array(narrow, rank, width_b),
            array(wide, SIDES * groups, share, wide_chunk),
            array(wide, share, width_b),
            array(narrow, rows_a, rank),
            array(narrow, rows_b, rank),
            array(narrow, rows_a, rank),
            array(narrow, rows_b, rank),
        ],
        in_specs=[VMEM] * 4,
        out_specs=[VMEM] * 8,
        scratch_shapes=[space(chunks, rank, chunk)] * 5
        + [space(half, width_b)] * 6
        + [space(rank, width_b)]
        + [space(piece, rank)] * 10
        + [space(rank, rank)] * 4
        + [pltpu.VMEM((rank, rank), narrow)] * 2
        + [
            space(SIDES * rows_a, rank),
            space(rows_a, rank),
            space(rows_b, rank),
            space(rank, wide_chunk),
            space(rank, width_b),
            space(rank, 1),
            space(rank, 1),
            space(2, 8, rank),
            space(col_count, 2, 8, rank),
        ]
        + [space(rank, 2 * rank)] * 2
        + [space(BLOCK, 2 * BLOCK)] * 2
        + Reduce.scratch(3 + chunks)
        + [DMA((1 + chunks,))] * 2
        + [DMA((2,))] * 2
        + [grams, grams, cols, cols],
        name="products",
        compiler_params=pltpu.CompilerParams(
            collective_id=2, has_side_effects=True, vmem_limit_bytes=62 * 2**20
        ),
    )(proj_a, proj_b, pair, buffer_b)


def ending_kernel(slabs, *refs):
    buffer_a, trans_a, basis_a, ortho_a, scaled_a = refs[:5]
    buffer_b, trans_b, ortho_b, scaled_b = refs[5:9]
    mom_a, update_a, new_a, mom_b, update_b = refs[9:]
    width = trans_a.shape[2]
    for k in range(trans_a.shape[0]):
        columns = slice(k * width, (k + 1) * width)
        change = narrow_dot(ortho_a[...], trans_a[k])
        mom_a[:, columns] = buffer_a[:, columns] - (1.0 - MU) * change
        update_a[:, columns] = narrow_dot(scaled_a[...], trans_a[k]).astype(jnp.bfloat16)
        new_a[:, columns] = basis_a[k]

    @pl.when(pl.program_id(0) < slabs)
    def _():
        mom_b[...] = buffer_b[...] - (1.0 - MU) * narrow_dot(ortho_b[...], trans_b[...])
        update_b[...] = narrow_dot(scaled_b[...], trans_b[...]).astype(jnp.bfloat16)


def ending(buffer_a, trans_a, basis_a, ortho_a, scaled_a, buffer_b, trans_b, ortho_b, scaled_b):
    steps, rank, width = trans_a.shape
    rows_a, rows_b, share = buffer_a.shape[0], buffer_b.shape[0], basis_a.shape[1]
    slabs = 4
    if width % 128 or rows_b % (16 * slabs) or steps % 2 or steps < 2 * slabs:
        flat = trans_a.swapaxes(0, 1).reshape(rank, -1)
        return (
            buffer_a - (1.0 - MU) * narrow_dot(ortho_a, flat),
            narrow_dot(scaled_a, flat).astype(jnp.bfloat16),
            basis_a.swapaxes(0, 1).reshape(share, -1),
            buffer_b - (1.0 - MU) * narrow_dot(ortho_b, trans_b),
            narrow_dot(scaled_b, trans_b).astype(jnp.bfloat16),
        )
    some = rows_b // slabs
    cut = pl.BlockSpec((rows_a, 2 * width), lambda j: (0, j))
    stack = pl.BlockSpec((2, rank, width), lambda j: (j, 0, 0))
    thin = pl.BlockSpec((2, share, width), lambda j: (j, 0, 0))
    fixed_a = pl.BlockSpec((rows_a, rank), lambda j: (0, 0))
    fixed_b = pl.BlockSpec(trans_b.shape, lambda j: (0, 0))
    slab = pl.BlockSpec((some, buffer_b.shape[1]), lambda j: (jnp.minimum(j, slabs - 1), 0))
    rows = pl.BlockSpec((some, rank), lambda j: (jnp.minimum(j, slabs - 1), 0))
    return pl.pallas_call(
        functools.partial(ending_kernel, slabs),
        grid=(steps // 2,),
        out_shape=[
            jax.ShapeDtypeStruct(buffer_a.shape, jnp.float32),
            jax.ShapeDtypeStruct(buffer_a.shape, jnp.bfloat16),
            jax.ShapeDtypeStruct((share, buffer_a.shape[1]), jnp.float32),
            jax.ShapeDtypeStruct(buffer_b.shape, jnp.float32),
            jax.ShapeDtypeStruct(buffer_b.shape, jnp.bfloat16),
        ],
        in_specs=[cut, stack, thin, fixed_a, fixed_a, slab, fixed_b, rows, rows],
        out_specs=[cut, cut, pl.BlockSpec((share, 2 * width), lambda j: (0, j)), slab, slab],
        name="ending",
    )(buffer_a, trans_a, basis_a, ortho_a, scaled_a, buffer_b, trans_b, ortho_b, scaled_b)


def shards(mom_a, grad_a, basis_a, mom_b, grad_b, basis_b):
    row_count = lax.axis_size("row")
    buffer_a, buffer_b = MU * mom_a + grad_a, MU * mom_b + grad_b
    proj_a, proj_b, pair = project(basis_a, basis_b, buffer_a, buffer_b)
    rank = proj_a.shape[0]
    scales = [
        math.sqrt(x.shape[0] * x.shape[1] * row_count * lax.axis_size("col") / rank)
        for x in (buffer_a, buffer_b)
    ]
    trans_a, trans_b, basis_a, basis_b, ortho_a, ortho_b, scaled_a, scaled_b = products(
        proj_a, proj_b, pair, buffer_b, scales
    )
    new_mom_a, update_a, new_basis_a, new_mom_b, update_b = ending(
        buffer_a, trans_a, basis_a, ortho_a, scaled_a, buffer_b, trans_b, ortho_b, scaled_b
    )
    return new_mom_a, update_a, new_basis_a, new_mom_b, update_b, basis_b


def solution(mesh):
    spec = P("row", "col")
    return jax.shard_map(
        shards, mesh=mesh, in_specs=(spec,) * 6, out_specs=(spec,) * 6, check_vma=False
    )
```
